32 devices in a mesh: group: 4 (over y, x), dp: 8 (over z, core).
Axes of the slice: x: 2, y: 2, z: 4, core: 2. Of those that a mesh axis runs over, the one named last changes fastest.
Arguments:
- layer_input: bfloat16 [3, 32, 320, 1024], P(None, ('group', 'dp')), may hold values from -6 to 6
- lengths: int32 [3, 32], P(None, ('group', 'dp')), may hold values from 256 to 320, as said below
- attend_gain: bfloat16 [1024], P('dp'), may hold values from 0.5 to 1.5
- attend_bias: bfloat16 [1024], P('dp'), may hold values from -1.75 to 1.75
- project_weight: bfloat16 [1024, 3072], P('dp'), may hold values from -0.1875 to 0.1875
- project_bias: bfloat16 [2048], P('dp'), may hold values from -0.625 to 0.625
- output_weight: bfloat16 [1024, 1024], P('dp'), may hold values from -2 to 2
- output_bias: bfloat16 [1024], P('dp'), may hold values from -3 to 3
- feed_gain: bfloat16 [1024], P('dp'), may hold values from 0.5 to 1.5
- feed_bias: bfloat16 [1024], P('dp'), may hold values from -1.75 to 1.75
- expand_weight: bfloat16 [1024, 4096], P('dp'), may hold values from -0.1875 to 0.1875
- expand_bias: bfloat16 [4096], P('dp'), may hold values from -3 to 3
- reduce_weight: bfloat16 [4096, 1024], P('dp'), may hold values from -0.09375 to 0.09375
- reduce_bias: bfloat16 [1024], P('dp'), may hold values from -3 to 3
- cotangent: bfloat16 [3, 32, 320, 1024], P(None, ('group', 'dp')), may hold values from -6 to 6
Outputs:
- layer_output: float32 [3, 32, 320, 1024], P(None, ('group', 'dp'))
- input_grad: float32 [3, 32, 320, 1024], P(None, ('group', 'dp'))
- attend_gain_grad: float32 [1024], P('dp')
- attend_bias_grad: float32 [1024], P('dp')
- project_weight_grad: float32 [1024, 3072], P('dp')
- project_bias_grad: float32 [2048], P('dp')
- output_weight_grad: float32 [1024, 1024], P('dp')
- output_bias_grad: float32 [1024], P('dp')
- feed_gain_grad: float32 [1024], P('dp')
- feed_bias_grad: float32 [1024], P('dp')
- expand_weight_grad: float32 [1024, 4096], P('dp')
- expand_bias_grad: float32 [4096], P('dp')
- reduce_weight_grad: float32 [4096, 1024], P('dp')
- reduce_bias_grad: float32 [1024], P('dp')
The draws below stay inside these ranges and needn't reach their ends.
Inputs may be any that keep to these rules, and one draw needn't show every extreme that they name: Sequence b of micro-batch m uses its first lengths[m, b] slots (64 buffer slots and the kept image tokens); the other slots are padding. Some sequence of every micro-batch uses all 320 slots and some uses 256.
All inputs are finite; a program needn't handle non-finite values.
Results may differ from the reference program's by a relative error of at most 0.019.
Values may be sent and summed in bfloat16 or wider, within the bound.
No kernel may reach another device: no remote copies, remote signals or barrier semaphores. Data moves between devices by JAX's collectives and lax.ppermute only.
A program may use at most 256 MiB of HBM per device.

```python
import jax
import jax.numpy as jnp
from jax import lax

D = 1024
H = 16
E = 64
FF = 4096
BUF = 64
KEEP = 256
MICRO = 3
L = 320
SEQS = 32


def draw_lengths(key, part):
    first_key, second_key, third_key = jax.random.split(jax.random.fold_in(key, 17), 3)
    least = BUF + 3 * KEEP // 4
    most = BUF + KEEP
    drawn = jax.random.randint(first_key, (MICRO, SEQS), least, most + 1)
    full_at = jax.random.randint(second_key, (MICRO, 1), 0, SEQS)
    offset = jax.random.randint(third_key, (MICRO, 1), 1, SEQS)
    short_at = (full_at + offset) % SEQS
    columns = jnp.arange(SEQS)[None, :]
    drawn = jnp.where(columns == full_at, most, drawn)
    drawn = jnp.where(columns == short_at, least, drawn)
    return drawn.astype(jnp.int32)


def block_levels(rng, dims, shards, low, top_value):
    level = 1.0
    for axis_at, shards_of in shards:
        draws = jax.random.uniform(jax.random.fold_in(jax.random.fold_in(rng, 6), axis_at), (shards_of,), jnp.float32, low / len(shards), top_value / len(shards))
        level = level * jnp.repeat(jnp.exp(draws), dims[axis_at] // shards_of).reshape((-1,) + (1,) * (len(dims) - 1 - axis_at))
    return level


def noise(stream_key, dims, width, bound, shards=(), held_as=jnp.bfloat16):
    values = width * jax.random.normal(stream_key, dims, jnp.float32)
    if shards:
        values = values * block_levels(stream_key, dims, shards, -0.22, 0.18)
    return jnp.clip(values, -bound, bound).astype(held_as)


def setup_inputs(seed: int = 0) -> dict:
    seeds = jax.random.split(jax.random.key(seed), 16)
    return {
        "layer_input": noise(seeds[0], (MICRO, SEQS, L, D), 1.0, 6.0, ((1, 32),)),
        "lengths": draw_lengths(jax.random.fold_in(seeds[15], 71), 0),
        "attend_gain": jnp.clip(1.0 + 0.1 * jax.random.normal(seeds[2], (D,), jnp.float32), 0.5, 1.5).astype(jnp.bfloat16),
        "attend_bias": noise(seeds[3], (D,), 0.3, 1.75, ((0, 8),)),
        "project_weight": noise(seeds[4], (D, 3 * D), D ** -0.5, 0.1875, ((0, 8),)),
        "project_bias": noise(seeds[5], (2 * D,), 0.1, 0.625, ((0, 8),)),
        "output_weight": noise(seeds[6], (D, D), (max(D // 128, 2)) ** -0.5, 2.0, ((0, 8),)),
        "output_bias": noise(seeds[7], (D,), 0.5, 3.0, ((0, 8),)),
        "feed_gain": jnp.clip(1.0 + 0.1 * jax.random.normal(seeds[8], (D,), jnp.float32), 0.5, 1.5).astype(jnp.bfloat16),
        "feed_bias": noise(seeds[9], (D,), 0.3, 1.75, ((0, 8),)),
        "expand_weight": noise(seeds[10], (D, FF), D ** -0.5, 0.1875, ((0, 8),)),
        "expand_bias": noise(seeds[11], (FF,), 0.5, 3.0, ((0, 8),)),
        "reduce_weight": noise(seeds[12], (FF, D), FF ** -0.5, 0.09375, ((0, 8),)),
        "reduce_bias": noise(seeds[13], (D,), 0.5, 3.0, ((0, 8),)),
        "cotangent": noise(seeds[14], (MICRO, SEQS, L, D), 1.0, 6.0, ((1, 32),)),
    }


EPS = 1e-06

@jax.custom_vjp
def low(v):
    return lax.optimization_barrier(v.astype(jnp.bfloat16)).astype(jnp.float32)

@jax.custom_vjp
def low_back(v):
    return v

def low_keep(v):
    return (low(v), None)

def low_pass(kept, grad):
    return (grad,)

def back_keep(v):
    return (v, None)

def back_low(kept, grad):
    return (low(grad),)
low.defvjp(low_keep, low_pass)
low_back.defvjp(back_keep, back_low)

def layer_norm(values, gain_vec, bias_vec):
    row_mean = lax.optimization_barrier(jnp.mean(values, -1, keepdims=True))
    centred = values - row_mean
    spread = lax.optimization_barrier(jnp.mean(centred * centred, -1, keepdims=True))
    return centred * lax.rsqrt(spread + EPS) * gain_vec + bias_vec

def project(former, latter):
    return jnp.einsum('bld,de->ble', former, latter, precision=lax.Precision.HIGHEST)

def forward(params, layer_in, valid_grid):
    attend_gain, attend_bias, project_weight, project_bias, output_weight, output_bias, feed_gain, feed_bias, expand_weight, expand_bias, reduce_weight, reduce_bias = params
    batch_count = layer_in.shape[0]
    highest = lax.Precision.HIGHEST
    masked = layer_in * valid_grid[:, :, None]
    normed = low(layer_norm(masked, attend_gain, attend_bias))
    zero_part = jnp.zeros_like(project_bias[:D])
    full_bias = jnp.concatenate([project_bias[:D], zero_part, project_bias[D:]])
    packed = low(low_back(project(normed, project_weight) + full_bias))
    packed = packed.reshape(batch_count, L, 3, H, E)
    queries = packed[:, :, 0]
    keys = packed[:, :, 1]
    values = packed[:, :, 2]
    scores = low_back(jnp.einsum('bqhe,bkhe->bhqk', queries, keys, precision=highest) * E ** (-0.5))
    scores = jnp.where(valid_grid[:, None, None, :] > 0, scores, -1e+30)
    row_max = lax.optimization_barrier(jnp.max(scores, -1, keepdims=True))
    weights = jnp.exp(scores - row_max)
    probs = low(weights / lax.optimization_barrier(jnp.sum(weights, -1, keepdims=True)))
    mixed = jnp.einsum('bhqk,bkhe->bqhe', probs, values, precision=highest)
    mixed = low(low_back(mixed.reshape(batch_count, L, D)))
    resid = masked + low_back(project(mixed, output_weight) + output_bias)
    normed_two = low(layer_norm(resid, feed_gain, feed_bias))
    hidden = low_back(project(normed_two, expand_weight) + expand_bias)
    activated = low(jax.nn.gelu(hidden, approximate=False))
    result = resid + low_back(project(activated, reduce_weight) + reduce_bias)
    return result * valid_grid[:, :, None]

def reference(layer_input, lengths, attend_gain, attend_bias, project_weight, project_bias, output_weight, output_bias, feed_gain, feed_bias, expand_weight, expand_bias, reduce_weight, reduce_bias, cotangent):
    params = tuple((weight_in.astype(jnp.float32) for weight_in in (attend_gain, attend_bias, project_weight, project_bias, output_weight, output_bias, feed_gain, feed_bias, expand_weight, expand_bias, reduce_weight, reduce_bias)))
    block_seqs = 8
    block_count = MICRO * SEQS // block_seqs
    input_blocks = layer_input.astype(jnp.float32).reshape(block_count, block_seqs, L, D)
    length_blocks = lengths.astype(jnp.int32).reshape(block_count, block_seqs)
    cot_blocks = cotangent.astype(jnp.float32).reshape(block_count, block_seqs, L, D)
    slot_ids = jnp.arange(L, dtype=jnp.int32)

    def scan_step(running, block_item):
        block_in, block_len, block_cot = block_item
        valid_grid = (slot_ids[None, :] < block_len[:, None]).astype(jnp.float32)
        block_out, pullback = jax.vjp(lambda weights_in, values_in: forward(weights_in, values_in, valid_grid), params, block_in)
        weight_grads, block_grad = pullback(block_cot)
        running = jax.tree.map(jnp.add, running, weight_grads)
        return (running, (block_out, block_grad))
    zero_grads = tuple((jnp.zeros_like(weight_in) for weight_in in params))
    totals, (out_blocks, grad_blocks) = lax.scan(scan_step, zero_grads, (input_blocks, length_blocks, cot_blocks))
    return (out_blocks.reshape(MICRO, SEQS, L, D), grad_blocks.reshape(MICRO, SEQS, L, D), totals[0], totals[1], totals[2], totals[3], totals[4], totals[5], totals[6], totals[7], totals[8], totals[9], totals[10], totals[11])
```

```python
import jax
import jax.numpy as jnp
from jax import lax
from jax.sharding import PartitionSpec as P

H = 16
E = 64


EPS = 1e-06


def as_sent(array):

    def short(part):
        return part.astype(jnp.bfloat16) if part.dtype == jnp.float32 else part

    return jax.tree.map(short, array)


def layer_norm(values, gain_vec, bias_vec):
    row_mean = jnp.mean(values, -1, keepdims=True)
    centred = values - row_mean
    spread = jnp.mean(centred * centred, -1, keepdims=True)
    return centred * lax.rsqrt(spread + EPS) * gain_vec + bias_vec


def exact_gelu(values):
    return jax.nn.gelu(values, approximate=False)


def dot_rows(former, latter):
    return jnp.dot(former, latter, preferred_element_type=jnp.float32)


def dot_left(former, latter):
    return lax.dot_general(
        former, latter, (((0,), (0,)), ((), ())), preferred_element_type=jnp.float32
    )


def dot_right(former, latter):
    return lax.dot_general(
        former, latter, (((1,), (1,)), ((), ())), preferred_element_type=jnp.float32
    )


def fetch_weights(shards):
    return (
        lax.all_gather(shards[0], "dp", axis=0, tiled=True),
        lax.all_gather(shards[1], "dp", axis=0, tiled=True),
        lax.all_gather(shards[2], "dp", axis=0, tiled=True),
        lax.all_gather(shards[3], "dp", axis=0, tiled=True),
        lax.all_gather(shards[4], "dp", axis=0, tiled=True),
        lax.all_gather(shards[5], "dp", axis=0, tiled=True),
        lax.all_gather(shards[6], "dp", axis=0, tiled=True),
        lax.all_gather(shards[7], "dp", axis=0, tiled=True),
        lax.all_gather(shards[8], "dp", axis=0, tiled=True),
        lax.all_gather(shards[9], "dp", axis=0, tiled=True),
        lax.all_gather(shards[10], "dp", axis=0, tiled=True),
        lax.all_gather(shards[11], "dp", axis=0, tiled=True),
    )


def reduce_grads(grads):
    return (
        lax.psum_scatter(
            grads[0].astype(jnp.bfloat16), "dp", scatter_dimension=0, tiled=True
        ).astype(jnp.float32),
        lax.psum_scatter(
            grads[1].astype(jnp.bfloat16), "dp", scatter_dimension=0, tiled=True
        ).astype(jnp.float32),
        lax.psum_scatter(
            grads[2].astype(jnp.bfloat16), "dp", scatter_dimension=0, tiled=True
        ).astype(jnp.float32),
        lax.psum_scatter(
            grads[3].astype(jnp.bfloat16), "dp", scatter_dimension=0, tiled=True
        ).astype(jnp.float32),
        lax.psum_scatter(
            grads[4].astype(jnp.bfloat16), "dp", scatter_dimension=0, tiled=True
        ).astype(jnp.float32),
        lax.psum_scatter(
            grads[5].astype(jnp.bfloat16), "dp", scatter_dimension=0, tiled=True
        ).astype(jnp.float32),
        lax.psum_scatter(
            grads[6].astype(jnp.bfloat16), "dp", scatter_dimension=0, tiled=True
        ).astype(jnp.float32),
        lax.psum_scatter(
            grads[7].astype(jnp.bfloat16), "dp", scatter_dimension=0, tiled=True
        ).astype(jnp.float32),
        lax.psum_scatter(
            grads[8].astype(jnp.bfloat16), "dp", scatter_dimension=0, tiled=True
        ).astype(jnp.float32),
        lax.psum_scatter(
            grads[9].astype(jnp.bfloat16), "dp", scatter_dimension=0, tiled=True
        ).astype(jnp.float32),
        lax.psum_scatter(
            grads[10].astype(jnp.bfloat16), "dp", scatter_dimension=0, tiled=True
        ).astype(jnp.float32),
        lax.psum_scatter(
            grads[11].astype(jnp.bfloat16), "dp", scatter_dimension=0, tiled=True
        ).astype(jnp.float32),
    )


def masked_scores(queries, keys, key_valid):
    scores = jnp.einsum(
        "sqhe,skhe->shqk", queries, keys, preferred_element_type=jnp.float32
    ) * E ** (-0.5)
    return jnp.where(key_valid, scores, -1e30)


def attend_forward(queries, keys, key_valid):
    scores = masked_scores(queries, keys, key_valid)
    row_max = jnp.max(scores, -1, keepdims=True)
    weights = jnp.exp(scores - row_max)
    row_total = jnp.sum(weights, -1, keepdims=True)
    return (weights / row_total, row_max + jnp.log(row_total))


def attend_backward(queries, keys, values, log_sum, key_valid, grad_mixed):
    probs = jnp.exp(masked_scores(queries, keys, key_valid) - log_sum)
    probs_low = probs.astype(jnp.bfloat16)
    grad_probs = jnp.einsum(
        "sqhe,skhe->shqk", grad_mixed, values, preferred_element_type=jnp.float32
    )
    grad_values = jnp.einsum(
        "shqk,sqhe->skhe", probs_low, grad_mixed, preferred_element_type=jnp.float32
    )
    inner = jnp.sum(grad_probs * probs, -1, keepdims=True)
    grad_scores = (probs * (grad_probs - inner)).astype(jnp.bfloat16)
    scale = E ** (-0.5)
    grad_queries = (
        jnp.einsum("shqk,skhe->sqhe", grad_scores, keys, preferred_element_type=jnp.float32) * scale
    )
    grad_keys = (
        jnp.einsum("shqk,sqhe->skhe", grad_scores, queries, preferred_element_type=jnp.float32)
        * scale
    )
    return (grad_queries, grad_keys, grad_values)


def local(
    layer_input,
    lengths,
    attend_gain,
    attend_bias,
    project_weight,
    project_bias,
    output_weight,
    output_bias,
    feed_gain,
    feed_bias,
    expand_weight,
    expand_bias,
    reduce_weight,
    reduce_bias,
    cotangent,
):
    shards = (
        attend_gain,
        attend_bias,
        project_weight,
        project_bias,
        output_weight,
        output_bias,
        feed_gain,
        feed_bias,
        expand_weight,
        expand_bias,
        reduce_weight,
        reduce_bias,
    )
    micro_count, seq_count, slot_count, width = layer_input.shape
    row_count = micro_count * seq_count * slot_count
    seq_total = micro_count * seq_count
    slot_ids = jnp.arange(slot_count, dtype=jnp.int32)
    gathered = fetch_weights(shards)
    valid_grid = (slot_ids[None, :] < lengths.reshape(-1)[:, None]).astype(jnp.float32)
    row_valid = valid_grid.reshape(row_count, 1)
    key_valid = valid_grid[:, None, None, :] > 0
    masked = layer_input.reshape(row_count, width).astype(jnp.float32) * row_valid
    normed, norm_one_back = jax.vjp(
        layer_norm, masked, gathered[0].astype(jnp.float32), gathered[1].astype(jnp.float32)
    )
    normed = normed.astype(jnp.bfloat16)
    bias_pair = gathered[3].astype(jnp.float32)
    full_bias = jnp.concatenate(
        [bias_pair[:width], jnp.zeros((width,), jnp.float32), bias_pair[width:]]
    )
    packed = (dot_rows(normed, gathered[2]) + full_bias).astype(jnp.bfloat16)
    packed = packed.reshape(seq_total, slot_count, 3, H, E)
    queries = packed[:, :, 0]
    keys = packed[:, :, 1]
    values = packed[:, :, 2]
    probs, log_sum = attend_forward(queries, keys, key_valid)
    mixed = jnp.einsum(
        "shqk,skhe->sqhe",
        probs.astype(jnp.bfloat16),
        values,
        preferred_element_type=jnp.float32,
    )
    mixed = mixed.reshape(row_count, width).astype(jnp.bfloat16)
    resid = masked + dot_rows(mixed, gathered[4]) + gathered[5].astype(jnp.float32)
    normed_two, norm_two_back = jax.vjp(
        layer_norm, resid, gathered[6].astype(jnp.float32), gathered[7].astype(jnp.float32)
    )
    normed_two = normed_two.astype(jnp.bfloat16)
    hidden = dot_rows(normed_two, gathered[8]) + gathered[9].astype(jnp.float32)
    activated, gelu_back = jax.vjp(exact_gelu, hidden)
    activated = activated.astype(jnp.bfloat16)
    result = (
        resid + dot_rows(activated, gathered[10]) + gathered[11].astype(jnp.float32)
    ) * row_valid
    layer_output = result.reshape(layer_input.shape)
    back_weights = gathered
    upstream = cotangent.reshape(row_count, width).astype(jnp.float32) * row_valid
    up_low = upstream.astype(jnp.bfloat16)
    grad_reduce_w = dot_left(activated, up_low)
    grad_reduce_b = jnp.sum(up_low, 0, dtype=jnp.float32)
    (grad_hidden,) = gelu_back(dot_right(up_low, back_weights[10]))
    hidden_low = grad_hidden.astype(jnp.bfloat16)
    grad_expand_w = dot_left(normed_two, hidden_low)
    grad_expand_b = jnp.sum(hidden_low, 0, dtype=jnp.float32)
    grad_resid_norm, grad_feed_gain, grad_feed_bias = norm_two_back(
        dot_right(hidden_low, back_weights[8])
    )
    grad_resid = upstream + grad_resid_norm
    branch_low = grad_resid.astype(jnp.bfloat16)
    grad_output_w = dot_left(mixed, branch_low)
    grad_output_b = jnp.sum(branch_low, 0, dtype=jnp.float32)
    grad_mixed = dot_right(branch_low, back_weights[4]).astype(jnp.bfloat16)
    grad_mixed = grad_mixed.reshape(seq_total, slot_count, H, E)
    grad_queries, grad_keys, grad_values = attend_backward(
        queries, keys, values, log_sum, key_valid, grad_mixed
    )
    grad_packed = jnp.stack([grad_queries, grad_keys, grad_values], 2).astype(jnp.bfloat16)
    grad_packed = grad_packed.reshape(row_count, 3 * width)
    grad_project_w = dot_left(normed, grad_packed)
    column_sums = jnp.sum(grad_packed, 0, dtype=jnp.float32)
    grad_project_b = jnp.concatenate([column_sums[:width], column_sums[2 * width :]])
    grad_in_norm, grad_attend_gain, grad_attend_bias = norm_one_back(
        dot_right(grad_packed, back_weights[2])
    )
    input_grad = ((grad_resid + grad_in_norm) * row_valid).reshape(layer_input.shape)
    grads = (
        grad_attend_gain,
        grad_attend_bias,
        grad_project_w,
        grad_project_b,
        grad_output_w,
        grad_output_b,
        grad_feed_gain,
        grad_feed_bias,
        grad_expand_w,
        grad_expand_b,
        grad_reduce_w,
        grad_reduce_b,
    )
    running = reduce_grads(grads)
    summed = jax.tree.map(
        lambda part: part.astype(jnp.float32), lax.psum(as_sent(running), "group")
    )
    return (
        layer_output,
        input_grad,
        summed[0],
        summed[1],
        summed[2],
        summed[3],
        summed[4],
        summed[5],
        summed[6],
        summed[7],
        summed[8],
        summed[9],
        summed[10],
        summed[11],
    )


def solution(mesh):
    return jax.shard_map(
        local,
        mesh=mesh,
        in_specs=(
            P(None, ("group", "dp"), None, None),
            P(None, ("group", "dp")),
            P("dp"),
            P("dp"),
            P("dp", None),
            P("dp"),
            P("dp", None),
            P("dp"),
            P("dp"),
            P("dp"),
            P("dp", None),
            P("dp"),
            P("dp", None),
            P("dp"),
            P(None, ("group", "dp"), None, None),
        ),
        out_specs=(
            P(None, ("group", "dp"), None, None),
            P(None, ("group", "dp"), None, None),
            P("dp"),
            P("dp"),
            P("dp", None),
            P("dp"),
            P("dp", None),
            P("dp"),
            P("dp"),
            P("dp"),
            P("dp", None),
            P("dp"),
            P("dp", None),
            P("dp"),
        ),
        check_vma=False,
    )
```

```python
import functools

import jax
import jax.numpy as jnp
from jax import lax
from jax.experimental import pallas as pl
from jax.experimental.pallas import tpu as pltpu
from jax.sharding import PartitionSpec as P

F32 = jnp.float32
BF16 = jnp.bfloat16
EPS = 1e-06
H = 16
E = 64
LANES = 128
HALF_ROOT = 2.0 ** -0.5
INV_ROOT_TAU = 0.3989422804014327
NN = (((1,), (0,)), ((), ()))
NT = (((1,), (1,)), ((), ()))
TN = (((0,), (0,)), ((), ()))


def mm(former, latter, dims=NN):
    return lax.dot_general(former, latter, dims, preferred_element_type=F32)


def params(mib):
    return pltpu.CompilerParams(vmem_limit_bytes=mib << 20, dimension_semantics=("arbitrary",))


def cost(flops, nbytes, other=0):
    return pl.CostEstimate(flops=int(flops), bytes_accessed=int(nbytes), transcendentals=int(other))


def once(shape):
    return pl.BlockSpec(shape, lambda *_: (0,) * len(shape), pipeline_mode=pl.Buffered(1))


def valid_rows(length, rows):
    return (lax.broadcasted_iota(jnp.int32, (rows, 1), 0) < length).astype(F32)


def norm_parts(values):
    centred = values - jnp.mean(values, -1, keepdims=True)
    scale = lax.rsqrt(jnp.mean(centred * centred, -1, keepdims=True) + EPS)
    return centred * scale, scale


def norm_back(unit, scale, grad, gain):
    grad_unit = grad * gain
    first = jnp.mean(grad_unit, -1, keepdims=True)
    second = jnp.mean(grad_unit * unit, -1, keepdims=True)
    return scale * (grad_unit - first - unit * second)


def column_sum(values):
    return jnp.sum(values, 0, keepdims=True)


def add_first(step, ref, value):
    @pl.when(step == 0)
    def _():
        ref[...] = value

    @pl.when(step > 0)
    def _():
        ref[...] += value


def collect(ring, pos, pieces, whole, sems):
    copies = []

    def put(source, target):
        copy = pltpu.make_async_copy(source, target, sems.at[len(copies)])
        copy.start()
        copies.append(copy)

    if not ring:
        put(pieces[0], whole)
    else:
        g, z, c = pos[0], pos[1], pos[2]
        for at in range(2):
            core = c if at == 0 else 1 - c
            own, near, far = pieces[3 * at : 3 * at + 3]
            put(own, whole.at[z, core])
            for k in range(1, Z):
                row = lax.rem(z + Z - k, Z)
                for over in range(3):
                    put(near.at[over, :, k - 1], whole.at[row, core, g ^ over])
                for part in range(2):
                    put(far.at[part, k - 1], whole.at[row, core, g ^ 3, part])
    for copy in copies:
        copy.wait()


def whole_shape(ring, pieces):
    if ring:
        return (Z, 2) + pieces[0].shape
    return pieces[0].shape


def collect_scratch(ring, pieces):
    return [
        pltpu.VMEM(whole_shape(ring, pieces), BF16),
        pltpu.SemaphoreType.DMA((32,)),
        pltpu.SemaphoreType.DMA,
    ]


def fill(ring, step, steps, pos, pieces, kept, whole, sems, sem):
    @pl.when(step == 0)
    def _():
        collect(ring, pos, pieces, whole, sems)
        pltpu.make_async_copy(whole, kept, sem).start()


def keep(step, steps, kept, whole, sem):
    @pl.when(step == steps - 1)
    def _():
        pltpu.make_async_copy(whole, kept, sem).wait()


def flat_rows(whole):
    value = whole[...]
    return value.reshape(-1, value.shape[-1])


def project_kernel(ring, count, lengths, pos, x, cot, gain, bias, weight_bias, *refs):
    pieces, (normed, packed, up, up_sum, kept, whole, sems, sem) = refs[:-8], refs[-8:]
    step = pl.program_id(0)
    fill(ring, step, count, pos, pieces, kept, whole, sems, sem)
    rows = x.shape[1]
    valid = valid_rows(lengths[step], rows)
    unit, _ = norm_parts(x[0].astype(F32) * valid)
    low = (unit * gain[...] + bias[...]).astype(BF16)
    normed[0] = low
    packed[0] = (mm(low, flat_rows(whole)) + weight_bias[...]).astype(BF16)
    upstream = cot[0].astype(F32) * valid
    up[0] = upstream.astype(BF16)
    add_first(step, up_sum, column_sum(upstream))
    keep(step, count, kept, whole, sem)


def project(ring, lengths, pos, x, cot, gain, bias, weight_bias, pieces):
    seqs, rows, width = x.shape
    wide = pieces[0].shape[-1]
    row_block = pl.BlockSpec((1, rows, width), lambda s, *_: (s, 0, 0))
    anywhere = pl.BlockSpec(memory_space=pl.ANY)
    *rest, kept = pl.pallas_call(
        functools.partial(project_kernel, ring, seqs),
        grid_spec=pltpu.PrefetchScalarGridSpec(
            num_scalar_prefetch=2,
            grid=(seqs,),
            in_specs=[
                row_block,
                row_block,
                once((1, width)),
                once((1, width)),
                once((1, wide)),
            ]
            + [anywhere] * len(pieces),
            out_specs=[
                row_block,
                pl.BlockSpec((1, rows, wide), lambda s, *_: (s, 0, 0)),
                row_block,
                pl.BlockSpec((1, width), lambda s, *_: (0, 0)),
                anywhere,
            ],
            scratch_shapes=collect_scratch(ring, pieces),
        ),
        out_shape=[
            jax.ShapeDtypeStruct(x.shape, BF16),
            jax.ShapeDtypeStruct((seqs, rows, wide), BF16),
            jax.ShapeDtypeStruct(x.shape, BF16),
            jax.ShapeDtypeStruct((1, width), F32),
            jax.ShapeDtypeStruct(whole_shape(ring, pieces), BF16),
        ],
        compiler_params=params(28),
        cost_estimate=cost(2 * seqs * rows * width * wide, seqs * rows * (4 * width + wide) * 2 + 4 * width * wide),
        name="norm_project",
    )(lengths, pos, x, cot, gain, bias, weight_bias, *pieces)
    return (*rest, kept.reshape(-1, wide))


def head_masks(rows):
    lane = lax.broadcasted_iota(jnp.int32, (rows, LANES), 1)
    return lane < E


def attend_kernel(seq, lengths, q, k, v, *refs):
    mixed, lse = refs[-2:]
    rows = q.shape[1]
    length = lengths[seq]
    key_ok = lax.broadcasted_iota(jnp.int32, (1, rows), 1) < length
    low_lane = head_masks(rows)
    for pair in range(q.shape[2] // LANES):
        at = slice(pair * LANES, (pair + 1) * LANES)
        qs, ks, vs = q[0, :, at], k[0, :, at], v[0, :, at]
        outs = []
        logs = []
        for head in range(2):
            keep = low_lane if head == 0 else ~low_lane
            qh = jnp.where(keep, qs, jnp.zeros_like(qs))
            scores = jnp.where(key_ok, mm(qh, ks, NT) * E**-0.5, -1e30)
            top = jnp.max(scores, -1, keepdims=True)
            weights = jnp.exp(scores - top)
            total = jnp.sum(weights, -1, keepdims=True)
            probs = (weights / total).astype(BF16)
            outs.append(mm(probs, vs))
            logs.append(top + jnp.log(total))
        mixed[0, :, at] = jnp.where(low_lane, outs[0], outs[1]).astype(BF16)
        lse[0, pair] = jnp.concatenate(logs, -1)


def attend(seq, lengths, packed, pairs, earlier=()):
    seqs, rows, wide = packed.shape
    width = wide // 3
    wid = pairs * LANES
    steps = width // wid
    block = lambda part: pl.BlockSpec((1, rows, wid), lambda j, *_: (seq, 0, part * steps + j))
    return pl.pallas_call(
        functools.partial(attend_kernel, seq),
        grid_spec=pltpu.PrefetchScalarGridSpec(
            num_scalar_prefetch=1,
            grid=(steps,),
            in_specs=[block(0), block(1), block(2)]
            + [pl.BlockSpec(memory_space=pl.ANY)] * len(earlier),
            out_specs=[
                pl.BlockSpec((1, rows, wid), lambda j, *_: (seq, 0, j)),
                pl.BlockSpec((1, pairs, rows, 2), lambda j, *_: (seq, j, 0, 0)),
            ],
        ),
        out_shape=[
            jax.ShapeDtypeStruct((seqs, rows, width), BF16),
            jax.ShapeDtypeStruct((seqs, width // LANES, rows, 2), F32),
        ],
        input_output_aliases={4: 0, 5: 1} if earlier else {},
        compiler_params=params(14),
        cost_estimate=cost(4 * rows * rows * width * 8, rows * wide * 3, H * rows * rows),
        name="attend",
    )(lengths, packed, packed, packed, *earlier)


def attend_back_kernel(seq, lengths, q, k, v, lse, grad, *refs):
    dq, dk, dv = refs[-3:]
    rows = q.shape[1]
    length = lengths[seq]
    key_ok = lax.broadcasted_iota(jnp.int32, (1, rows), 1) < length
    low_lane = head_masks(rows)
    for pair in range(q.shape[2] // LANES):
        at = slice(pair * LANES, (pair + 1) * LANES)
        qs, ks, vs, gs = q[0, :, at], k[0, :, at], v[0, :, at], grad[0, :, at]
        sums = []
        for head in range(2):
            keep = low_lane if head == 0 else ~low_lane
            qh = jnp.where(keep, qs, jnp.zeros_like(qs))
            gh = jnp.where(keep, gs, jnp.zeros_like(gs))
            scores = jnp.where(key_ok, mm(qh, ks, NT) * E**-0.5, -1e30)
            probs = jnp.exp(scores - lse[0, pair, :, head : head + 1])
            grad_probs = mm(gh, vs, NT)
            inner = jnp.sum(grad_probs * probs, -1, keepdims=True)
            grad_scores = (probs * (grad_probs - inner)).astype(BF16)
            sums.append(
                (
                    mm(grad_scores, ks) * E**-0.5,
                    mm(grad_scores, qs, TN) * E**-0.5,
                    mm(probs.astype(BF16), gs, TN),
                )
            )
        for ref, first, second in zip((dq, dk, dv), sums[0], sums[1]):
            ref[0, :, at] = jnp.where(low_lane, first, second).astype(BF16)


def attend_back(seq, lengths, packed, lse, grad, pairs, earlier=()):
    seqs, rows, wide = packed.shape
    width = wide // 3
    wid = pairs * LANES
    steps = width // wid
    block = lambda part: pl.BlockSpec((1, rows, wid), lambda j, *_: (seq, 0, part * steps + j))
    out = pl.BlockSpec((1, rows, wid), lambda j, *_: (seq, 0, j))
    return pl.pallas_call(
        functools.partial(attend_back_kernel, seq),
        grid_spec=pltpu.PrefetchScalarGridSpec(
            num_scalar_prefetch=1,
            grid=(steps,),
            in_specs=[
                block(0),
                block(1),
                block(2),
                pl.BlockSpec((1, pairs, rows, 2), lambda j, *_: (seq, j, 0, 0)),
                out,
            ]
            + [pl.BlockSpec(memory_space=pl.ANY)] * len(earlier),
            out_specs=[out] * 3,
        ),
        out_shape=[jax.ShapeDtypeStruct((seqs, rows, width), BF16)] * 3,
        input_output_aliases={6: 0, 7: 1, 8: 2} if earlier else {},
        compiler_params=params(16),
        cost_estimate=cost(10 * rows * rows * width * 8, rows * wide * 5, H * rows * rows),
        name="attend_back",
    )(lengths, packed, packed, packed, lse, grad, *earlier)


def branch_kernel(ring, count, lengths, pos, x, mixed, weight_bias, gain, bias, *refs):
    pieces, (resid, normed, kept, whole, sems, sem) = refs[:-6], refs[-6:]
    step = pl.program_id(0)
    fill(ring, step, count, pos, pieces, kept, whole, sems, sem)
    rows, width = x.shape[1:]
    valid = valid_rows(lengths[step], rows)
    weight = whole[..., :width].reshape(-1, width)
    total = x[0].astype(F32) * valid + mm(mixed[0], weight) + weight_bias[...]
    resid[0] = total
    unit, _ = norm_parts(total)
    normed[0] = (unit * gain[...] + bias[...]).astype(BF16)
    keep(step, count, kept, whole, sem)


def branch(ring, lengths, pos, x, mixed, weight_bias, gain, bias, pieces):
    seqs, rows, width = x.shape
    wide = pieces[0].shape[-1]
    row_block = pl.BlockSpec((1, rows, width), lambda s, *_: (s, 0, 0))
    vec = once((1, width))
    anywhere = pl.BlockSpec(memory_space=pl.ANY)
    resid, normed, kept = pl.pallas_call(
        functools.partial(branch_kernel, ring, seqs),
        grid_spec=pltpu.PrefetchScalarGridSpec(
            num_scalar_prefetch=2,
            grid=(seqs,),
            in_specs=[row_block, row_block, vec, vec, vec] + [anywhere] * len(pieces),
            out_specs=[row_block, row_block, anywhere],
            scratch_shapes=collect_scratch(ring, pieces),
        ),
        out_shape=[
            jax.ShapeDtypeStruct(x.shape, F32),
            jax.ShapeDtypeStruct(x.shape, BF16),
            jax.ShapeDtypeStruct(whole_shape(ring, pieces), BF16),
        ],
        compiler_params=params(26),
        cost_estimate=cost(2 * seqs * rows * width * width, seqs * rows * width * 10 + 4 * width * wide),
        name="branch",
    )(lengths, pos, x, mixed, weight_bias, gain, bias, *pieces)
    return resid, normed, kept.reshape(-1, wide)


def store_halves(ref, value):
    _, shards, quarters, rows, _ = ref.shape
    for shard in range(shards):
        for quarter in range(quarters):
            for half in range(2):
                at = ((shard * quarters + quarter) * 2 + half) * rows
                ref[half, shard, quarter] = value[at : at + rows]


def expand_kernel(half, seqs, order, normed, up, weight, bias, *refs):
    act, slope, grad = refs[-3:]
    rows = normed.shape[0] // seqs

    def body(s, carry):
        at = pl.ds(pl.multiple_of(s * rows, rows), rows)
        hidden = mm(normed[at, :], weight[...]) + bias[...]
        phi = 0.5 + 0.5 * lax.erf(hidden * HALF_ROOT)
        act[at, :] = (hidden * phi).astype(BF16)
        slope[at, :] = (phi + hidden * (INV_ROOT_TAU * jnp.exp(-0.5 * hidden * hidden))).astype(BF16)
        return carry

    lax.fori_loop(0, seqs, body, 0)
    store_halves(grad, mm(act[...], up[...], TN).astype(BF16))


def expand(half, seqs, order, normed, up, weight, bias, earlier=()):
    count, width = normed.shape
    hidden = bias.shape[1]
    size = hidden // 8
    column = lambda i, order: (0, order[0] * i + order[1 + half])
    skip = (weight.shape[1] - hidden) // size
    weight_column = lambda i, order: (0, skip + order[0] * i + order[1 + half])
    wide = pl.BlockSpec((count, size), column)
    shape = jax.ShapeDtypeStruct((count, hidden), BF16)
    return pl.pallas_call(
        functools.partial(expand_kernel, half, seqs),
        grid_spec=pltpu.PrefetchScalarGridSpec(
            num_scalar_prefetch=1,
            grid=(4,),
            in_specs=[
                once((count, width)),
                once((count, width)),
                pl.BlockSpec((width, size), weight_column),
                pl.BlockSpec((1, size), column),
            ]
            + [pl.BlockSpec(memory_space=pl.ANY)] * len(earlier),
            out_specs=[wide, wide, pl.BlockSpec((2, 1, 4, size // 8, width), lambda i, *_: (0, i, 0, 0, 0))],
        ),
        out_shape=[shape, shape, jax.ShapeDtypeStruct((2, 4, 4, size // 8, width), BF16)],
        input_output_aliases={5: 0, 6: 1} if earlier else {},
        compiler_params=params(24),
        cost_estimate=cost(2 * count * width * hidden, count * hidden * 2 + width * hidden * 2, count * hidden),
        name="expand_half",
    )(order, normed, up, weight, bias, *earlier)


def reduce_kernel(lengths, resid, act, weight, bias, out):
    rows = resid.shape[1]
    valid = valid_rows(lengths[pl.program_id(0)], rows)
    out[0] = (resid[0] + mm(act[0], weight[...]) + bias[...]) * valid


def reduce_out(lengths, resid, act, weight, bias):
    seqs, rows, width = resid.shape
    hidden = weight.shape[0]
    row_block = pl.BlockSpec((1, rows, width), lambda s, *_: (s, 0, 0))
    return pl.pallas_call(
        reduce_kernel,
        grid_spec=pltpu.PrefetchScalarGridSpec(
            num_scalar_prefetch=1,
            grid=(seqs,),
            in_specs=[
                row_block,
                pl.BlockSpec((1, rows, hidden), lambda s, *_: (s, 0, 0)),
                once((hidden, width)),
                once((1, width)),
            ],
            out_specs=row_block,
        ),
        out_shape=jax.ShapeDtypeStruct(resid.shape, F32),
        compiler_params=params(26),
        cost_estimate=cost(2 * seqs * rows * width * hidden, seqs * rows * (8 * width + 2 * hidden) + 2 * width * hidden),
        name="reduce_out",
    )(lengths, resid, act.reshape(seqs, rows, hidden), weight, bias)


def hidden_back_kernel(ring, seqs, pos, up, slope, *refs):
    pieces, (grad, grad_sum, kept, whole, sems, sem) = refs[:-6], refs[-6:]
    step = pl.program_id(0)
    fill(ring, step, 8, pos, pieces, kept, whole, sems, sem)
    rows = up.shape[0] // seqs
    if ring:
        block = whole[step // 2, step % 2]
    else:
        size = whole.shape[0] // 8
        block = whole[pl.ds(pl.multiple_of(step * size, size), size), :]
    weight = block.reshape(-1, block.shape[-1])

    def body(s, total):
        at = pl.ds(pl.multiple_of(s * rows, rows), rows)
        low = (mm(up[at, :], weight, NT) * slope[at, :].astype(F32)).astype(BF16)
        grad[at, :] = low
        return total + column_sum(low.astype(F32))

    grad_sum[...] = lax.fori_loop(0, seqs, body, jnp.zeros(grad_sum.shape, F32))
    keep(step, 8, kept, whole, sem)


def hidden_back(ring, seqs, pos, up, slope, pieces):
    count, width = up.shape
    hidden = slope.shape[1]
    size = hidden // 8
    wide = pl.BlockSpec((count, size), lambda i, *_: (0, i))
    anywhere = pl.BlockSpec(memory_space=pl.ANY)
    grad, grad_sum, kept = pl.pallas_call(
        functools.partial(hidden_back_kernel, ring, seqs),
        grid_spec=pltpu.PrefetchScalarGridSpec(
            num_scalar_prefetch=1,
            grid=(8,),
            in_specs=[once((count, width)), wide] + [anywhere] * len(pieces),
            out_specs=[wide, pl.BlockSpec((1, size), lambda i, *_: (0, i)), anywhere],
            scratch_shapes=collect_scratch(ring, pieces),
        ),
        out_shape=[
            jax.ShapeDtypeStruct((count, hidden), BF16),
            jax.ShapeDtypeStruct((1, hidden), F32),
            jax.ShapeDtypeStruct(whole_shape(ring, pieces), BF16),
        ],
        compiler_params=params(22),
        cost_estimate=cost(2 * count * width * hidden, count * hidden * 4 + 4 * width * hidden),
        name="hidden_back",
    )(pos, up, slope, *pieces)
    return grad, grad_sum, kept.reshape(hidden, width)


def weight_grad_kernel(half, parts, order, inputs, *refs):
    grads, (out, picked) = refs[:parts], refs[-2:]
    step = pl.program_id(0)

    @pl.when(step == 0)
    def _():
        for i in range(4):
            size = picked.shape[1] // 4
            at = pl.multiple_of((order[0] * i + order[1 + half]) * size, size)
            picked[:, i * size : (i + 1) * size] = inputs[:, pl.ds(at, size)]

    for at, grad in enumerate(grads):

        @pl.when((step == at) | (parts == 1))
        def _(grad=grad):
            store_halves(out, mm(picked[...], grad[...], TN).astype(BF16))


def weight_grad(half, order, inputs, grads, wide, first=0, earlier=()):
    count, width = inputs.shape
    size = 1024
    if len(grads) == 1:
        spec = [pl.BlockSpec((count, size), lambda j, *_: (0, j))]
    else:
        spec = [once((count, size))] * len(grads)
    here = sum(grad.shape[1] for grad in grads)
    rows = width // 64
    return pl.pallas_call(
        functools.partial(weight_grad_kernel, half, len(grads)),
        grid_spec=pltpu.PrefetchScalarGridSpec(
            num_scalar_prefetch=1,
            grid=(here // size,),
            in_specs=[once((count, width)), *spec]
            + [pl.BlockSpec(memory_space=pl.ANY)] * len(earlier),
            out_specs=pl.BlockSpec(
                (2, 4, 4, rows, size), lambda j, *_: (0, 0, 0, 0, first // size + j)
            ),
            scratch_shapes=[pltpu.VMEM((count, width // 2), BF16)],
        ),
        out_shape=jax.ShapeDtypeStruct((2, 4, 4, rows, wide), BF16),
        input_output_aliases={2 + len(grads): 0} if earlier else {},
        compiler_params=params(20),
        cost_estimate=cost(count * width * here, count * (width + here) * 2 + width * here),
        name="weight_grad",
    )(order, inputs, *grads, *earlier)


def norm_two_kernel(lengths, hidden_grad, weight, resid, cot, gain, *outs):
    grad_resid, low_ref, mixed_grad, gain_grad, bias_grad, out_bias_grad = outs
    step = pl.program_id(0)
    rows, width = resid.shape[1:]
    valid = valid_rows(lengths[step], rows)
    grad = mm(hidden_grad[0], weight[:, width:], NT)
    unit, scale = norm_parts(resid[0])
    total = cot[0].astype(F32) * valid + norm_back(unit, scale, grad, gain[...])
    grad_resid[0] = total
    low = total.astype(BF16)
    low_ref[0] = low
    mixed_grad[0] = mm(low, weight[:, :width], NT).astype(BF16)
    add_first(step, gain_grad, column_sum(grad * unit))
    add_first(step, bias_grad, column_sum(grad))
    add_first(step, out_bias_grad, column_sum(low.astype(F32)))


def norm_two_back(lengths, hidden_grad, weight, resid, cot, gain):
    seqs, rows, width = resid.shape
    hidden = hidden_grad.shape[1]
    row_block = pl.BlockSpec((1, rows, width), lambda s, *_: (s, 0, 0))
    vec = pl.BlockSpec((1, width), lambda s, *_: (0, 0))
    return pl.pallas_call(
        norm_two_kernel,
        grid_spec=pltpu.PrefetchScalarGridSpec(
            num_scalar_prefetch=1,
            grid=(seqs,),
            in_specs=[
                pl.BlockSpec((1, rows, hidden), lambda s, *_: (s, 0, 0)),
                once((width, width + hidden)),
                row_block,
                row_block,
                once((1, width)),
            ],
            out_specs=[row_block] * 3 + [vec] * 3,
        ),
        out_shape=[
            jax.ShapeDtypeStruct(resid.shape, F32),
            jax.ShapeDtypeStruct(resid.shape, BF16),
            jax.ShapeDtypeStruct(resid.shape, BF16),
        ]
        + [jax.ShapeDtypeStruct((1, width), F32)] * 3,
        compiler_params=params(40),
        cost_estimate=cost(2 * seqs * rows * width * (hidden + width), seqs * rows * (2 * hidden + 14 * width)),
        name="norm_two_back",
    )(lengths, hidden_grad.reshape(seqs, rows, hidden), weight, resid, cot, gain)


def norm_one_kernel(lengths, dq, dk, dv, weight, x, grad_resid, gain, *outs):
    input_grad, gain_grad, bias_grad, q_sum, v_sum = outs
    step = pl.program_id(0)
    rows, width = x.shape[1:]
    valid = valid_rows(lengths[step], rows)
    grad = mm(dq[0], weight[:, :width], NT)
    grad += mm(dk[0], weight[:, width : 2 * width], NT)
    grad += mm(dv[0], weight[:, 2 * width :], NT)
    unit, scale = norm_parts(x[0].astype(F32) * valid)
    input_grad[0] = (grad_resid[0] + norm_back(unit, scale, grad, gain[...])) * valid
    add_first(step, gain_grad, column_sum(grad * unit))
    add_first(step, bias_grad, column_sum(grad))
    add_first(step, q_sum, column_sum(dq[0].astype(F32)))
    add_first(step, v_sum, column_sum(dv[0].astype(F32)))


def norm_one_back(lengths, dq, dk, dv, weight, x, grad_resid, gain):
    seqs, rows, width = x.shape
    row_block = pl.BlockSpec((1, rows, width), lambda s, *_: (s, 0, 0))
    vec = pl.BlockSpec((1, width), lambda s, *_: (0, 0))
    return pl.pallas_call(
        norm_one_kernel,
        grid_spec=pltpu.PrefetchScalarGridSpec(
            num_scalar_prefetch=1,
            grid=(seqs,),
            in_specs=[row_block] * 3
            + [once((width, 3 * width)), row_block, row_block, once((1, width))],
            out_specs=[row_block] + [vec] * 4,
        ),
        out_shape=[jax.ShapeDtypeStruct(x.shape, F32)] + [jax.ShapeDtypeStruct((1, width), F32)] * 4,
        compiler_params=params(32),
        cost_estimate=cost(6 * seqs * rows * width * width, seqs * rows * width * 16 + 6 * width * width),
        name="norm_one_back",
    )(lengths, dq, dk, dv, weight, x, grad_resid, gain)

def near_kernel(pos, *refs):
    for at in range(4):
        mine, other, out = refs[at], refs[4 + at], refs[8 + at]
        total = mine[...].astype(F32) + other[...].astype(F32)
        out[...] = total.astype(BF16).reshape(out.shape)


def near_sum(pos, own, arrived):
    _, shards, _, rows, wide = own.shape
    x = lambda pos: pos[0] % 2
    y = lambda pos: pos[0] // 2
    over_x = (1, 1, 2, 1, rows, wide)
    over_y = (1, 1, 1, 2, rows, wide)
    specs = [
        pl.BlockSpec(over_x, lambda s, pos: (0, s, 0, x(pos), 0, 0)),
        pl.BlockSpec(over_y, lambda s, pos: (1, s, y(pos), 0, 0, 0)),
        pl.BlockSpec(over_x, lambda s, pos: (0, s, 0, 1 - x(pos), 0, 0)),
        pl.BlockSpec(over_y, lambda s, pos: (1, s, 1 - y(pos), 0, 0, 0)),
    ]
    shape = (2, shards, 2, 2, rows, wide)
    return pl.pallas_call(
        near_kernel,
        grid_spec=pltpu.PrefetchScalarGridSpec(
            num_scalar_prefetch=1,
            grid=(shards,),
            in_specs=specs * 2,
            out_specs=[pl.BlockSpec((1, 2, rows, wide), lambda s, pos: (s, 0, 0, 0))] * 4,
        ),
        out_shape=[jax.ShapeDtypeStruct((shards, 2, rows, wide), BF16)] * 4,
        compiler_params=params(14),
        cost_estimate=cost(own.size, own.size * 6),
        name="near_sum",
    )(pos, *[own.reshape(shape)] * 4, *[arrived.reshape(shape)] * 4)


AXES = ("group", "dp")
Z = 4


def permutation(move):
    pairs = []
    for g in range(4):
        for d in range(2 * Z):
            to_g, to_z, to_c = move(g, d // 2, d % 2)
            pairs.append((g * 2 * Z + d, (to_g * Z + to_z) * 2 + to_c))
    return pairs


CORE = permutation(lambda g, z, c: (g, z, 1 - c))
OVER_X = permutation(lambda g, z, c: (g ^ 1, z, c))
OVER_Y = permutation(lambda g, z, c: (g ^ 2, z, c))
OVER_XY = permutation(lambda g, z, c: (g ^ 3, z, c))
OVER_Z = [permutation(lambda g, z, c, k=k: (g, (z + k) % Z, c)) for k in range(Z)]
NEAR_Z = permutation(lambda g, z, c: (g, z ^ 1, c))
FAR_Z = permutation(lambda g, z, c: (g, z ^ 2, c))


def send(array, pairs):
    return lax.ppermute(array, AXES, pairs)


def tie(value, *others):
    return lax.optimization_barrier((value,) + others)[0]


def pick(array, index, axis):
    return lax.dynamic_index_in_dim(array, index, axis, keepdims=False)


def plus(former, latter):
    return (former.astype(F32) + latter.astype(F32)).astype(BF16)


def quarters(shard, g):
    rows, wide = shard.shape
    parts = shard.reshape(4, 2, rows // 8, wide)
    return parts, pick(parts, g, 0)


def send_quarter(mine):
    return [send(mine, OVER_Z[k]) for k in range(1, Z)]


def send_xy(first, second):
    return send(first, OVER_X), send(second, OVER_Y)


def scatter_core(other):
    return send(other, CORE)


def scatter_far(first, second, from_x, from_y, g):
    x, y = g % 2, g // 2
    first = plus(first, from_x)
    second = plus(second, from_y)
    return pick(first, y, 1), pick(second, x, 1), pick(first, 1 - y, 1), pick(second, 1 - x, 1)


def scatter_z(first, second, from_y, from_x, z):
    quarter = jnp.stack([plus(first, from_y), plus(second, from_x)], 1)
    return pick(quarter, z, 0), [pick(quarter, (z + k) % Z, 0) for k in range(1, Z)]


def send_z(parts):
    return [send(part, OVER_Z[k]) for k, part in enumerate(parts, 1)]


def spread(mine, arrived):
    total = mine.astype(F32)
    for part in arrived:
        total = total + part.astype(F32)
    return total.astype(BF16)


def send_near(mine):
    return [send(mine, OVER_X), send(mine, OVER_Y), send(mine, OVER_XY)]


def placed(mine, others, g):
    grid = jnp.stack([mine, *others]).reshape(2, 2, *mine.shape)
    grid = jnp.where(g % 2 == 1, grid[:, ::-1], grid)
    grid = jnp.where(g // 2 == 1, grid[::-1], grid)
    return grid.astype(F32).reshape(-1, mine.shape[-1])


VEC = (0, 1, 3, 5, 6, 7, 9, 11)


def joined(vectors):
    total = sum(v.shape[0] for v in vectors)
    at = 0
    out = None
    for v in vectors:
        wide = lax.pad(v, jnp.zeros((), v.dtype), [(at, total - at - v.shape[0], 0)])
        out = wide if out is None else out + wide
        at += v.shape[0]
    return out


def split_vectors(everyone, shards):
    full = {}
    at = 0
    for i in VEC:
        size = shards[i].shape[0]
        full[i] = everyone[:, at : at + size].reshape(1, -1).astype(F32)
        at += size
    return full


def gather_vectors(shards):
    packed = joined([shards[i] for i in VEC])
    return lax.all_gather(packed, "dp", axis=0, tiled=False)


def reduce_vectors(grads, shards, ring, after=()):
    packed = joined([grads[i].reshape(-1) for i in VEC])
    if ring:
        total = tie(packed.reshape(-1, LANES), *after)
        for pairs in (CORE, OVER_X, OVER_Y, NEAR_Z, FAR_Z):
            total = total + send(total, pairs)
        total = total.reshape(-1)
    else:
        total = lax.psum(packed, ("group", "dp"))
    d = lax.axis_index("dp")
    at = 0
    summed = {}
    for i in VEC:
        size = shards[i].shape[0]
        summed[i] = lax.dynamic_slice(total, (at + d * size,), (size,))
        at += grads[i].size
    return summed


def plain_sum(other, own):
    wide = own.shape[-1]
    low = jnp.concatenate([a.transpose(1, 2, 0, 3, 4).reshape(-1, wide) for a in (other, own)])
    part = lax.psum_scatter(low, "dp", scatter_dimension=0, tiled=True)
    return lax.psum(part, "group").astype(F32)


def local(ring, layer_input, lengths, *rest):
    shards, cot = rest[:12], rest[12]
    micro, seqs, rows, width = layer_input.shape
    count = micro * seqs
    g = lax.axis_index("group")
    d = lax.axis_index("dp")
    z, c = d // 2, d % 2
    pos = jnp.stack([g, z, c]).astype(jnp.int32)
    order = [2, 1 - c, c] if ring else [1, 0, 4]
    order = jnp.stack([jnp.asarray(v, jnp.int32) for v in order])
    lens = lengths.reshape(-1)
    x = layer_input.reshape(count, rows, width)
    cot = cot.reshape(count, rows, width)
    flat = lambda a: a.reshape(count * rows, a.shape[-1])
    wanted = (shards[2], jnp.concatenate([shards[4], shards[8]], 1), shards[10])

    everyone = gather_vectors(shards)
    if ring:
        parts_p, mine_p = quarters(wanted[0], g)
        parts_e, mine_e = quarters(wanted[1], g)
        parts_r, mine_r = quarters(wanted[2], g)
        ring_p = send_quarter(mine_p)
        core_p, core_e = send(parts_p, CORE), send(parts_e, CORE)
        stack_p = jnp.stack(tie(ring_p, core_p, core_e, everyone), 1)
        x_p, y_p = send_xy(stack_p, stack_p)
        ring_e = send_quarter(tie(mine_e, stack_p))
        b_p, a_p = send_xy(y_p[1], x_p[0])
        near_p = tie(jnp.stack([stack_p, x_p, y_p]), a_p, b_p)
        far_p = jnp.stack([a_p, b_p])
        pieces_p = [parts_p, near_p, far_p, core_p, send(near_p, CORE), send(far_p, CORE)]
        stack_e = jnp.stack(tie(ring_e, pieces_p), 1)
        lens_project, mine_r = tie((lens, mine_r), stack_e)
        x_e, y_e = send_xy(stack_e, stack_e)
        ring_r = send_quarter(mine_r)
    else:
        pieces = [lax.all_gather(w, "dp", axis=0, tiled=True) for w in wanted]
        pieces_p, pieces_e, pieces_r = [[w] for w in pieces]
        lens_project = lens
    full = split_vectors(everyone, shards)
    project_b = jnp.concatenate(
        [full[3][:, :width], jnp.zeros((1, width), F32), full[3][:, width:]], -1
    )
    normed, packed, up, up_sum, project_w = project(
        ring, lens_project, pos, x, cot, full[0], full[1], project_b, pieces_p
    )
    mixed, lse = attend(0, lens, packed, 4)
    lens_attend = lens
    if ring:
        x_e, y_e = tie((x_e, y_e), mixed)
        near_e = jnp.stack([stack_e, x_e, y_e])
        lens_attend = tie(lens, near_e)
        b_e, a_e = send_xy(y_e[1], x_e[0])
        near_core_e, core_r = send(near_e, CORE), send(parts_r, CORE)
    for seq in range(1, count):
        mixed, lse = attend(seq, lens_attend, packed, 4, (mixed, lse))
    lens_branch = lens
    if ring:
        a_e, b_e, ring_r = tie((a_e, b_e, ring_r), mixed)
        far_e = jnp.stack([a_e, b_e])
        pieces_e = [parts_e, near_e, far_e, core_e, near_core_e, send(far_e, CORE)]
        stack_r = jnp.stack(ring_r, 1)
        lens_branch = tie(lens, stack_r)
        x_r, y_r = send_xy(stack_r, stack_r)
    resid, normed_two, joint_w = branch(
        ring, lens_branch, pos, x, mixed, full[5], full[6], full[7], pieces_e
    )
    act, slope, reduce_far = expand(
        0, count, order, flat(normed_two), flat(up), joint_w, full[9]
    )
    expand_b = full[9]
    if ring:
        x_r, y_r = tie((x_r, y_r), reduce_far)
        near_r = jnp.stack([stack_r, x_r, y_r])
        expand_b = tie(expand_b, near_r)
        b_r, a_r = send_xy(y_r[1], x_r[0])
        near_core_r, arrived = send(near_r, CORE), send(tie(reduce_far, near_r), CORE)
    act, slope, reduce_near = expand(
        1, count, order, flat(normed_two), flat(up), joint_w, expand_b, (act, slope)
    )
    up_back = up
    if ring:
        a_r, b_r = tie((a_r, b_r), reduce_near)
        far_r = jnp.stack([a_r, b_r])
        pieces_r = [parts_r, near_r, far_r, core_r, near_core_r, send(far_r, CORE)]
        rs = near_sum(pos, reduce_near, arrived)
        up_back = tie(up, rs)
        from_x, from_y = send_xy(rs[2], rs[3])
    hidden_grad, hidden_sum, reduce_w = hidden_back(
        ring, count, pos, flat(up_back), slope, pieces_r
    )
    order_far = order
    if ring:
        from_x, from_y = tie((from_x, from_y), hidden_sum)
        rs = scatter_far(rs[0], rs[1], from_x, from_y, g)
        order_far = tie(order, rs)
        from_x, from_y = send_xy(rs[3], rs[2])
    joint = 5 * width
    expand_far = weight_grad(0, order_far, flat(normed_two), (hidden_grad,), joint, width)
    lens_two = lens
    if ring:
        from_x, from_y = tie((from_x, from_y), expand_far)
        mine_z, parts_z = scatter_z(rs[0], rs[1], from_y, from_x, z)
        lens_two = tie(lens, parts_z)
        arrived_r = send_z(parts_z)
    grad_resid, branch_low, mixed_grad, gain_two_grad, bias_two_grad, output_b_grad = norm_two_back(
        lens_two, hidden_grad, joint_w, resid, cot, full[6]
    )
    joint_far = weight_grad(
        0, order, flat(mixed), (flat(branch_low),), joint, 0, (expand_far,)
    )
    order_near = order
    if ring:
        order_near = tie(order, joint_far)
        arrived = send(joint_far, CORE)
    expand_near = weight_grad(1, order_near, flat(normed_two), (hidden_grad,), joint, width)
    joint_near = weight_grad(
        1, order_near, flat(mixed), (flat(branch_low),), joint, 0, (expand_near,)
    )
    lens_back = lens
    if ring:
        arrived_r = tie(arrived_r, joint_near)
        spread_r = spread(mine_z, arrived_r)
        es = near_sum(pos, joint_near, arrived)
        lens_back = tie(lens, es, spread_r)
        from_x, from_y = send_xy(es[2], es[3])
        near_r = send_near(spread_r)
    thirds = attend_back(0, lens_back, packed, lse, mixed_grad, 2)
    for seq in range(1, count - 1):
        thirds = attend_back(seq, lens_back, packed, lse, mixed_grad, 2, thirds)
    if ring:
        from_x, from_y, near_r = tie((from_x, from_y, near_r), thirds[0])
        es = scatter_far(es[0], es[1], from_x, from_y, g)
        lens_back = tie(lens, es)
        from_x, from_y = send_xy(es[3], es[2])
    for seq in range(max(1, count - 1), count):
        thirds = attend_back(seq, lens_back, packed, lse, mixed_grad, 2, thirds)
    order_p = order
    if ring:
        from_x, from_y = tie((from_x, from_y), thirds[0])
        mine_z, parts_z = scatter_z(es[0], es[1], from_y, from_x, z)
        order_p = tie(order, parts_z)
        arrived_e = send_z(parts_z)
    thirds_flat = [flat(t) for t in thirds]
    project_far = weight_grad(0, order_p, flat(normed), thirds_flat, 3 * width)
    order_near = order
    if ring:
        order_near = tie(order, project_far)
        arrived = send(project_far, CORE)
    project_near = weight_grad(1, order_near, flat(normed), thirds_flat, 3 * width)
    lens_one = lens
    if ring:
        ps = near_sum(pos, project_near, arrived)
        lens_one = tie(lens, ps)
        from_x, from_y = send_xy(ps[2], ps[3])
    input_grad, gain_one_grad, bias_one_grad, query_sum, value_sum = norm_one_back(
        lens_one, *thirds, project_w, x, grad_resid, full[0]
    )
    lens_out = lens
    if ring:
        from_x, from_y, arrived_e = tie((from_x, from_y, arrived_e), gain_one_grad)
        ps = scatter_far(ps[0], ps[1], from_x, from_y, g)
        spread_e = spread(mine_z, arrived_e)
        lens_out = tie(lens, ps, spread_e)
        from_x, from_y = send_xy(ps[3], ps[2])
        near_e = send_near(spread_e)
    layer_output = reduce_out(lens_out, resid, act, reduce_w, full[11])
    vectors = {
        0: gain_one_grad,
        1: bias_one_grad,
        3: jnp.concatenate([query_sum, value_sum], -1),
        5: output_b_grad,
        6: gain_two_grad,
        7: bias_two_grad,
        9: hidden_sum,
        11: up_sum,
    }
    sums = {}
    if ring:
        (from_x, from_y, near_e), layer_output = lax.optimization_barrier(
            ((from_x, from_y, near_e), layer_output)
        )
        mine_z, parts_z = scatter_z(ps[0], ps[1], from_y, from_x, z)
        arrived_p = send_z(parts_z)
        sums.update(reduce_vectors(vectors, shards, ring, parts_z))
        sums[10] = placed(spread_r, near_r, g)
        joint_sum = placed(spread_e, near_e, g)
        spread_p = spread(mine_z, arrived_p)
        sums[2] = placed(spread_p, send_near(spread_p), g)
    else:
        sums.update(reduce_vectors(vectors, shards, ring))
        sums[10] = plain_sum(reduce_far, reduce_near)
        joint_sum = plain_sum(joint_far, joint_near)
        sums[2] = plain_sum(project_far, project_near)
    sums[4] = joint_sum[:, :width]
    sums[8] = joint_sum[:, width:]
    return (
        layer_output.reshape(layer_input.shape),
        input_grad.reshape(layer_input.shape),
        *[sums[i] for i in range(12)],
    )


def solution(mesh):
    ring = mesh.shape["group"] == 4 and mesh.shape["dp"] == 2 * Z
    rows = P(None, ("group", "dp"), None, None)
    vec = P("dp")
    mat = P("dp", None)
    kinds = (vec, vec, mat, vec, mat, vec, vec, vec, mat, vec, mat, vec)
    return jax.shard_map(
        functools.partial(local, ring),
        mesh=mesh,
        in_specs=(rows, P(None, ("group", "dp")), *kinds, rows),
        out_specs=(rows, rows, *kinds),
        check_vma=False,
    )
```

```python
import functools

import jax
import jax.numpy as jnp
from jax import lax
from jax.experimental import pallas as pl
from jax.experimental.pallas import tpu as pltpu
from jax.sharding import PartitionSpec as P

F32 = jnp.float32
BF16 = jnp.bfloat16
EPS = 1e-06
H = 16
E = 64
LANES = 128
HALF_ROOT = 2.0 ** -0.5
INV_ROOT_TAU = 0.3989422804014327
NN = (((1,), (0,)), ((), ()))
NT = (((1,), (1,)), ((), ()))
TN = (((0,), (0,)), ((), ()))


def mm(former, latter, dims=NN):
    return lax.dot_general(former, latter, dims, preferred_element_type=F32)


def params(mib):
    return pltpu.CompilerParams(vmem_limit_bytes=mib << 20, dimension_semantics=("arbitrary",))


def cost(flops, nbytes, other=0):
    return pl.CostEstimate(flops=int(flops), bytes_accessed=int(nbytes), transcendentals=int(other))


def once(shape):
    return pl.BlockSpec(memory_space=pltpu.VMEM)


def valid_rows(length, rows):
    return (lax.broadcasted_iota(jnp.int32, (rows, 1), 0) < length).astype(F32)


def norm_parts(values):
    centred = values - jnp.mean(values, -1, keepdims=True)
    scale = lax.rsqrt(jnp.mean(centred * centred, -1, keepdims=True) + EPS)
    return centred * scale, scale


def norm_back(unit, scale, grad, gain):
    grad_unit = grad * gain
    first = jnp.mean(grad_unit, -1, keepdims=True)
    second = jnp.mean(grad_unit * unit, -1, keepdims=True)
    return scale * (grad_unit - first - unit * second)


def far(shape, dtype):
    return pltpu.HBM(shape, dtype)


def held(array):
    return pltpu.with_memory_space_constraint(array, pltpu.HBM)


def column_sum(values):
    return jnp.sum(values, 0, keepdims=True)


def add_first(step, ref, value):
    @pl.when(step == 0)
    def _():
        ref[...] = value

    @pl.when(step > 0)
    def _():
        ref[...] += value


def collect(ring, pos, pieces, whole, sems):
    copies = []

    def put(source, target):
        copy = pltpu.make_async_copy(source, target, sems.at[len(copies)])
        copy.start()
        copies.append(copy)

    if not ring:
        put(pieces[0], whole)
    else:
        g, z, c = pos[0], pos[1], pos[2]
        for at in range(2):
            core = c if at == 0 else 1 - c
            own, near, far = pieces[3 * at : 3 * at + 3]
            put(own, whole.at[z, core])
            for k in range(1, Z):
                row = lax.rem(z + Z - k, Z)
                for over in range(3):
                    put(near.at[over, :, k - 1], whole.at[row, core, g ^ over])
                for part in range(2):
                    put(far.at[part, k - 1], whole.at[row, core, g ^ 3, part])
    for copy in copies:
        copy.wait()


def whole_shape(ring, pieces):
    if ring:
        return (Z, 2) + pieces[0].shape
    return pieces[0].shape


def collect_scratch(ring, pieces):
    return [
        pltpu.VMEM(whole_shape(ring, pieces), BF16),
        pltpu.SemaphoreType.DMA((32,)),
        pltpu.SemaphoreType.DMA,
    ]


def fill(ring, step, steps, pos, pieces, kept, whole, sems, sem):
    @pl.when(step == 0)
    def _():
        collect(ring, pos, pieces, whole, sems)
        pltpu.make_async_copy(whole, kept, sem).start()


def keep(step, steps, kept, whole, sem):
    @pl.when(step == steps - 1)
    def _():
        pltpu.make_async_copy(whole, kept, sem).wait()


def flat_rows(whole):
    value = whole[...]
    return value.reshape(-1, value.shape[-1])


def project_kernel(ring, count, rows_each, lengths, pos, x, cot, *refs):
    normed, packed, up, up_sum, kept, table, whole, sems, sem, weight_bias = refs[-10:]
    pieces = refs[:-10] if ring else refs[:-12]
    step = pl.program_id(0)
    fill(ring, step, count, pos, pieces, kept, whole, sems, sem)
    rows, width = x.shape[1:]

    @pl.when(step == 0)
    def _():
        if ring:
            columns = whole[..., 3 * width :].reshape(width, LANES).astype(F32)
            table[...] = columns.T[: table.shape[0], :]
            weight_bias[...] = jnp.zeros(weight_bias.shape, F32)
            for shard in range(width // rows_each):
                for part in range(2):
                    at = (2 * shard + part) * rows_each
                    at += width if at >= width else 0
                    source = table[2 + part : 3 + part, shard * rows_each : (shard + 1) * rows_each]
                    weight_bias[:, at : at + rows_each] = source
        else:
            table[...] = refs[-12][...]
            weight_bias[...] = refs[-11][...]

    valid = valid_rows(lengths[step], rows)
    unit, _ = norm_parts(x[0].astype(F32) * valid)
    low = (unit * table[0:1, :] + table[1:2, :]).astype(BF16)
    normed[0] = low
    weight = whole[..., : 3 * width].reshape(width, 3 * width)
    packed[0] = (mm(low, weight) + weight_bias[...]).astype(BF16)
    upstream = cot[0].astype(F32) * valid
    up[0] = upstream.astype(BF16)
    add_first(step, up_sum, column_sum(upstream))
    keep(step, count, kept, whole, sem)


def project(ring, rows_each, lengths, pos, x, cot, pieces, vectors=()):
    seqs, rows, width = x.shape
    wide = 3 * width
    row_block = pl.BlockSpec((1, rows, width), lambda s, *_: (s, 0, 0))
    anywhere = pl.BlockSpec(memory_space=pl.ANY)
    normed, packed, up, up_sum, kept, table = pl.pallas_call(
        functools.partial(project_kernel, ring, seqs, rows_each),
        grid_spec=pltpu.PrefetchScalarGridSpec(
            num_scalar_prefetch=2,
            grid=(seqs,),
            in_specs=[row_block, row_block]
            + [anywhere] * len(pieces)
            + [once(v.shape) for v in vectors],
            out_specs=[
                row_block,
                pl.BlockSpec((1, rows, wide), lambda s, *_: (s, 0, 0)),
                row_block,
                pl.BlockSpec((1, width), lambda s, *_: (0, 0)),
                anywhere,
                pl.BlockSpec((16, width), lambda s, *_: (0, 0)),
            ],
            scratch_shapes=collect_scratch(ring, pieces) + [pltpu.VMEM((1, wide), F32)],
        ),
        out_shape=[
            jax.ShapeDtypeStruct(x.shape, BF16),
            far((seqs, rows, wide), BF16),
            jax.ShapeDtypeStruct(x.shape, BF16),
            jax.ShapeDtypeStruct((1, width), F32),
            far(whole_shape(ring, pieces), BF16),
            jax.ShapeDtypeStruct((16, width), F32),
        ],
        compiler_params=params(30),
        cost_estimate=cost(2 * seqs * rows * width * wide, seqs * rows * (4 * width + wide) * 2 + 4 * width * wide),
        name="norm_project",
    )(lengths, pos, x, cot, *pieces, *vectors)
    return normed, packed, up, up_sum, kept.reshape(width, -1), table


LEAST = 256
RATE = E**-0.5 * 1.4426950408889634


def attend_kernel(seq, lengths, q, k, v, *refs):
    mixed, lse = refs[-2:]
    rows = q.shape[1]
    length = lengths[seq]
    key_ok = lax.broadcasted_iota(jnp.int32, (1, rows - LEAST), 1) + LEAST < length
    lane = lax.broadcasted_iota(jnp.int32, (rows, LANES), 1)
    low_lane = lane < E
    logs = jnp.zeros((rows, LANES), F32)
    for pair in range(q.shape[2] // LANES):
        at = slice(pair * LANES, (pair + 1) * LANES)
        qs, ks, vs = q[0, :, at], k[0, :, at], v[0, :, at]
        outs = []
        for head in range(2):
            keep = low_lane if head == 0 else ~low_lane
            scores = mm(jnp.where(keep, qs, jnp.zeros_like(qs)), ks, NT)
            scores = jnp.concatenate(
                [scores[:, :LEAST], jnp.where(key_ok, scores[:, LEAST:], -1e30)], 1
            )
            top = jnp.max(scores, -1, keepdims=True)
            weights = jnp.exp2((scores - top) * RATE)
            total = jnp.sum(weights, -1, keepdims=True)
            outs.append(mm(weights.astype(BF16), vs) * (1.0 / total))
            logs = jnp.where(lane == 2 * pair + head, top * RATE + jnp.log2(total), logs)
        mixed[0, :, at] = jnp.where(low_lane, outs[0], outs[1]).astype(BF16)
    lse[0, 0] = logs.T[: lse.shape[2], :]


def attend(seq, lengths, packed, earlier=()):
    seqs, rows, wide = packed.shape
    width = wide // 3
    wid = 4 * LANES
    steps = width // wid
    block = lambda part: pl.BlockSpec((1, rows, wid), lambda j, *_: (seq, 0, part * steps + j))
    return pl.pallas_call(
        functools.partial(attend_kernel, seq),
        grid_spec=pltpu.PrefetchScalarGridSpec(
            num_scalar_prefetch=1,
            grid=(steps,),
            in_specs=[block(0), block(1), block(2)]
            + [pl.BlockSpec(memory_space=pl.ANY)] * len(earlier),
            out_specs=[
                pl.BlockSpec((1, rows, wid), lambda j, *_: (seq, 0, j)),
                pl.BlockSpec((1, 1, 8, rows), lambda j, *_: (seq, j, 0, 0)),
            ],
        ),
        out_shape=[
            jax.ShapeDtypeStruct((seqs, rows, width), BF16),
            jax.ShapeDtypeStruct((seqs, steps, 8, rows), F32),
        ],
        input_output_aliases={4: 0, 5: 1} if earlier else {},
        compiler_params=params(16),
        cost_estimate=cost(4 * rows * rows * width * 8, rows * wide * 3, H * rows * rows),
        name="attend",
    )(lengths, *[held(packed)] * 3, *earlier)


def attend_back_kernel(seq, lengths, q, k, v, lse, grad, *refs):
    out = refs[-1]
    rows = q.shape[1]
    length = lengths[seq + pl.program_id(0)]
    key_ok = lax.broadcasted_iota(jnp.int32, (rows - LEAST, 1), 0) + LEAST < length
    low_lane = lax.broadcasted_iota(jnp.int32, (rows, LANES), 1) < E
    for pair in range(q.shape[2] // LANES):
        at = slice(pair * LANES, (pair + 1) * LANES)
        qs, ks, vs, gs = q[0, :, at], k[0, :, at], v[0, :, at], grad[0, :, at]
        sums = []
        for head in range(2):
            keep = low_lane if head == 0 else ~low_lane
            scores = mm(jnp.where(keep, ks, jnp.zeros_like(ks)), qs, NT)
            grad_probs = mm(jnp.where(keep, vs, jnp.zeros_like(vs)), gs, NT)
            row = 2 * pair + head
            probs = jnp.exp2(scores * RATE - lse[0, 0, row : row + 1, :])
            probs = jnp.concatenate(
                [probs[:LEAST], jnp.where(key_ok, probs[LEAST:], 0.0)], 0
            )
            inner = jnp.sum(grad_probs * probs, 0, keepdims=True)
            grad_scores = (probs * (grad_probs - inner)).astype(BF16)
            sums.append(
                (
                    mm(grad_scores, ks, TN) * E**-0.5,
                    mm(grad_scores, qs) * E**-0.5,
                    mm(probs.astype(BF16), gs),
                )
            )
        for part, first, second in zip(range(3), sums[0], sums[1]):
            out[0, part, :, at] = jnp.where(low_lane, first, second).astype(BF16)


def attend_back(seq, here, lengths, packed, lse, grad, earlier=()):
    seqs, rows, wide = packed.shape
    width = wide // 3
    wid = 4 * LANES
    steps = width // wid
    block = lambda part: pl.BlockSpec(
        (1, rows, wid), lambda s, j, *_: (seq + s, 0, part * steps + j)
    )
    return pl.pallas_call(
        functools.partial(attend_back_kernel, seq),
        grid_spec=pltpu.PrefetchScalarGridSpec(
            num_scalar_prefetch=1,
            grid=(here, steps),
            in_specs=[
                block(0),
                block(1),
                block(2),
                pl.BlockSpec((1, 1, 8, rows), lambda s, j, *_: (seq + s, j, 0, 0)),
                pl.BlockSpec((1, rows, wid), lambda s, j, *_: (seq + s, 0, j)),
            ]
            + [pl.BlockSpec(memory_space=pl.ANY)] * len(earlier),
            out_specs=pl.BlockSpec((1, 3, rows, wid), lambda s, j, *_: (seq + s, 0, 0, j)),
        ),
        out_shape=far((seqs, 3, rows, width), BF16),
        input_output_aliases={6: 0} if earlier else {},
        compiler_params=pltpu.CompilerParams(
            vmem_limit_bytes=18 << 20, dimension_semantics=("arbitrary",) * 2
        ),
        cost_estimate=cost(10 * here * rows * rows * width * 8, here * rows * wide * 5, here * H * rows * rows),
        name="attend_back",
    )(lengths, *[held(packed)] * 3, lse, grad, *[held(a) for a in earlier])


def branch_kernel(ring, count, lengths, pos, x, mixed, table, *refs):
    pieces, (resid, normed, kept, whole, sems, sem) = refs[:-6], refs[-6:]
    step = pl.program_id(0)
    fill(ring, step, count, pos, pieces, kept, whole, sems, sem)
    rows, width = x.shape[1:]
    valid = valid_rows(lengths[step], rows)
    weight = whole[..., :width].reshape(-1, width)
    total = x[0].astype(F32) * valid + mm(mixed[0], weight) + table[4:5, :]
    resid[0] = total
    unit, _ = norm_parts(total)
    normed[0] = (unit * table[5:6, :] + table[6:7, :]).astype(BF16)
    keep(step, count, kept, whole, sem)


def branch(ring, lengths, pos, x, mixed, table, pieces):
    seqs, rows, width = x.shape
    wide = pieces[0].shape[-1]
    row_block = pl.BlockSpec((1, rows, width), lambda s, *_: (s, 0, 0))
    anywhere = pl.BlockSpec(memory_space=pl.ANY)
    resid, normed, kept = pl.pallas_call(
        functools.partial(branch_kernel, ring, seqs),
        grid_spec=pltpu.PrefetchScalarGridSpec(
            num_scalar_prefetch=2,
            grid=(seqs,),
            in_specs=[row_block, row_block, once(table.shape)] + [anywhere] * len(pieces),
            out_specs=[row_block, row_block, anywhere],
            scratch_shapes=collect_scratch(ring, pieces),
        ),
        out_shape=[
            far(x.shape, F32),
            jax.ShapeDtypeStruct(x.shape, BF16),
            far(whole_shape(ring, pieces), BF16),
        ],
        compiler_params=params(26),
        cost_estimate=cost(2 * seqs * rows * width * width, seqs * rows * width * 10 + 4 * width * wide),
        name="branch",
    )(lengths, pos, x, mixed, table, *pieces)
    return resid, normed, kept.reshape(-1, wide)


def store_halves(ref, value):
    _, shards, quarters, rows, _ = ref.shape
    for shard in range(shards):
        for quarter in range(quarters):
            for half in range(2):
                at = ((shard * quarters + quarter) * 2 + half) * rows
                ref[half, shard, quarter] = value[at : at + rows]


def expand_kernel(seqs, normed, up, weight, bias, act, slope, grad):
    rows = normed.shape[0] // seqs
    for s in range(seqs):
        at = slice(s * rows, (s + 1) * rows)
        hidden = mm(normed[at, :], weight[...]) + bias[...]
        phi = 0.5 + 0.5 * lax.erf(hidden * HALF_ROOT)
        act[at, :] = (hidden * phi).astype(BF16)
        slope[at, :] = (phi + hidden * (INV_ROOT_TAU * jnp.exp(-0.5 * hidden * hidden))).astype(BF16)
    grad[...] = mm(act[...], up[...], TN).astype(BF16)


def expand(seqs, normed, up, weight, bias):
    count, width = normed.shape
    hidden = bias.shape[1]
    size = hidden // 8
    skip = (weight.shape[1] - hidden) // size
    wide = pl.BlockSpec((count, size), lambda i: (0, i))
    shape = far((count, hidden), BF16)
    return pl.pallas_call(
        functools.partial(expand_kernel, seqs),
        grid=(8,),
        in_specs=[
            once((count, width)),
            once((count, width)),
            pl.BlockSpec((width, size), lambda i: (0, skip + i)),
            pl.BlockSpec((1, size), lambda i: (0, i)),
        ],
        out_specs=[wide, wide, pl.BlockSpec((size, width), lambda i: (i, 0))],
        out_shape=[shape, shape, far((hidden, width), BF16)],
        compiler_params=params(26),
        cost_estimate=cost(4 * count * width * hidden, count * hidden * 4 + width * hidden * 4, count * hidden),
        name="expand",
    )(normed, up, held(weight), bias)


def reduce_kernel(lengths, resid, act, weight, table, out):
    rows = resid.shape[1]
    valid = valid_rows(lengths[pl.program_id(0)], rows)
    out[0] = (resid[0] + mm(act[0], weight[...]) + table[11:12, :]) * valid


def reduce_out(lengths, resid, act, weight, table):
    seqs, rows, width = resid.shape
    hidden = weight.shape[0]
    row_block = pl.BlockSpec((1, rows, width), lambda s, *_: (s, 0, 0))
    return pl.pallas_call(
        reduce_kernel,
        grid_spec=pltpu.PrefetchScalarGridSpec(
            num_scalar_prefetch=1,
            grid=(seqs,),
            in_specs=[
                row_block,
                pl.BlockSpec((1, rows, hidden), lambda s, *_: (s, 0, 0)),
                once((hidden, width)),
                once(table.shape),
            ],
            out_specs=row_block,
        ),
        out_shape=far(resid.shape, F32),
        compiler_params=params(26),
        cost_estimate=cost(2 * seqs * rows * width * hidden, seqs * rows * (8 * width + 2 * hidden) + 2 * width * hidden),
        name="reduce_out",
    )(lengths, held(resid), held(act.reshape(seqs, rows, hidden)), weight, table)


def hidden_back_kernel(seqs, up, weight, slope, grad, grad_sum):
    rows = up.shape[0] // seqs
    total = None
    for s in range(seqs):
        at = slice(s * rows, (s + 1) * rows)
        low = (mm(up[at, :], weight[...], NT) * slope[at, :].astype(F32)).astype(BF16)
        grad[at, :] = low
        part = column_sum(low.astype(F32))
        total = part if s == 0 else total + part
    grad_sum[...] = total


def hidden_back(seqs, up, weight, slope):
    count, width = up.shape
    hidden = slope.shape[1]
    size = hidden // 8
    wide = pl.BlockSpec((count, size), lambda i: (0, i))
    return pl.pallas_call(
        functools.partial(hidden_back_kernel, seqs),
        grid=(8,),
        in_specs=[once((count, width)), pl.BlockSpec((size, width), lambda i: (i, 0)), wide],
        out_specs=[wide, pl.BlockSpec((1, size), lambda i: (0, i))],
        out_shape=[far((count, hidden), BF16), jax.ShapeDtypeStruct((1, hidden), F32)],
        compiler_params=params(20),
        cost_estimate=cost(2 * count * width * hidden, count * hidden * 4 + 2 * width * hidden),
        name="hidden_back",
    )(up, held(weight), held(slope))


def whole_grad_kernel(inputs, grads, *refs):
    refs[-1][...] = mm(inputs[...], grads[...], TN).astype(BF16)


def whole_grad(inputs, grads, wide, first=0, earlier=()):
    count, width = inputs.shape
    here = grads.shape[1]
    size = 512
    return pl.pallas_call(
        whole_grad_kernel,
        grid=(here // size,),
        in_specs=[once((count, width)), pl.BlockSpec((count, size), lambda j: (0, j))]
        + [pl.BlockSpec(memory_space=pl.ANY)] * len(earlier),
        out_specs=pl.BlockSpec((width, size), lambda j: (0, first // size + j)),
        out_shape=far((width, wide), BF16),
        input_output_aliases={2: 0} if earlier else {},
        compiler_params=params(20),
        cost_estimate=cost(2 * count * width * here, count * (width + here) * 2 + 2 * width * here),
        name="whole_grad",
    )(inputs, held(grads), *[held(a) for a in earlier])


def store_halves(ref, value):
    _, shards, quarters, rows, _ = ref.shape
    for shard in range(shards):
        for quarter in range(quarters):
            for half in range(2):
                at = ((shard * quarters + quarter) * 2 + half) * rows
                ref[half, shard, quarter] = value[at : at + rows]


def weight_grad_kernel(half, order, inputs, grads, *refs):
    out, picked = refs[-2:]

    @pl.when(pl.program_id(0) == 0)
    def _():
        for i in range(4):
            size = picked.shape[1] // 4
            at = pl.multiple_of((order[0] * i + order[1 + half]) * size, size)
            picked[:, i * size : (i + 1) * size] = inputs[:, pl.ds(at, size)]

    block = grads[...].reshape(inputs.shape[0], grads.shape[-1])
    store_halves(out, mm(picked[...], block, TN).astype(BF16))


def weight_grad(half, order, inputs, grads, wide, first=0, earlier=()):
    count, width = inputs.shape
    seqs, parts, each, size = grads.shape
    rows = width // 64
    return pl.pallas_call(
        functools.partial(weight_grad_kernel, half),
        grid_spec=pltpu.PrefetchScalarGridSpec(
            num_scalar_prefetch=1,
            grid=(parts,),
            in_specs=[
                once((count, width)),
                pl.BlockSpec((seqs, 1, each, size), lambda j, *_: (0, j, 0, 0)),
            ]
            + [pl.BlockSpec(memory_space=pl.ANY)] * len(earlier),
            out_specs=pl.BlockSpec(
                (2, 4, 4, rows, size), lambda j, *_: (0, 0, 0, 0, first // size + j)
            ),
            scratch_shapes=[pltpu.VMEM((count, width // 2), BF16)],
        ),
        out_shape=jax.ShapeDtypeStruct((2, 4, 4, rows, wide), BF16),
        input_output_aliases={3: 0} if earlier else {},
        compiler_params=params(20),
        cost_estimate=cost(count * width * parts * size, count * (width + parts * size) * 2 + width * parts * size),
        name="weight_grad",
    )(order, inputs, grads, *earlier)


def norm_two_kernel(lengths, hidden_grad, weight, resid, cot, table, *outs):
    grad_resid, low_ref, mixed_grad, gain_grad, bias_grad, out_bias_grad = outs
    step = pl.program_id(0)
    rows, width = resid.shape[1:]
    valid = valid_rows(lengths[step], rows)
    grad = mm(hidden_grad[0], weight[:, width:], NT)
    unit, scale = norm_parts(resid[0])
    total = cot[0].astype(F32) * valid + norm_back(unit, scale, grad, table[5:6, :])
    grad_resid[0] = total
    low = total.astype(BF16)
    low_ref[0] = low
    mixed_grad[0] = mm(low, weight[:, :width], NT).astype(BF16)
    add_first(step, gain_grad, column_sum(grad * unit))
    add_first(step, bias_grad, column_sum(grad))
    add_first(step, out_bias_grad, column_sum(low.astype(F32)))


def norm_two_back(lengths, hidden_grad, weight, resid, cot, table):
    seqs, rows, width = resid.shape
    hidden = hidden_grad.shape[1]
    row_block = pl.BlockSpec((1, rows, width), lambda s, *_: (s, 0, 0))
    vec = pl.BlockSpec((1, width), lambda s, *_: (0, 0))
    return pl.pallas_call(
        norm_two_kernel,
        grid_spec=pltpu.PrefetchScalarGridSpec(
            num_scalar_prefetch=1,
            grid=(seqs,),
            in_specs=[
                pl.BlockSpec((1, rows, hidden), lambda s, *_: (s, 0, 0)),
                once((width, width + hidden)),
                row_block,
                row_block,
                once(table.shape),
            ],
            out_specs=[row_block] * 3 + [vec] * 3,
        ),
        out_shape=[
            far(resid.shape, F32),
            jax.ShapeDtypeStruct(resid.shape, BF16),
            jax.ShapeDtypeStruct(resid.shape, BF16),
        ]
        + [jax.ShapeDtypeStruct((1, width), F32)] * 3,
        compiler_params=params(40),
        cost_estimate=cost(2 * seqs * rows * width * (hidden + width), seqs * rows * (2 * hidden + 14 * width)),
        name="norm_two_back",
    )(lengths, held(hidden_grad.reshape(seqs, rows, hidden)), weight, held(resid), cot, table)


def norm_one_kernel(lengths, thirds, weight, x, grad_resid, table, *outs):
    input_grad, gain_grad, bias_grad, q_sum, v_sum = outs
    step = pl.program_id(0)
    rows, width = x.shape[1:]
    valid = valid_rows(lengths[step], rows)
    grad = mm(thirds[0, 0], weight[:, :width], NT)
    grad += mm(thirds[0, 1], weight[:, width : 2 * width], NT)
    grad += mm(thirds[0, 2], weight[:, 2 * width : 3 * width], NT)
    unit, scale = norm_parts(x[0].astype(F32) * valid)
    input_grad[0] = (grad_resid[0] + norm_back(unit, scale, grad, table[0:1, :])) * valid
    add_first(step, gain_grad, column_sum(grad * unit))
    add_first(step, bias_grad, column_sum(grad))
    add_first(step, q_sum, column_sum(thirds[0, 0].astype(F32)))
    add_first(step, v_sum, column_sum(thirds[0, 2].astype(F32)))


def norm_one_back(lengths, thirds, weight, x, grad_resid, table):
    seqs, rows, width = x.shape
    row_block = pl.BlockSpec((1, rows, width), lambda s, *_: (s, 0, 0))
    vec = pl.BlockSpec((1, width), lambda s, *_: (0, 0))
    return pl.pallas_call(
        norm_one_kernel,
        grid_spec=pltpu.PrefetchScalarGridSpec(
            num_scalar_prefetch=1,
            grid=(seqs,),
            in_specs=[
                pl.BlockSpec((1, 3, rows, width), lambda s, *_: (s, 0, 0, 0)),
            ]
            + [once(weight.shape), row_block, row_block, once(table.shape)],
            out_specs=[row_block] + [vec] * 4,
        ),
        out_shape=[far(x.shape, F32)] + [jax.ShapeDtypeStruct((1, width), F32)] * 4,
        compiler_params=params(32),
        cost_estimate=cost(6 * seqs * rows * width * width, seqs * rows * width * 16 + 6 * width * width),
        name="norm_one_back",
    )(lengths, held(thirds), weight, x, held(grad_resid), table)

def near_kernel(pos, *refs):
    for at in range(4):
        mine, other, out = refs[at], refs[4 + at], refs[8 + at]
        total = mine[...].astype(F32) + other[...].astype(F32)
        out[...] = total.astype(BF16).reshape(out.shape)


def near_sum(pos, own, arrived):
    _, shards, _, rows, wide = own.shape
    x = lambda pos: pos[0] % 2
    y = lambda pos: pos[0] // 2
    over_x = (1, 1, 2, 1, rows, wide)
    over_y = (1, 1, 1, 2, rows, wide)
    specs = [
        pl.BlockSpec(over_x, lambda s, pos: (0, s, 0, x(pos), 0, 0)),
        pl.BlockSpec(over_y, lambda s, pos: (1, s, y(pos), 0, 0, 0)),
        pl.BlockSpec(over_x, lambda s, pos: (0, s, 0, 1 - x(pos), 0, 0)),
        pl.BlockSpec(over_y, lambda s, pos: (1, s, 1 - y(pos), 0, 0, 0)),
    ]
    shape = (2, shards, 2, 2, rows, wide)
    return pl.pallas_call(
        near_kernel,
        grid_spec=pltpu.PrefetchScalarGridSpec(
            num_scalar_prefetch=1,
            grid=(shards,),
            in_specs=specs * 2,
            out_specs=[pl.BlockSpec((1, 2, rows, wide), lambda s, pos: (s, 0, 0, 0))] * 4,
        ),
        out_shape=[jax.ShapeDtypeStruct((shards, 2, rows, wide), BF16)] * 4,
        compiler_params=params(14),
        cost_estimate=cost(own.size, own.size * 6),
        name="near_sum",
    )(pos, *[own.reshape(shape)] * 4, *[arrived.reshape(shape)] * 4)


AXES = ("group", "dp")
Z = 4


def permutation(move):
    pairs = []
    for g in range(4):
        for d in range(2 * Z):
            to_g, to_z, to_c = move(g, d // 2, d % 2)
            pairs.append((g * 2 * Z + d, (to_g * Z + to_z) * 2 + to_c))
    return pairs


CORE = permutation(lambda g, z, c: (g, z, 1 - c))
OVER_X = permutation(lambda g, z, c: (g ^ 1, z, c))
OVER_Y = permutation(lambda g, z, c: (g ^ 2, z, c))
OVER_XY = permutation(lambda g, z, c: (g ^ 3, z, c))
OVER_Z = [permutation(lambda g, z, c, k=k: (g, (z + k) % Z, c)) for k in range(Z)]
NEAR_Z = permutation(lambda g, z, c: (g, z ^ 1, c))
FAR_Z = permutation(lambda g, z, c: (g, z ^ 2, c))


def send(array, pairs):
    return lax.ppermute(array, AXES, pairs)


def tie(value, *others):
    return lax.optimization_barrier((value,) + others)[0]


def pick(array, index, axis):
    return lax.dynamic_index_in_dim(array, index, axis, keepdims=False)


def plus(former, latter):
    return (former.astype(F32) + latter.astype(F32)).astype(BF16)


def quarters(shard, g):
    rows, wide = shard.shape
    parts = shard.reshape(4, 2, rows // 8, wide)
    return parts, pick(parts, g, 0)


def send_quarter(mine):
    return [send(mine, OVER_Z[k]) for k in range(1, Z)]


def send_xy(first, second):
    return send(first, OVER_X), send(second, OVER_Y)


def scatter_core(other):
    return send(other, CORE)


def scatter_far(first, second, from_x, from_y, g):
    x, y = g % 2, g // 2
    first = plus(first, from_x)
    second = plus(second, from_y)
    return pick(first, y, 1), pick(second, x, 1), pick(first, 1 - y, 1), pick(second, 1 - x, 1)


def scatter_z(first, second, from_y, from_x, z):
    quarter = jnp.stack([plus(first, from_y), plus(second, from_x)], 1)
    return pick(quarter, z, 0), [pick(quarter, (z + k) % Z, 0) for k in range(1, Z)]


def send_z(parts):
    return [send(part, OVER_Z[k]) for k, part in enumerate(parts, 1)]


def spread(mine, arrived):
    total = mine.astype(F32)
    for part in arrived:
        total = total + part.astype(F32)
    return total.astype(BF16)


def send_near(mine):
    return [send(mine, OVER_X), send(mine, OVER_Y), send(mine, OVER_XY)]


def placed(mine, others, g):
    grid = jnp.stack([mine, *others]).reshape(2, 2, *mine.shape)
    grid = jnp.where(g % 2 == 1, grid[:, ::-1], grid)
    grid = jnp.where(g // 2 == 1, grid[::-1], grid)
    return grid.astype(F32).reshape(-1, mine.shape[-1])


def trade(shard, g):
    rows, wide = shard.shape
    parts = shard.reshape(4, rows // 4, wide)
    return pick(parts, g, 0), [pick(parts, g ^ over, 0) for over in (1, 2, 3)]


def send_trade(parts):
    return [send(part, pairs) for part, pairs in zip(parts, (OVER_X, OVER_Y, OVER_XY))]


VEC = (0, 1, 3, 5, 6, 7, 9, 11)


def joined(vectors):
    total = sum(v.shape[0] for v in vectors)
    at = 0
    out = None
    for v in vectors:
        wide = lax.pad(v, jnp.zeros((), v.dtype), [(at, total - at - v.shape[0], 0)])
        out = wide if out is None else out + wide
        at += v.shape[0]
    return out


def widened(weight, vectors):
    rows = weight.shape[0]
    columns = joined(vectors).reshape(-1, rows).T
    columns = jnp.pad(columns, ((0, 0), (0, LANES - columns.shape[1])))
    return jnp.concatenate([weight, columns], 1)


def spaced(table, first, last, rows):
    part = table[first:last].reshape(last - first, -1, rows)
    return part.transpose(1, 0, 2).reshape(1, -1)


def packed_vectors(grads):
    return joined([grads[i].reshape(-1) for i in VEC])


def own_vectors(total, grads, shards):
    d = lax.axis_index("dp")
    at = 0
    summed = {}
    for i in VEC:
        size = shards[i].shape[0]
        summed[i] = lax.dynamic_slice(total, (at + d * size,), (size,))
        at += grads[i].size
    return summed


def over_dp(array):
    return lax.psum_scatter(array, "dp", scatter_dimension=0, tiled=True)


def local(ring, layer_input, lengths, *rest):
    shards, cot = rest[:12], rest[12]
    micro, seqs, rows, width = layer_input.shape
    count = micro * seqs
    g = lax.axis_index("group")
    d = lax.axis_index("dp")
    z, c = d // 2, d % 2
    pos = jnp.stack([g, z, c]).astype(jnp.int32)
    order = [2, 1 - c, c] if ring else [1, 0, 4]
    order = jnp.stack([jnp.asarray(v, jnp.int32) for v in order])
    lens = lengths.reshape(-1)
    x = layer_input.reshape(count, rows, width)
    cot = cot.reshape(count, rows, width)
    flat = lambda a: a.reshape(count * rows, a.shape[-1])
    rows_each = shards[2].shape[0]
    wanted = (widened(shards[2], [shards[i] for i in VEC]), jnp.concatenate([shards[4], shards[8]], 1), shards[10])

    if ring:
        parts_p, mine_p = quarters(wanted[0], g)
        parts_e, mine_e = quarters(wanted[1], g)
        ring_p = send_quarter(mine_p)
        core_p, core_e = send(parts_p, CORE), send(parts_e, CORE)
        stack_p = jnp.stack(tie(ring_p, core_p, core_e), 1)
        x_p, y_p = send_xy(stack_p, stack_p)
        mine_e = tie(mine_e, stack_p)
        e_one, e_three = send(mine_e, OVER_Z[1]), send(mine_e, OVER_Z[3])
        x_p, y_p, e_one, e_three, mine_e = tie((x_p, y_p, e_one, e_three, mine_e))
        b_p, a_p = send_xy(y_p[1], x_p[0])
        e_two = send(mine_e, OVER_Z[2])
        near_p = tie(jnp.stack([stack_p, x_p, y_p]), a_p, b_p)
        far_p = jnp.stack([a_p, b_p])
        pieces_p = [parts_p, near_p, far_p, core_p, send(near_p, CORE), send(far_p, CORE)]
        vectors = ()
    else:
        pieces = [lax.all_gather(w, "dp", axis=0, tiled=True) for w in wanted]
        pieces_p, pieces_e, reduce_w = [pieces[0]], [pieces[1]], pieces[2]
        table = pieces[0][:, 3 * width : 3 * width + 16].T.astype(F32)
        pair = spaced(table, 2, 4, rows_each)
        middle = jnp.zeros((1, width), F32)
        vectors = (table, jnp.concatenate([pair[:, :width], middle, pair[:, width:]], -1))
    normed, packed, up, up_sum, project_w, table = project(
        ring, rows_each, lens, pos, x, cot, pieces_p, vectors
    )
    expand_b = spaced(table, 7, 11, rows_each)
    lens_attend = lens
    if ring:
        stack_e = jnp.stack(tie((e_one, e_two, e_three), normed), 1)
        lens_attend, shard_r = tie((lens, wanted[2]), stack_e)
        x_e, y_e = send_xy(stack_e, stack_e)
        reduce_w = lax.all_gather(shard_r, "dp", axis=0, tiled=True)
    mixed, lse = attend(0, lens_attend, packed)
    for seq in range(1, count - 1):
        mixed, lse = attend(seq, lens_attend, packed, (mixed, lse))
    if ring:
        x_e, y_e = tie((x_e, y_e), mixed)
        near_e = jnp.stack([stack_e, x_e, y_e])
        lens_attend = tie(lens, near_e)
        b_e, a_e = send_xy(y_e[1], x_e[0])
        near_core_e = send(near_e, CORE)
    for seq in range(max(1, count - 1), count):
        mixed, lse = attend(seq, lens_attend, packed, (mixed, lse))
    if ring:
        a_e, b_e = tie((a_e, b_e), mixed)
        far_e = jnp.stack([a_e, b_e])
        pieces_e = [parts_e, near_e, far_e, core_e, near_core_e, send(far_e, CORE)]
    resid, normed_two, joint_w = branch(ring, lens, pos, x, mixed, table, pieces_e)
    act, slope, reduce_grad = expand(count, flat(normed_two), flat(up), joint_w, expand_b)
    shard_r = over_dp(reduce_grad)
    hidden_grad, hidden_sum = hidden_back(count, flat(up), reduce_w, slope)
    grad_resid, branch_low, mixed_grad, gain_two_grad, bias_two_grad, output_b_grad = norm_two_back(
        lens, hidden_grad, joint_w, resid, cot, table
    )
    thirds = attend_back(0, 1, lens, packed, lse, mixed_grad)
    expand_grad = whole_grad(flat(normed_two), tie(hidden_grad, thirds), 4 * width)
    shard_e = over_dp(expand_grad)
    lens_back = tie(lens, expand_grad)
    thirds = attend_back(1, count - 1, lens_back, packed, lse, mixed_grad, (thirds,))
    branch_part = branch_low.reshape(count, 1, rows, width)
    project_far = weight_grad(0, order, flat(mixed), branch_part, 4 * width)
    order_far = order
    if ring:
        mine_r, parts_r = trade(tie(shard_r, thirds), g)
        order_far = tie(order, parts_r)
        arrived_r = send_trade(parts_r)
    project_far = weight_grad(
        0, order_far, flat(normed), thirds, 4 * width, width, (project_far,)
    )
    order_near = order
    if ring:
        order_near = tie(order, project_far)
        arrived = send(project_far, CORE)
    project_near = weight_grad(1, order_near, flat(mixed), branch_part, 4 * width)
    project_near = weight_grad(
        1, order_near, flat(normed), thirds, 4 * width, width, (project_near,)
    )
    lens_one = lens
    if ring:
        spread_r = spread(mine_r, tie(arrived_r, project_near))
        ps = near_sum(pos, project_near, arrived)
        lens_one = tie(lens, ps, spread_r)
        from_x, from_y = send_xy(ps[2], ps[3])
    input_grad, gain_one_grad, bias_one_grad, query_sum, value_sum = norm_one_back(
        lens_one, thirds, project_w, x, grad_resid, table
    )
    vectors = {
        0: gain_one_grad,
        1: bias_one_grad,
        3: jnp.concatenate([query_sum, value_sum], -1),
        5: output_b_grad,
        6: gain_two_grad,
        7: bias_two_grad,
        9: hidden_sum,
        11: up_sum,
    }
    total = packed_vectors(vectors)
    lens_out = lens
    if ring:
        total = total.reshape(-1, LANES)
        total = total + send(total, CORE)
        total = (total + send(total, OVER_XY)) + (send(total, OVER_X) + send(total, OVER_Y))
        total, from_x, from_y = tie((total, from_x, from_y))
        ps = scatter_far(ps[0], ps[1], from_x, from_y, g)
        lens_out = tie(lens, ps)
        from_x, from_y = send_xy(ps[3], ps[2])
        column = [send(total, OVER_Z[k]) for k in range(1, Z)]
    layer_output = reduce_out(lens_out, resid, act, reduce_w, table)
    sums = {}
    if ring:
        (from_x, from_y, column), layer_output = lax.optimization_barrier(
            ((from_x, from_y, column), layer_output)
        )
        mine_z, parts_z = scatter_z(ps[0], ps[1], from_y, from_x, z)
        arrived_p = send_z(parts_z)
        spread_r = tie(spread_r, parts_z)
        x_r, y_r = send_xy(spread_r, spread_r)
        half = spread_r.shape[0] // 2
        b_r, a_r = send_xy(y_r[half:], x_r[:half])
        sums[10] = placed(spread_r, [x_r, y_r, jnp.concatenate([a_r, b_r])], g)
        total = (total + column[1]) + (column[0] + column[2])
        mine_e, parts_e = trade(tie(shard_e, (x_r, y_r)), g)
        arrived_e = send_trade(parts_e)
        spread_p = spread(mine_z, tie(arrived_p, parts_e))
        near_p = send_near(spread_p)
        spread_e = spread(mine_e, tie(arrived_e, spread_p))
        near_e = send_near(spread_e)
        joint_sum = placed(spread_p, near_p, g)
        sums[8] = placed(spread_e, near_e, g)
    else:
        total = lax.psum(total, ("group", "dp"))
        sums[10] = lax.psum(shard_r, "group").astype(F32)
        sums[8] = lax.psum(shard_e, "group").astype(F32)
        parts = [a.transpose(1, 2, 0, 3, 4) for a in (project_far, project_near)]
        parts = over_dp(jnp.concatenate(parts).reshape(width, 4 * width))
        joint_sum = lax.psum(parts, "group").astype(F32)
    sums.update(own_vectors(total.reshape(-1), vectors, shards))
    sums[4] = joint_sum[:, :width]
    sums[2] = joint_sum[:, width:]
    return (
        layer_output.reshape(layer_input.shape),
        input_grad.reshape(layer_input.shape),
        *[sums[i] for i in range(12)],
    )


def solution(mesh):
    ring = mesh.shape["group"] == 4 and mesh.shape["dp"] == 2 * Z
    rows = P(None, ("group", "dp"), None, None)
    vec = P("dp")
    mat = P("dp", None)
    kinds = (vec, vec, mat, vec, mat, vec, vec, vec, mat, vec, mat, vec)
    return jax.shard_map(
        functools.partial(local, ring),
        mesh=mesh,
        in_specs=(rows, P(None, ("group", "dp")), *kinds, rows),
        out_specs=(rows, rows, *kinds),
        check_vma=False,
    )
```

```python
import functools

import jax
import jax.numpy as jnp
from jax import lax
from jax.experimental import pallas as pl
from jax.experimental.pallas import tpu as pltpu
from jax.sharding import PartitionSpec as P

F32 = jnp.float32
BF16 = jnp.bfloat16
EPS = 1e-06
H = 16
E = 64
LANES = 128
HALF_ROOT = 2.0 ** -0.5
INV_ROOT_TAU = 0.3989422804014327
NN = (((1,), (0,)), ((), ()))
NT = (((1,), (1,)), ((), ()))
TN = (((0,), (0,)), ((), ()))


def mm(former, latter, dims=NN):
    return lax.dot_general(former, latter, dims, preferred_element_type=F32)


def params(mib):
    return pltpu.CompilerParams(vmem_limit_bytes=mib << 20, dimension_semantics=("arbitrary",))


def cost(flops, nbytes, other=0):
    return pl.CostEstimate(flops=int(flops), bytes_accessed=int(nbytes), transcendentals=int(other))


def once(shape):
    return pl.BlockSpec(memory_space=pltpu.VMEM)


def valid_rows(length, rows):
    return (lax.broadcasted_iota(jnp.int32, (rows, 1), 0) < length).astype(F32)


def norm_parts(values):
    centred = values - jnp.mean(values, -1, keepdims=True)
    scale = lax.rsqrt(jnp.mean(centred * centred, -1, keepdims=True) + EPS)
    return centred * scale, scale


def norm_back(unit, scale, grad, gain):
    grad_unit = grad * gain
    first = jnp.mean(grad_unit, -1, keepdims=True)
    second = jnp.mean(grad_unit * unit, -1, keepdims=True)
    return scale * (grad_unit - first - unit * second)


def far(shape, dtype):
    return pltpu.HBM(shape, dtype)


def held(array):
    return pltpu.with_memory_space_constraint(array, pltpu.HBM)


def column_sum(values):
    return jnp.sum(values, 0, keepdims=True)


def add_first(step, ref, value):
    @pl.when(step == 0)
    def _():
        ref[...] = value

    @pl.when(step > 0)
    def _():
        ref[...] += value


def collect(ring, pos, pieces, whole, sems):
    copies = []

    def put(source, target):
        copy = pltpu.make_async_copy(source, target, sems.at[len(copies)])
        copy.start()
        copies.append(copy)

    if not ring:
        put(pieces[0], whole)
    else:
        g, z, c = pos[0], pos[1], pos[2]
        for at in range(2):
            core = c if at == 0 else 1 - c
            own, near, far = pieces[3 * at : 3 * at + 3]
            put(own, whole.at[z, core])
            for k in range(1, Z):
                row = lax.rem(z + Z - k, Z)
                for over in range(3):
                    put(near.at[over, :, k - 1], whole.at[row, core, g ^ over])
                for part in range(2):
                    put(far.at[part, k - 1], whole.at[row, core, g ^ 3, part])
    for copy in copies:
        copy.wait()


def whole_shape(ring, pieces):
    if ring:
        return (Z, 2) + pieces[0].shape
    return pieces[0].shape


def collect_scratch(ring, pieces):
    return [
        pltpu.VMEM(whole_shape(ring, pieces), BF16),
        pltpu.SemaphoreType.DMA((32,)),
        pltpu.SemaphoreType.DMA,
    ]


def fill(ring, step, steps, pos, pieces, kept, whole, sems, sem):
    @pl.when(step == 0)
    def _():
        collect(ring, pos, pieces, whole, sems)
        pltpu.make_async_copy(whole, kept, sem).start()


def keep(step, steps, kept, whole, sem):
    @pl.when(step == steps - 1)
    def _():
        pltpu.make_async_copy(whole, kept, sem).wait()


def flat_rows(whole):
    value = whole[...]
    return value.reshape(-1, value.shape[-1])


def project_kernel(ring, count, rows_each, lengths, pos, x, cot, *refs):
    normed, packed, up, up_sum, kept, table, whole, sems, sem, weight_bias = refs[-10:]
    pieces = refs[:-10] if ring else refs[:-12]
    step = pl.program_id(0)
    fill(ring, step, count, pos, pieces, kept, whole, sems, sem)
    rows, width = x.shape[1:]

    @pl.when(step == 0)
    def _():
        if ring:
            columns = whole[..., 3 * width :].reshape(width, LANES).astype(F32)
            table[...] = columns.T[: table.shape[0], :]
            weight_bias[...] = jnp.zeros(weight_bias.shape, F32)
            for shard in range(width // rows_each):
                for part in range(2):
                    at = (2 * shard + part) * rows_each
                    at += width if at >= width else 0
                    source = table[2 + part : 3 + part, shard * rows_each : (shard + 1) * rows_each]
                    weight_bias[:, at : at + rows_each] = source
        else:
            table[...] = refs[-12][...]
            weight_bias[...] = refs[-11][...]

    valid = valid_rows(lengths[step], rows)
    unit, _ = norm_parts(x[0].astype(F32) * valid)
    low = (unit * table[0:1, :] + table[1:2, :]).astype(BF16)
    normed[0] = low
    weight = whole[..., : 3 * width].reshape(width, 3 * width)
    packed[0] = (mm(low, weight) + weight_bias[...]).astype(BF16)
    upstream = cot[0].astype(F32) * valid
    up[0] = upstream.astype(BF16)
    add_first(step, up_sum, column_sum(upstream))
    keep(step, count, kept, whole, sem)


def project(ring, rows_each, lengths, pos, x, cot, pieces, vectors=()):
    seqs, rows, width = x.shape
    wide = 3 * width
    row_block = pl.BlockSpec((1, rows, width), lambda s, *_: (s, 0, 0))
    anywhere = pl.BlockSpec(memory_space=pl.ANY)
    normed, packed, up, up_sum, kept, table = pl.pallas_call(
        functools.partial(project_kernel, ring, seqs, rows_each),
        grid_spec=pltpu.PrefetchScalarGridSpec(
            num_scalar_prefetch=2,
            grid=(seqs,),
            in_specs=[row_block, row_block]
            + [anywhere] * len(pieces)
            + [once(v.shape) for v in vectors],
            out_specs=[
                row_block,
                pl.BlockSpec((1, rows, wide), lambda s, *_: (s, 0, 0)),
                row_block,
                pl.BlockSpec((1, width), lambda s, *_: (0, 0)),
                anywhere,
                pl.BlockSpec((16, width), lambda s, *_: (0, 0)),
            ],
            scratch_shapes=collect_scratch(ring, pieces) + [pltpu.VMEM((1, wide), F32)],
        ),
        out_shape=[
            jax.ShapeDtypeStruct(x.shape, BF16),
            far((seqs, rows, wide), BF16),
            jax.ShapeDtypeStruct(x.shape, BF16),
            jax.ShapeDtypeStruct((1, width), F32),
            far(whole_shape(ring, pieces), BF16),
            jax.ShapeDtypeStruct((16, width), F32),
        ],
        compiler_params=params(30),
        cost_estimate=cost(2 * seqs * rows * width * wide, seqs * rows * (4 * width + wide) * 2 + 4 * width * wide),
        name="norm_project",
    )(lengths, pos, x, cot, *[held(piece) for piece in pieces], *vectors)
    return normed, packed, up, up_sum, kept.reshape(width, -1), table


LEAST = 256
RATE = E**-0.5 * 1.4426950408889634


def attend_kernel(seq, lengths, q, k, v, *refs):
    mixed, lse = refs[-2:]
    rows = q.shape[1]
    length = lengths[seq]
    key_ok = lax.broadcasted_iota(jnp.int32, (1, rows - LEAST), 1) + LEAST < length
    lane = lax.broadcasted_iota(jnp.int32, (rows, LANES), 1)
    low_lane = lane < E
    logs = jnp.zeros((rows, LANES), F32)
    for pair in range(q.shape[2] // LANES):
        at = slice(pair * LANES, (pair + 1) * LANES)
        qs, ks, vs = q[0, :, at], k[0, :, at], v[0, :, at]
        outs = []
        for head in range(2):
            keep = low_lane if head == 0 else ~low_lane
            scores = mm(jnp.where(keep, qs, jnp.zeros_like(qs)), ks, NT)
            scores = jnp.concatenate(
                [scores[:, :LEAST], jnp.where(key_ok, scores[:, LEAST:], -1e30)], 1
            )
            top = jnp.max(scores, -1, keepdims=True)
            weights = jnp.exp2((scores - top) * RATE)
            total = jnp.sum(weights, -1, keepdims=True)
            outs.append(mm(weights.astype(BF16), vs) * (1.0 / total))
            logs = jnp.where(lane == 2 * pair + head, top * RATE + jnp.log2(total), logs)
        mixed[0, :, at] = jnp.where(low_lane, outs[0], outs[1]).astype(BF16)
    lse[0, 0] = logs.T[: lse.shape[2], :]


def attend(seq, lengths, packed, earlier=()):
    seqs, rows, wide = packed.shape
    width = wide // 3
    wid = 4 * LANES
    steps = width // wid
    block = lambda part: pl.BlockSpec((1, rows, wid), lambda j, *_: (seq, 0, part * steps + j))
    return pl.pallas_call(
        functools.partial(attend_kernel, seq),
        grid_spec=pltpu.PrefetchScalarGridSpec(
            num_scalar_prefetch=1,
            grid=(steps,),
            in_specs=[block(0), block(1), block(2)]
            + [pl.BlockSpec(memory_space=pl.ANY)] * len(earlier),
            out_specs=[
                pl.BlockSpec((1, rows, wid), lambda j, *_: (seq, 0, j)),
                pl.BlockSpec((1, 1, 8, rows), lambda j, *_: (seq, j, 0, 0)),
            ],
        ),
        out_shape=[
            jax.ShapeDtypeStruct((seqs, rows, width), BF16),
            jax.ShapeDtypeStruct((seqs, steps, 8, rows), F32),
        ],
        input_output_aliases={4: 0, 5: 1} if earlier else {},
        compiler_params=params(16),
        cost_estimate=cost(4 * rows * rows * width * 8, rows * wide * 3, H * rows * rows),
        name="attend",
    )(lengths, *[held(packed)] * 3, *earlier)


def attend_back_kernel(seq, lengths, q, k, v, lse, grad, *refs):
    out = refs[-1]
    rows = q.shape[1]
    length = lengths[seq + pl.program_id(0)]
    key_ok = lax.broadcasted_iota(jnp.int32, (rows - LEAST, 1), 0) + LEAST < length
    low_lane = lax.broadcasted_iota(jnp.int32, (rows, LANES), 1) < E
    for pair in range(q.shape[2] // LANES):
        at = slice(pair * LANES, (pair + 1) * LANES)
        qs, ks, vs, gs = q[0, :, at], k[0, :, at], v[0, :, at], grad[0, :, at]
        sums = []
        for head in range(2):
            keep = low_lane if head == 0 else ~low_lane
            scores = mm(jnp.where(keep, ks, jnp.zeros_like(ks)), qs, NT)
            grad_probs = mm(jnp.where(keep, vs, jnp.zeros_like(vs)), gs, NT)
            row = 2 * pair + head
            probs = jnp.exp2(scores * RATE - lse[0, 0, row : row + 1, :])
            probs = jnp.concatenate(
                [probs[:LEAST], jnp.where(key_ok, probs[LEAST:], 0.0)], 0
            )
            inner = jnp.sum(grad_probs * probs, 0, keepdims=True)
            grad_scores = (probs * (grad_probs - inner)).astype(BF16)
            sums.append(
                (
                    mm(grad_scores, ks, TN) * E**-0.5,
                    mm(grad_scores, qs) * E**-0.5,
                    mm(probs.astype(BF16), gs),
                )
            )
        for part, first, second in zip(range(3), sums[0], sums[1]):
            out[0, part, :, at] = jnp.where(low_lane, first, second).astype(BF16)


def attend_back(seq, here, lengths, packed, lse, grad, earlier=()):
    seqs, rows, wide = packed.shape
    width = wide // 3
    wid = 4 * LANES
    steps = width // wid
    block = lambda part: pl.BlockSpec(
        (1, rows, wid), lambda s, j, *_: (seq + s, 0, part * steps + j)
    )
    return pl.pallas_call(
        functools.partial(attend_back_kernel, seq),
        grid_spec=pltpu.PrefetchScalarGridSpec(
            num_scalar_prefetch=1,
            grid=(here, steps),
            in_specs=[
                block(0),
                block(1),
                block(2),
                pl.BlockSpec((1, 1, 8, rows), lambda s, j, *_: (seq + s, j, 0, 0)),
                pl.BlockSpec((1, rows, wid), lambda s, j, *_: (seq + s, 0, j)),
            ]
            + [pl.BlockSpec(memory_space=pl.ANY)] * len(earlier),
            out_specs=pl.BlockSpec((1, 3, rows, wid), lambda s, j, *_: (seq + s, 0, 0, j)),
        ),
        out_shape=far((seqs, 3, rows, width), BF16),
        input_output_aliases={6: 0} if earlier else {},
        compiler_params=pltpu.CompilerParams(
            vmem_limit_bytes=18 << 20, dimension_semantics=("arbitrary",) * 2
        ),
        cost_estimate=cost(10 * here * rows * rows * width * 8, here * rows * wide * 5, here * H * rows * rows),
        name="attend_back",
    )(lengths, *[held(packed)] * 3, lse, grad, *[held(a) for a in earlier])


def branch_kernel(ring, count, lengths, pos, x, mixed, table, *refs):
    pieces, (resid, normed, kept, whole, sems, sem) = refs[:-6], refs[-6:]
    step = pl.program_id(0)
    fill(ring, step, count, pos, pieces, kept, whole, sems, sem)
    rows, width = x.shape[1:]
    valid = valid_rows(lengths[step], rows)
    weight = whole[..., :width].reshape(-1, width)
    total = x[0].astype(F32) * valid + mm(mixed[0], weight) + table[4:5, :]
    resid[0] = total
    unit, _ = norm_parts(total)
    normed[0] = (unit * table[5:6, :] + table[6:7, :]).astype(BF16)
    keep(step, count, kept, whole, sem)


def branch(ring, lengths, pos, x, mixed, table, pieces):
    seqs, rows, width = x.shape
    wide = pieces[0].shape[-1]
    row_block = pl.BlockSpec((1, rows, width), lambda s, *_: (s, 0, 0))
    anywhere = pl.BlockSpec(memory_space=pl.ANY)
    resid, normed, kept = pl.pallas_call(
        functools.partial(branch_kernel, ring, seqs),
        grid_spec=pltpu.PrefetchScalarGridSpec(
            num_scalar_prefetch=2,
            grid=(seqs,),
            in_specs=[row_block, row_block, once(table.shape)] + [anywhere] * len(pieces),
            out_specs=[row_block, row_block, anywhere],
            scratch_shapes=collect_scratch(ring, pieces),
        ),
        out_shape=[
            far(x.shape, F32),
            jax.ShapeDtypeStruct(x.shape, BF16),
            far(whole_shape(ring, pieces), BF16),
        ],
        compiler_params=params(26),
        cost_estimate=cost(2 * seqs * rows * width * width, seqs * rows * width * 10 + 4 * width * wide),
        name="branch",
    )(lengths, pos, x, mixed, table, *[held(piece) for piece in pieces])
    return resid, normed, kept.reshape(-1, wide)


def store_halves(ref, value):
    _, shards, quarters, rows, _ = ref.shape
    for shard in range(shards):
        for quarter in range(quarters):
            for half in range(2):
                at = ((shard * quarters + quarter) * 2 + half) * rows
                ref[half, shard, quarter] = value[at : at + rows]


def expand_kernel(seqs, normed, up, weight, bias, act, slope, grad):
    rows = normed.shape[0] // seqs
    for s in range(seqs):
        at = slice(s * rows, (s + 1) * rows)
        hidden = mm(normed[at, :], weight[...]) + bias[...]
        phi = 0.5 + 0.5 * lax.erf(hidden * HALF_ROOT)
        act[at, :] = (hidden * phi).astype(BF16)
        slope[at, :] = (phi + hidden * (INV_ROOT_TAU * jnp.exp(-0.5 * hidden * hidden))).astype(BF16)
    grad[...] = mm(act[...], up[...], TN).astype(BF16)


def expand(seqs, normed, up, weight, bias):
    count, width = normed.shape
    hidden = bias.shape[1]
    size = hidden // 4
    skip = (weight.shape[1] - hidden) // size
    wide = pl.BlockSpec((count, size), lambda i: (0, i))
    shape = far((count, hidden), BF16)
    return pl.pallas_call(
        functools.partial(expand_kernel, seqs),
        grid=(4,),
        in_specs=[
            once((count, width)),
            once((count, width)),
            pl.BlockSpec((width, size), lambda i: (0, skip + i)),
            pl.BlockSpec((1, size), lambda i: (0, i)),
        ],
        out_specs=[wide, wide, pl.BlockSpec((size, width), lambda i: (i, 0))],
        out_shape=[shape, shape, far((hidden, width), BF16)],
        compiler_params=params(36),
        cost_estimate=cost(4 * count * width * hidden, count * hidden * 4 + width * hidden * 4, count * hidden),
        name="expand",
    )(normed, up, held(weight), bias)


def reduce_kernel(lengths, resid, act, weight, table, out):
    rows = resid.shape[1]
    valid = valid_rows(lengths[pl.program_id(0)], rows)
    out[0] = (resid[0] + mm(act[0], weight[...]) + table[11:12, :]) * valid


def reduce_out(lengths, resid, act, weight, table):
    seqs, rows, width = resid.shape
    hidden = weight.shape[0]
    row_block = pl.BlockSpec((1, rows, width), lambda s, *_: (s, 0, 0))
    return pl.pallas_call(
        reduce_kernel,
        grid_spec=pltpu.PrefetchScalarGridSpec(
            num_scalar_prefetch=1,
            grid=(seqs,),
            in_specs=[
                row_block,
                pl.BlockSpec((1, rows, hidden), lambda s, *_: (s, 0, 0)),
                once((hidden, width)),
                once(table.shape),
            ],
            out_specs=row_block,
        ),
        out_shape=far(resid.shape, F32),
        compiler_params=params(26),
        cost_estimate=cost(2 * seqs * rows * width * hidden, seqs * rows * (8 * width + 2 * hidden) + 2 * width * hidden),
        name="reduce_out",
    )(lengths, held(resid), held(act.reshape(seqs, rows, hidden)), weight, table)


def hidden_back_kernel(seqs, up, weight, slope, grad, grad_sum):
    rows = up.shape[0] // seqs
    total = None
    for s in range(seqs):
        at = slice(s * rows, (s + 1) * rows)
        low = (mm(up[at, :], weight[...], NT) * slope[at, :].astype(F32)).astype(BF16)
        grad[at, :] = low
        part = column_sum(low.astype(F32))
        total = part if s == 0 else total + part
    grad_sum[...] = total


def hidden_back(seqs, up, weight, slope):
    count, width = up.shape
    hidden = slope.shape[1]
    size = hidden // 4
    wide = pl.BlockSpec((count, size), lambda i: (0, i))
    return pl.pallas_call(
        functools.partial(hidden_back_kernel, seqs),
        grid=(4,),
        in_specs=[once((count, width)), pl.BlockSpec((size, width), lambda i: (i, 0)), wide],
        out_specs=[wide, pl.BlockSpec((1, size), lambda i: (0, i))],
        out_shape=[far((count, hidden), BF16), jax.ShapeDtypeStruct((1, hidden), F32)],
        compiler_params=params(28),
        cost_estimate=cost(2 * count * width * hidden, count * hidden * 4 + 2 * width * hidden),
        name="hidden_back",
    )(up, held(weight), held(slope))


def whole_grad_kernel(inputs, grads, out):
    out[...] = mm(inputs[...], grads[...], TN).astype(BF16)


def whole_grad(inputs, grads, first):
    count, width = inputs.shape
    here = grads.shape[1] - first
    size = 1024
    return pl.pallas_call(
        whole_grad_kernel,
        grid=(here // size,),
        in_specs=[
            once((count, width)),
            pl.BlockSpec((count, size), lambda j: (0, first // size + j)),
        ],
        out_specs=pl.BlockSpec((width, size), lambda j: (0, j)),
        out_shape=far((width, here), BF16),
        compiler_params=params(28),
        cost_estimate=cost(2 * count * width * here, count * (width + here) * 2 + 2 * width * here),
        name="whole_grad",
    )(inputs, held(grads))


def pick_columns(half, order, inputs, picked):
    @pl.when(pl.program_id(0) == 0)
    def _():
        for i in range(4):
            size = picked.shape[1] // 4
            at = pl.multiple_of((order[0] * i + order[1 + half]) * size, size)
            picked[:, i * size : (i + 1) * size] = inputs[:, pl.ds(at, size)]


def weight_grad_kernel(half, order, inputs, grads, *refs):
    out, picked = refs[-2:]
    pick_columns(half, order, inputs, picked)
    block = grads[...].reshape(inputs.shape[0], grads.shape[-1])
    value = mm(picked[...], block, TN).astype(BF16)
    _, shards, _, rows, _ = out.shape
    for shard in range(shards):
        for quarter in range(4):
            for part in range(2):
                at = ((shard * 4 + quarter) * 2 + part) * rows
                out[part, shard, quarter ^ order[3]] = value[at : at + rows]


def grad_spec(grads):
    if len(grads.shape) == 2:
        return pl.BlockSpec((grads.shape[0], 1024), lambda j, *_: (0, j)), 1
    seqs, parts, each, size = grads.shape
    return pl.BlockSpec((seqs, 1, each, size), lambda j, *_: (0, j, 0, 0)), parts


def weight_grad(half, order, inputs, grads, wide, first=0, earlier=()):
    count, width = inputs.shape
    size = 1024
    spec, parts = grad_spec(grads)
    rows = width // 64
    return pl.pallas_call(
        functools.partial(weight_grad_kernel, half),
        grid_spec=pltpu.PrefetchScalarGridSpec(
            num_scalar_prefetch=1,
            grid=(parts,),
            in_specs=[once((count, width)), spec]
            + [pl.BlockSpec(memory_space=pl.ANY)] * len(earlier),
            out_specs=pl.BlockSpec(
                (2, 4, 4, rows, size), lambda j, *_: (0, 0, 0, 0, first // size + j)
            ),
            scratch_shapes=[pltpu.VMEM((count, width // 2), BF16)],
        ),
        out_shape=jax.ShapeDtypeStruct((2, 4, 4, rows, wide), BF16),
        input_output_aliases={3: 0} if earlier else {},
        compiler_params=params(20),
        cost_estimate=cost(count * width * parts * size, count * (width + parts * size) * 2 + width * parts * size),
        name="weight_grad",
    )(order, inputs, held(grads), *earlier)


def norm_two_kernel(lengths, hidden_grad, weight, resid, cot, table, *outs):
    grad_resid, low_ref, mixed_grad, gain_grad, bias_grad, out_bias_grad = outs
    step = pl.program_id(0)
    rows, width = resid.shape[1:]
    valid = valid_rows(lengths[step], rows)
    grad = mm(hidden_grad[0], weight[:, width:], NT)
    unit, scale = norm_parts(resid[0])
    total = cot[0].astype(F32) * valid + norm_back(unit, scale, grad, table[5:6, :])
    grad_resid[0] = total
    low = total.astype(BF16)
    low_ref[0] = low
    mixed_grad[0] = mm(low, weight[:, :width], NT).astype(BF16)
    add_first(step, gain_grad, column_sum(grad * unit))
    add_first(step, bias_grad, column_sum(grad))
    add_first(step, out_bias_grad, column_sum(low.astype(F32)))


def norm_two_back(lengths, hidden_grad, weight, resid, cot, table):
    seqs, rows, width = resid.shape
    hidden = hidden_grad.shape[1]
    row_block = pl.BlockSpec((1, rows, width), lambda s, *_: (s, 0, 0))
    vec = pl.BlockSpec((1, width), lambda s, *_: (0, 0))
    return pl.pallas_call(
        norm_two_kernel,
        grid_spec=pltpu.PrefetchScalarGridSpec(
            num_scalar_prefetch=1,
            grid=(seqs,),
            in_specs=[
                pl.BlockSpec((1, rows, hidden), lambda s, *_: (s, 0, 0)),
                once((width, width + hidden)),
                row_block,
                row_block,
                once(table.shape),
            ],
            out_specs=[row_block] * 3 + [vec] * 3,
        ),
        out_shape=[
            far(resid.shape, F32),
            jax.ShapeDtypeStruct(resid.shape, BF16),
            jax.ShapeDtypeStruct(resid.shape, BF16),
        ]
        + [jax.ShapeDtypeStruct((1, width), F32)] * 3,
        compiler_params=params(40),
        cost_estimate=cost(2 * seqs * rows * width * (hidden + width), seqs * rows * (2 * hidden + 14 * width)),
        name="norm_two_back",
    )(lengths, held(hidden_grad.reshape(seqs, rows, hidden)), weight, held(resid), cot, table)


def norm_one_kernel(lengths, thirds, weight, x, grad_resid, table, *outs):
    input_grad, gain_grad, bias_grad, q_sum, v_sum = outs
    step = pl.program_id(0)
    rows, width = x.shape[1:]
    valid = valid_rows(lengths[step], rows)
    grad = mm(thirds[0, 0], weight[:, :width], NT)
    grad += mm(thirds[0, 1], weight[:, width : 2 * width], NT)
    grad += mm(thirds[0, 2], weight[:, 2 * width : 3 * width], NT)
    unit, scale = norm_parts(x[0].astype(F32) * valid)
    input_grad[0] = (grad_resid[0] + norm_back(unit, scale, grad, table[0:1, :])) * valid
    add_first(step, gain_grad, column_sum(grad * unit))
    add_first(step, bias_grad, column_sum(grad))
    add_first(step, q_sum, column_sum(thirds[0, 0].astype(F32)))
    add_first(step, v_sum, column_sum(thirds[0, 2].astype(F32)))


def norm_one_back(lengths, thirds, weight, x, grad_resid, table):
    seqs, rows, width = x.shape
    row_block = pl.BlockSpec((1, rows, width), lambda s, *_: (s, 0, 0))
    vec = pl.BlockSpec((1, width), lambda s, *_: (0, 0))
    return pl.pallas_call(
        norm_one_kernel,
        grid_spec=pltpu.PrefetchScalarGridSpec(
            num_scalar_prefetch=1,
            grid=(seqs,),
            in_specs=[
                pl.BlockSpec((1, 3, rows, width), lambda s, *_: (s, 0, 0, 0)),
            ]
            + [once(weight.shape), row_block, row_block, once(table.shape)],
            out_specs=[row_block] + [vec] * 4,
        ),
        out_shape=[far(x.shape, F32)] + [jax.ShapeDtypeStruct((1, width), F32)] * 4,
        compiler_params=params(32),
        cost_estimate=cost(6 * seqs * rows * width * width, seqs * rows * width * 16 + 6 * width * width),
        name="norm_one_back",
    )(lengths, held(thirds), weight, x, held(grad_resid), table)

def near_kernel(*refs):
    for at in range(4):
        mine, other, out = refs[at], refs[4 + at], refs[8 + at]
        total = mine[...].astype(F32) + other[...].astype(F32)
        out[...] = total.astype(BF16).reshape(out.shape)


def near_sum(own, arrived):
    _, shards, _, rows, wide = own.shape
    over_x = (1, 1, 2, 1, rows, wide)
    over_y = (1, 1, 1, 2, rows, wide)
    specs = [
        pl.BlockSpec(over_x, lambda s: (0, s, 0, 0, 0, 0)),
        pl.BlockSpec(over_y, lambda s: (1, s, 0, 0, 0, 0)),
        pl.BlockSpec(over_x, lambda s: (0, s, 0, 1, 0, 0)),
        pl.BlockSpec(over_y, lambda s: (1, s, 1, 0, 0, 0)),
    ]
    shape = (2, shards, 2, 2, rows, wide)
    return pl.pallas_call(
        near_kernel,
        grid=(shards,),
        in_specs=specs * 2,
        out_specs=[pl.BlockSpec((1, 2, rows, wide), lambda s: (s, 0, 0, 0))] * 4,
        out_shape=[jax.ShapeDtypeStruct((shards, 2, rows, wide), BF16)] * 4,
        compiler_params=params(14),
        cost_estimate=cost(own.size, own.size * 6),
        name="near_sum",
    )(*[own.reshape(shape)] * 4, *[arrived.reshape(shape)] * 4)


AXES = ("group", "dp")
Z = 4


def permutation(move):
    pairs = []
    for g in range(4):
        for d in range(2 * Z):
            to_g, to_z, to_c = move(g, d // 2, d % 2)
            pairs.append((g * 2 * Z + d, (to_g * Z + to_z) * 2 + to_c))
    return pairs


CORE = permutation(lambda g, z, c: (g, z, 1 - c))
OVER_X = permutation(lambda g, z, c: (g ^ 1, z, c))
OVER_Y = permutation(lambda g, z, c: (g ^ 2, z, c))
OVER_XY = permutation(lambda g, z, c: (g ^ 3, z, c))
OVER_Z = [permutation(lambda g, z, c, k=k: (g, (z + k) % Z, c)) for k in range(Z)]
NEAR_Z = permutation(lambda g, z, c: (g, z ^ 1, c))
FAR_Z = permutation(lambda g, z, c: (g, z ^ 2, c))


def send(array, pairs):
    return lax.ppermute(array, AXES, pairs)


def tie(value, *others):
    return lax.optimization_barrier((value,) + others)[0]


def pick(array, index, axis):
    return lax.dynamic_index_in_dim(array, index, axis, keepdims=False)


def plus(former, latter):
    return (former.astype(F32) + latter.astype(F32)).astype(BF16)


def quarters(shard, g):
    rows, wide = shard.shape
    parts = shard.reshape(4, 2, rows // 8, wide)
    return parts, pick(parts, g, 0)


def send_quarter(mine):
    return [send(mine, OVER_Z[k]) for k in range(1, Z)]


def send_xy(first, second):
    return send(first, OVER_X), send(second, OVER_Y)


def scatter_core(other):
    return send(other, CORE)


def scatter_far(first, second, from_x, from_y):
    first = plus(first, from_x)
    second = plus(second, from_y)
    return first[:, 0], second[:, 0], first[:, 1], second[:, 1]


def scatter_z(first, second, from_y, from_x, z):
    quarter = jnp.stack([plus(first, from_y), plus(second, from_x)], 1)
    return pick(quarter, z, 0), [pick(quarter, (z + k) % Z, 0) for k in range(1, Z)]


def send_z(parts):
    return [send(part, OVER_Z[k]) for k, part in enumerate(parts, 1)]


def spread(mine, arrived):
    total = mine.astype(F32)
    for part in arrived:
        total = total + part.astype(F32)
    return total.astype(BF16)


def send_near(mine):
    return [send(mine, OVER_X), send(mine, OVER_Y), send(mine, OVER_XY)]


def placed(mine, others, g):
    grid = jnp.stack([mine, *others]).reshape(2, 2, *mine.shape)
    grid = jnp.where(g % 2 == 1, grid[:, ::-1], grid)
    grid = jnp.where(g // 2 == 1, grid[::-1], grid)
    return grid.astype(F32).reshape(-1, mine.shape[-1])


def trade(shard, g):
    rows, wide = shard.shape
    parts = shard.reshape(4, rows // 4, wide)
    return pick(parts, g, 0), [pick(parts, g ^ over, 0) for over in (1, 2, 3)]


def send_trade(parts):
    return [send(part, pairs) for part, pairs in zip(parts, (OVER_X, OVER_Y, OVER_XY))]


def spread_xy(mine):
    half = mine.shape[0] // 2
    over_x, over_y = send_xy(mine, mine)
    second, first = send_xy(over_y[half:], over_x[:half])
    return [over_x, over_y, jnp.concatenate([first, second])]


VEC = (0, 1, 3, 5, 6, 7, 9, 11)


def joined(vectors):
    total = sum(v.shape[0] for v in vectors)
    at = 0
    out = None
    for v in vectors:
        wide = lax.pad(v, jnp.zeros((), v.dtype), [(at, total - at - v.shape[0], 0)])
        out = wide if out is None else out + wide
        at += v.shape[0]
    return out


def widened(weight, vectors):
    rows = weight.shape[0]
    columns = joined(vectors).reshape(-1, rows).T
    columns = jnp.pad(columns, ((0, 0), (0, LANES - columns.shape[1])))
    return jnp.concatenate([weight, columns], 1)


def spaced(table, first, last, rows):
    part = table[first:last].reshape(last - first, -1, rows)
    return part.transpose(1, 0, 2).reshape(1, -1)


def packed_vectors(grads):
    return joined([grads[i].reshape(-1) for i in VEC])


def own_vectors(total, grads, shards):
    d = lax.axis_index("dp")
    at = 0
    summed = {}
    for i in VEC:
        size = shards[i].shape[0]
        summed[i] = lax.dynamic_slice(total, (at + d * size,), (size,))
        at += grads[i].size
    return summed


def over_dp(array):
    return lax.psum_scatter(array, "dp", scatter_dimension=0, tiled=True)


def local(ring, layer_input, lengths, *rest):
    shards, cot = rest[:12], rest[12]
    micro, seqs, rows, width = layer_input.shape
    count = micro * seqs
    g = lax.axis_index("group")
    d = lax.axis_index("dp")
    z, c = d // 2, d % 2
    pos = jnp.stack([g, z, c]).astype(jnp.int32)
    order = [2, 1 - c, c, g] if ring else [1, 0, 4, 0]
    order = jnp.stack([jnp.asarray(v, jnp.int32) for v in order])
    lens = lengths.reshape(-1)
    x = layer_input.reshape(count, rows, width)
    cot = cot.reshape(count, rows, width)
    flat = lambda a: a.reshape(count * rows, a.shape[-1])
    rows_each = shards[2].shape[0]
    wanted = (widened(shards[2], [shards[i] for i in VEC]), jnp.concatenate([shards[4], shards[8]], 1), shards[10])

    if ring:
        parts_p, mine_p = quarters(wanted[0], g)
        parts_e, mine_e = quarters(wanted[1], g)
        ring_p = send_quarter(mine_p)
        core_p, core_e = send(parts_p, CORE), send(parts_e, CORE)
        stack_p = jnp.stack(tie(ring_p, core_p, core_e), 1)
        x_p, y_p = send_xy(stack_p, stack_p)
        mine_e = tie(mine_e, stack_p)
        e_one, e_two = send(mine_e, OVER_Z[1]), send(mine_e, OVER_Z[2])
        x_p, y_p, e_one, e_two, mine_e = tie((x_p, y_p, e_one, e_two, mine_e))
        b_p, a_p = send_xy(y_p[1], x_p[0])
        e_three = send(mine_e, OVER_Z[3])
        near_p = jnp.stack([stack_p, x_p, y_p])
        near_core_p = send(near_p, CORE)
        a_p, b_p, e_three, near_core_p = tie((a_p, b_p, e_three, near_core_p))
        far_p = jnp.stack([a_p, b_p])
        pieces_p = [parts_p, near_p, far_p, core_p, near_core_p, send(far_p, CORE)]
        stack_e = jnp.stack(tie((e_one, e_two, e_three), pieces_p), 1)
        lens_project, shard_r = tie((lens, wanted[2]), stack_e)
        x_e, y_e = send_xy(stack_e, stack_e)
        reduce_w = lax.all_gather(shard_r, "dp", axis=0, tiled=True)
        vectors = ()
    else:
        pieces = [lax.all_gather(w, "dp", axis=0, tiled=True) for w in wanted]
        pieces_p, pieces_e, reduce_w = [pieces[0]], [pieces[1]], pieces[2]
        lens_project = lens
        table = pieces[0][:, 3 * width : 3 * width + 16].T.astype(F32)
        pair = spaced(table, 2, 4, rows_each)
        middle = jnp.zeros((1, width), F32)
        vectors = (table, jnp.concatenate([pair[:, :width], middle, pair[:, width:]], -1))
    normed, packed, up, up_sum, project_w, table = project(
        ring, rows_each, lens_project, pos, x, cot, pieces_p, vectors
    )
    expand_b = spaced(table, 7, 11, rows_each)
    mixed, lse = attend(0, lens, packed)
    lens_attend = lens
    if ring:
        x_e, y_e = tie((x_e, y_e), mixed)
        near_e = jnp.stack([stack_e, x_e, y_e])
        lens_attend = tie(lens, near_e)
        b_e, a_e = send_xy(y_e[1], x_e[0])
        near_core_e = send(near_e, CORE)
    for seq in range(1, count):
        mixed, lse = attend(seq, lens_attend, packed, (mixed, lse))
    if ring:
        a_e, b_e = tie((a_e, b_e), mixed)
        far_e = jnp.stack([a_e, b_e])
        pieces_e = [parts_e, near_e, far_e, core_e, near_core_e, send(far_e, CORE)]
    resid, normed_two, joint_w = branch(ring, lens, pos, x, mixed, table, pieces_e)
    act, slope, reduce_grad = expand(count, flat(normed_two), flat(up), joint_w, expand_b)
    shard_r = over_dp(reduce_grad)
    hidden_grad, hidden_sum = hidden_back(count, flat(up), reduce_w, slope)
    grad_resid, branch_low, mixed_grad, gain_two_grad, bias_two_grad, output_b_grad = norm_two_back(
        lens, hidden_grad, joint_w, resid, cot, table
    )
    thirds = attend_back(0, count, lens, packed, lse, mixed_grad)
    expand_grad = whole_grad(flat(normed_two), tie(hidden_grad, thirds), 0)
    shard_e = over_dp(expand_grad)
    branch_part = flat(branch_low)
    project_far = weight_grad(0, order, flat(mixed), branch_part, 4 * width)
    project_near = weight_grad(1, order, flat(mixed), branch_part, 4 * width)
    order_far = order
    if ring:
        mine_r, parts_r = trade(tie(shard_r, (project_far, project_near)), g)
        order_far = tie(order, parts_r)
        arrived_r = send_trade(parts_r)
    project_far = weight_grad(
        0, order_far, flat(normed), thirds, 4 * width, width, (project_far,)
    )
    order_near = order
    if ring:
        order_near = tie(order, project_far)
        arrived = send(project_far, CORE)
    project_near = weight_grad(
        1, order_near, flat(normed), thirds, 4 * width, width, (project_near,)
    )
    lens_one = lens
    if ring:
        spread_r = spread(mine_r, tie(arrived_r, project_near))
        ps = near_sum(project_near, arrived)
        lens_one = tie(lens, ps, spread_r)
        from_x, from_y = send_xy(ps[2], ps[3])
    input_grad, gain_one_grad, bias_one_grad, query_sum, value_sum = norm_one_back(
        lens_one, thirds, project_w, x, grad_resid, table
    )
    vectors = {
        0: gain_one_grad,
        1: bias_one_grad,
        3: jnp.concatenate([query_sum, value_sum], -1),
        5: output_b_grad,
        6: gain_two_grad,
        7: bias_two_grad,
        9: hidden_sum,
        11: up_sum,
    }
    total = packed_vectors(vectors)
    lens_out = lens
    if ring:
        total = total.reshape(-1, LANES)
        total = total + send(total, CORE)
        total = (total + send(total, OVER_XY)) + (send(total, OVER_X) + send(total, OVER_Y))
        total, from_x, from_y = tie((total, from_x, from_y))
        ps = scatter_far(ps[0], ps[1], from_x, from_y)
        lens_out = tie(lens, ps)
        from_x, from_y = send_xy(ps[3], ps[2])
        column = [send(total, OVER_Z[k]) for k in range(1, Z)]
    layer_output = reduce_out(lens_out, resid, act, reduce_w, table)
    sums = {}
    if ring:
        (from_x, from_y, column), layer_output = lax.optimization_barrier(
            ((from_x, from_y, column), layer_output)
        )
        mine_z, parts_z = scatter_z(ps[0], ps[1], from_y, from_x, z)
        arrived_p = send_z(parts_z)
        spread_r = tie(spread_r, parts_z)
        x_r, y_r = send_xy(spread_r, spread_r)
        half = spread_r.shape[0] // 2
        b_r, a_r = send_xy(y_r[half:], x_r[:half])
        sums[10] = placed(spread_r, [x_r, y_r, jnp.concatenate([a_r, b_r])], g)
        total = (total + column[1]) + (column[0] + column[2])
        mine_e, parts_e = trade(tie(shard_e, (x_r, y_r)), g)
        arrived_e = send_trade(parts_e)
        spread_p = spread(mine_z, tie(arrived_p, parts_e))
        near_p = send_near(spread_p)
        spread_e = spread(mine_e, tie(arrived_e, spread_p))
        near_e = send_near(spread_e)
        joint_sum = placed(spread_p, near_p, g)
        sums[8] = placed(spread_e, near_e, g)
    else:
        total = lax.psum(total, ("group", "dp"))
        sums[10] = lax.psum(shard_r, "group").astype(F32)
        sums[8] = lax.psum(shard_e, "group").astype(F32)
        parts = [a.transpose(1, 2, 0, 3, 4) for a in (project_far, project_near)]
        parts = over_dp(jnp.concatenate(parts).reshape(width, 4 * width))
        joint_sum = lax.psum(parts, "group").astype(F32)
    sums.update(own_vectors(total.reshape(-1), vectors, shards))
    sums[4] = joint_sum[:, :width]
    sums[2] = joint_sum[:, width:]
    return (
        layer_output.reshape(layer_input.shape),
        input_grad.reshape(layer_input.shape),
        *[sums[i] for i in range(12)],
    )


def solution(mesh):
    ring = mesh.shape["group"] == 4 and mesh.shape["dp"] == 2 * Z
    rows = P(None, ("group", "dp"), None, None)
    vec = P("dp")
    mat = P("dp", None)
    kinds = (vec, vec, mat, vec, mat, vec, vec, vec, mat, vec, mat, vec)
    return jax.shard_map(
        functools.partial(local, ring),
        mesh=mesh,
        in_specs=(rows, P(None, ("group", "dp")), *kinds, rows),
        out_specs=(rows, rows, *kinds),
        check_vma=False,
    )
```

```python
import functools

import jax
import jax.numpy as jnp
from jax import lax
from jax.experimental import pallas as pl
from jax.experimental.pallas import tpu as pltpu
from jax.sharding import PartitionSpec as P

F32 = jnp.float32
BF16 = jnp.bfloat16
EPS = 1e-06
H = 16
E = 64
LANES = 128
HALF_ROOT = 2.0 ** -0.5
INV_ROOT_TAU = 0.3989422804014327
NN = (((1,), (0,)), ((), ()))
NT = (((1,), (1,)), ((), ()))
TN = (((0,), (0,)), ((), ()))


def mm(former, latter, dims=NN):
    return lax.dot_general(former, latter, dims, preferred_element_type=F32)


def params(mib):
    return pltpu.CompilerParams(vmem_limit_bytes=mib << 20, dimension_semantics=("arbitrary",))


def cost(flops, nbytes, other=0):
    return pl.CostEstimate(flops=int(flops), bytes_accessed=int(nbytes), transcendentals=int(other))


def once(shape):
    return pl.BlockSpec(memory_space=pltpu.VMEM)


def valid_rows(length, rows):
    return (lax.broadcasted_iota(jnp.int32, (rows, 1), 0) < length).astype(F32)


def norm_parts(values):
    centred = values - jnp.mean(values, -1, keepdims=True)
    scale = lax.rsqrt(jnp.mean(centred * centred, -1, keepdims=True) + EPS)
    return centred * scale, scale


def norm_back(unit, scale, grad, gain):
    grad_unit = grad * gain
    first = jnp.mean(grad_unit, -1, keepdims=True)
    second = jnp.mean(grad_unit * unit, -1, keepdims=True)
    return scale * (grad_unit - first - unit * second)


def far(shape, dtype):
    return pltpu.HBM(shape, dtype)


def held(array):
    return pltpu.with_memory_space_constraint(array, pltpu.HBM)


def column_sum(values):
    return jnp.sum(values, 0, keepdims=True)


def add_first(step, ref, value):
    @pl.when(step == 0)
    def _():
        ref[...] = value

    @pl.when(step > 0)
    def _():
        ref[...] += value


def collect(ring, pos, pieces, whole, sems):
    copies = []

    def put(source, target):
        copy = pltpu.make_async_copy(source, target, sems.at[len(copies)])
        copy.start()
        copies.append(copy)

    if not ring:
        put(pieces[0], whole)
    else:
        g, z, c = pos[0], pos[1], pos[2]
        for at in range(2):
            core = c if at == 0 else 1 - c
            own, near, far = pieces[3 * at : 3 * at + 3]
            put(own, whole.at[z, core])
            for k in range(1, Z):
                row = lax.rem(z + Z - k, Z)
                for over in range(3):
                    put(near.at[over, :, k - 1], whole.at[row, core, g ^ over])
                for part in range(2):
                    put(far.at[part, k - 1], whole.at[row, core, g ^ 3, part])
    for copy in copies:
        copy.wait()


def whole_shape(ring, pieces):
    if ring:
        return (Z, 2) + pieces[0].shape
    return pieces[0].shape


def collect_scratch(ring, pieces):
    return [
        pltpu.VMEM(whole_shape(ring, pieces), BF16),
        pltpu.SemaphoreType.DMA((32,)),
        pltpu.SemaphoreType.DMA,
    ]


def fill(ring, step, steps, pos, pieces, kept, whole, sems, sem):
    @pl.when(step == 0)
    def _():
        collect(ring, pos, pieces, whole, sems)
        pltpu.make_async_copy(whole, kept, sem).start()


def keep(step, steps, kept, whole, sem):
    @pl.when(step == steps - 1)
    def _():
        pltpu.make_async_copy(whole, kept, sem).wait()


def flat_rows(whole):
    value = whole[...]
    return value.reshape(-1, value.shape[-1])


def project_kernel(ring, count, rows_each, lengths, pos, x, cot, *refs):
    normed, packed, up, up_sum, kept, table, whole, sems, sem, weight_bias = refs[-10:]
    pieces = refs[:-10] if ring else refs[:-12]
    step = pl.program_id(0)
    fill(ring, step, count, pos, pieces, kept, whole, sems, sem)
    rows, width = x.shape[1:]

    @pl.when(step == 0)
    def _():
        if ring:
            columns = whole[..., 3 * width :].reshape(width, LANES).astype(F32)
            table[...] = columns.T[: table.shape[0], :]
            weight_bias[...] = jnp.zeros(weight_bias.shape, F32)
            for shard in range(width // rows_each):
                for part in range(2):
                    at = (2 * shard + part) * rows_each
                    at += width if at >= width else 0
                    source = table[2 + part : 3 + part, shard * rows_each : (shard + 1) * rows_each]
                    weight_bias[:, at : at + rows_each] = source
        else:
            table[...] = refs[-12][...]
            weight_bias[...] = refs[-11][...]

    valid = valid_rows(lengths[step], rows)
    unit, _ = norm_parts(x[0].astype(F32) * valid)
    low = (unit * table[0:1, :] + table[1:2, :]).astype(BF16)
    normed[0] = low
    weight = whole[..., : 3 * width].reshape(width, 3 * width)
    packed[0] = (mm(low, weight) + weight_bias[...]).astype(BF16)
    upstream = cot[0].astype(F32) * valid
    up[0] = upstream.astype(BF16)
    add_first(step, up_sum, column_sum(upstream))
    keep(step, count, kept, whole, sem)


def project(ring, rows_each, lengths, pos, x, cot, pieces, vectors=()):
    seqs, rows, width = x.shape
    wide = 3 * width
    row_block = pl.BlockSpec((1, rows, width), lambda s, *_: (s, 0, 0))
    anywhere = pl.BlockSpec(memory_space=pl.ANY)
    normed, packed, up, up_sum, kept, table = pl.pallas_call(
        functools.partial(project_kernel, ring, seqs, rows_each),
        grid_spec=pltpu.PrefetchScalarGridSpec(
            num_scalar_prefetch=2,
            grid=(seqs,),
            in_specs=[row_block, row_block]
            + [anywhere] * len(pieces)
            + [once(v.shape) for v in vectors],
            out_specs=[
                row_block,
                pl.BlockSpec((1, rows, wide), lambda s, *_: (s, 0, 0)),
                row_block,
                pl.BlockSpec((1, width), lambda s, *_: (0, 0)),
                anywhere,
                pl.BlockSpec((16, width), lambda s, *_: (0, 0)),
            ],
            scratch_shapes=collect_scratch(ring, pieces) + [pltpu.VMEM((1, wide), F32)],
        ),
        out_shape=[
            jax.ShapeDtypeStruct(x.shape, BF16),
            far((seqs, rows, wide), BF16),
            jax.ShapeDtypeStruct(x.shape, BF16),
            jax.ShapeDtypeStruct((1, width), F32),
            far(whole_shape(ring, pieces), BF16),
            jax.ShapeDtypeStruct((16, width), F32),
        ],
        compiler_params=params(30),
        cost_estimate=cost(2 * seqs * rows * width * wide, seqs * rows * (4 * width + wide) * 2 + 4 * width * wide),
        name="norm_project",
    )(lengths, pos, held(x), held(cot), *[held(piece) for piece in pieces], *vectors)
    return normed, packed, up, up_sum, kept.reshape(width, -1), table


LEAST = 256
RATE = E**-0.5 * 1.4426950408889634


def attend_kernel(seq, lengths, q, k, v, *refs):
    mixed, lse = refs[-2:]
    rows = q.shape[1]
    length = lengths[seq + pl.program_id(0)]
    key_ok = lax.broadcasted_iota(jnp.int32, (1, rows - LEAST), 1) + LEAST < length
    lane = lax.broadcasted_iota(jnp.int32, (rows, LANES), 1)
    low_lane = lane < E
    logs = jnp.zeros((rows, LANES), F32)
    for pair in range(q.shape[2] // LANES):
        at = slice(pair * LANES, (pair + 1) * LANES)
        qs, ks, vs = q[0, :, at], k[0, :, at], v[0, :, at]
        outs = []
        for head in range(2):
            keep = low_lane if head == 0 else ~low_lane
            scores = mm(jnp.where(keep, qs, jnp.zeros_like(qs)), ks, NT)
            scores = jnp.concatenate(
                [scores[:, :LEAST], jnp.where(key_ok, scores[:, LEAST:], -1e30)], 1
            )
            top = jnp.max(scores, -1, keepdims=True)
            weights = jnp.exp2((scores - top) * RATE)
            total = jnp.sum(weights, -1, keepdims=True)
            outs.append(mm(weights.astype(BF16), vs) * (1.0 / total))
            logs = jnp.where(lane == 2 * pair + head, top * RATE + jnp.log2(total), logs)
        mixed[0, :, at] = jnp.where(low_lane, outs[0], outs[1]).astype(BF16)
    lse[0, 0] = logs.T[: lse.shape[2], :]


def attend(seq, here, lengths, packed, earlier=()):
    seqs, rows, wide = packed.shape
    width = wide // 3
    wid = 4 * LANES
    steps = width // wid
    block = lambda part: pl.BlockSpec((1, rows, wid), lambda s, j, *_: (seq + s, 0, part * steps + j))
    return pl.pallas_call(
        functools.partial(attend_kernel, seq),
        grid_spec=pltpu.PrefetchScalarGridSpec(
            num_scalar_prefetch=1,
            grid=(here, steps),
            in_specs=[block(0), block(1), block(2)]
            + [pl.BlockSpec(memory_space=pl.ANY)] * len(earlier),
            out_specs=[
                pl.BlockSpec((1, rows, wid), lambda s, j, *_: (seq + s, 0, j)),
                pl.BlockSpec((1, 1, 8, rows), lambda s, j, *_: (seq + s, j, 0, 0)),
            ],
        ),
        out_shape=[
            jax.ShapeDtypeStruct((seqs, rows, width), BF16),
            jax.ShapeDtypeStruct((seqs, steps, 8, rows), F32),
        ],
        input_output_aliases={4: 0, 5: 1} if earlier else {},
        compiler_params=pltpu.CompilerParams(
            vmem_limit_bytes=16 << 20, dimension_semantics=("arbitrary",) * 2
        ),
        cost_estimate=cost(4 * here * rows * rows * width * 8, here * rows * wide * 3, here * H * rows * rows),
        name="attend",
    )(lengths, *[held(packed)] * 3, *earlier)


def attend_back_kernel(seq, lengths, q, k, v, lse, grad, *refs):
    out = refs[-1]
    rows = q.shape[1]
    length = lengths[seq + pl.program_id(0)]
    key_ok = lax.broadcasted_iota(jnp.int32, (rows - LEAST, 1), 0) + LEAST < length
    low_lane = lax.broadcasted_iota(jnp.int32, (rows, LANES), 1) < E
    for pair in range(q.shape[2] // LANES):
        at = slice(pair * LANES, (pair + 1) * LANES)
        qs, ks, vs, gs = q[0, :, at], k[0, :, at], v[0, :, at], grad[0, :, at]
        sums = []
        for head in range(2):
            keep = low_lane if head == 0 else ~low_lane
            scores = mm(jnp.where(keep, ks, jnp.zeros_like(ks)), qs, NT)
            grad_probs = mm(jnp.where(keep, vs, jnp.zeros_like(vs)), gs, NT)
            row = 2 * pair + head
            probs = jnp.exp2(scores * RATE - lse[0, 0, row : row + 1, :])
            probs = jnp.concatenate(
                [probs[:LEAST], jnp.where(key_ok, probs[LEAST:], 0.0)], 0
            )
            inner = jnp.sum(grad_probs * probs, 0, keepdims=True)
            grad_scores = (probs * (grad_probs - inner)).astype(BF16)
            sums.append(
                (
                    mm(grad_scores, ks, TN) * E**-0.5,
                    mm(grad_scores, qs) * E**-0.5,
                    mm(probs.astype(BF16), gs),
                )
            )
        for part, first, second in zip(range(3), sums[0], sums[1]):
            out[0, part, :, at] = jnp.where(low_lane, first, second).astype(BF16)


def attend_back(seq, here, lengths, packed, lse, grad, earlier=()):
    seqs, rows, wide = packed.shape
    width = wide // 3
    wid = 4 * LANES
    steps = width // wid
    block = lambda part: pl.BlockSpec(
        (1, rows, wid), lambda s, j, *_: (seq + s, 0, part * steps + j)
    )
    return pl.pallas_call(
        functools.partial(attend_back_kernel, seq),
        grid_spec=pltpu.PrefetchScalarGridSpec(
            num_scalar_prefetch=1,
            grid=(here, steps),
            in_specs=[
                block(0),
                block(1),
                block(2),
                pl.BlockSpec((1, 1, 8, rows), lambda s, j, *_: (seq + s, j, 0, 0)),
                pl.BlockSpec((1, rows, wid), lambda s, j, *_: (seq + s, 0, j)),
            ]
            + [pl.BlockSpec(memory_space=pl.ANY)] * len(earlier),
            out_specs=pl.BlockSpec((1, 3, rows, wid), lambda s, j, *_: (seq + s, 0, 0, j)),
        ),
        out_shape=far((seqs, 3, rows, width), BF16),
        input_output_aliases={6: 0} if earlier else {},
        compiler_params=pltpu.CompilerParams(
            vmem_limit_bytes=18 << 20, dimension_semantics=("arbitrary",) * 2
        ),
        cost_estimate=cost(10 * here * rows * rows * width * 8, here * rows * wide * 5, here * H * rows * rows),
        name="attend_back",
    )(lengths, *[held(packed)] * 3, lse, grad, *[held(a) for a in earlier])


def branch_kernel(ring, count, lengths, pos, x, mixed, table, *refs):
    pieces, (resid, normed, kept, whole, sems, sem) = refs[:-6], refs[-6:]
    step = pl.program_id(0)
    fill(ring, step, count, pos, pieces, kept, whole, sems, sem)
    rows, width = x.shape[1:]
    valid = valid_rows(lengths[step], rows)
    weight = whole[..., :width].reshape(-1, width)
    total = x[0].astype(F32) * valid + mm(mixed[0], weight) + table[4:5, :]
    resid[0] = total
    unit, _ = norm_parts(total)
    normed[0] = (unit * table[5:6, :] + table[6:7, :]).astype(BF16)
    keep(step, count, kept, whole, sem)


def branch(ring, lengths, pos, x, mixed, table, pieces):
    seqs, rows, width = x.shape
    wide = pieces[0].shape[-1]
    row_block = pl.BlockSpec((1, rows, width), lambda s, *_: (s, 0, 0))
    anywhere = pl.BlockSpec(memory_space=pl.ANY)
    resid, normed, kept = pl.pallas_call(
        functools.partial(branch_kernel, ring, seqs),
        grid_spec=pltpu.PrefetchScalarGridSpec(
            num_scalar_prefetch=2,
            grid=(seqs,),
            in_specs=[row_block, row_block, once(table.shape)] + [anywhere] * len(pieces),
            out_specs=[row_block, row_block, anywhere],
            scratch_shapes=collect_scratch(ring, pieces),
        ),
        out_shape=[
            far(x.shape, F32),
            jax.ShapeDtypeStruct(x.shape, BF16),
            far(whole_shape(ring, pieces), BF16),
        ],
        compiler_params=params(26),
        cost_estimate=cost(2 * seqs * rows * width * width, seqs * rows * width * 10 + 4 * width * wide),
        name="branch",
    )(lengths, pos, held(x), mixed, table, *pieces)
    return resid, normed, kept.reshape(-1, wide)


def store_halves(ref, value):
    _, shards, quarters, rows, _ = ref.shape
    for shard in range(shards):
        for quarter in range(quarters):
            for half in range(2):
                at = ((shard * quarters + quarter) * 2 + half) * rows
                ref[half, shard, quarter] = value[at : at + rows]


def expand_kernel(seqs, normed, up, weight, bias, act, slope, grad):
    rows = normed.shape[0] // seqs
    for s in range(seqs):
        at = slice(s * rows, (s + 1) * rows)
        hidden = mm(normed[at, :], weight[...]) + bias[...]
        phi = 0.5 + 0.5 * lax.erf(hidden * HALF_ROOT)
        act[at, :] = (hidden * phi).astype(BF16)
        slope[at, :] = (phi + hidden * (INV_ROOT_TAU * jnp.exp(-0.5 * hidden * hidden))).astype(BF16)
    grad[...] = mm(act[...], up[...], TN).astype(BF16)


def expand(seqs, normed, up, weight, bias):
    count, width = normed.shape
    hidden = bias.shape[1]
    size = hidden // 4
    skip = (weight.shape[1] - hidden) // size
    wide = pl.BlockSpec((count, size), lambda i: (0, i))
    shape = far((count, hidden), BF16)
    return pl.pallas_call(
        functools.partial(expand_kernel, seqs),
        grid=(4,),
        in_specs=[
            once((count, width)),
            once((count, width)),
            pl.BlockSpec((width, size), lambda i: (0, skip + i)),
            pl.BlockSpec((1, size), lambda i: (0, i)),
        ],
        out_specs=[wide, wide, pl.BlockSpec((size, width), lambda i: (i, 0))],
        out_shape=[shape, shape, far((hidden, width), BF16)],
        compiler_params=params(36),
        cost_estimate=cost(4 * count * width * hidden, count * hidden * 4 + width * hidden * 4, count * hidden),
        name="expand",
    )(normed, up, held(weight), bias)


def reduce_kernel(lengths, resid, act, weight, table, out):
    rows = resid.shape[1]
    valid = valid_rows(lengths[pl.program_id(0)], rows)
    out[0] = (resid[0] + mm(act[0], weight[...]) + table[11:12, :]) * valid


def reduce_out(lengths, resid, act, weight, table):
    seqs, rows, width = resid.shape
    hidden = weight.shape[0]
    row_block = pl.BlockSpec((1, rows, width), lambda s, *_: (s, 0, 0))
    return pl.pallas_call(
        reduce_kernel,
        grid_spec=pltpu.PrefetchScalarGridSpec(
            num_scalar_prefetch=1,
            grid=(seqs,),
            in_specs=[
                row_block,
                pl.BlockSpec((1, rows, hidden), lambda s, *_: (s, 0, 0)),
                once((hidden, width)),
                once(table.shape),
            ],
            out_specs=row_block,
        ),
        out_shape=far(resid.shape, F32),
        compiler_params=params(26),
        cost_estimate=cost(2 * seqs * rows * width * hidden, seqs * rows * (8 * width + 2 * hidden) + 2 * width * hidden),
        name="reduce_out",
    )(lengths, held(resid), held(act.reshape(seqs, rows, hidden)), held(weight), table)


def hidden_back_kernel(seqs, up, weight, slope, grad, grad_sum):
    rows = up.shape[0] // seqs
    total = None
    for s in range(seqs):
        at = slice(s * rows, (s + 1) * rows)
        low = (mm(up[at, :], weight[...], NT) * slope[at, :].astype(F32)).astype(BF16)
        grad[at, :] = low
        part = column_sum(low.astype(F32))
        total = part if s == 0 else total + part
    grad_sum[...] = total


def hidden_back(seqs, up, weight, slope):
    count, width = up.shape
    hidden = slope.shape[1]
    size = hidden // 4
    wide = pl.BlockSpec((count, size), lambda i: (0, i))
    return pl.pallas_call(
        functools.partial(hidden_back_kernel, seqs),
        grid=(4,),
        in_specs=[once((count, width)), pl.BlockSpec((size, width), lambda i: (i, 0)), wide],
        out_specs=[wide, pl.BlockSpec((1, size), lambda i: (0, i))],
        out_shape=[far((count, hidden), BF16), jax.ShapeDtypeStruct((1, hidden), F32)],
        compiler_params=params(28),
        cost_estimate=cost(2 * count * width * hidden, count * hidden * 4 + 2 * width * hidden),
        name="hidden_back",
    )(up, held(weight), held(slope))


def whole_grad_kernel(inputs, grads, out):
    out[...] = mm(inputs[...], grads[...], TN).astype(BF16)


def whole_grad(inputs, grads, first):
    count, width = inputs.shape
    here = grads.shape[1] - first
    size = 1024
    return pl.pallas_call(
        whole_grad_kernel,
        grid=(here // size,),
        in_specs=[
            once((count, width)),
            pl.BlockSpec((count, size), lambda j: (0, first // size + j)),
        ],
        out_specs=pl.BlockSpec((width, size), lambda j: (0, j)),
        out_shape=far((width, here), BF16),
        compiler_params=params(28),
        cost_estimate=cost(2 * count * width * here, count * (width + here) * 2 + 2 * width * here),
        name="whole_grad",
    )(inputs, held(grads))


def pick_columns(half, order, inputs, picked):
    @pl.when(pl.program_id(0) == 0)
    def _():
        for i in range(4):
            size = picked.shape[1] // 4
            at = pl.multiple_of((order[0] * i + order[1 + half]) * size, size)
            picked[:, i * size : (i + 1) * size] = inputs[:, pl.ds(at, size)]


def weight_grad_kernel(half, order, inputs, grads, *refs):
    out, picked = refs[-2:]
    pick_columns(half, order, inputs, picked)
    block = grads[...].reshape(inputs.shape[0], grads.shape[-1])
    value = mm(picked[...], block, TN).astype(BF16)
    _, shards, _, rows, _ = out.shape
    for shard in range(shards):
        for quarter in range(4):
            for part in range(2):
                at = ((shard * 4 + quarter) * 2 + part) * rows
                out[part, shard, quarter ^ order[3]] = value[at : at + rows]


def grad_spec(grads):
    if len(grads.shape) == 2:
        return pl.BlockSpec((grads.shape[0], 1024), lambda j, *_: (0, j)), 1
    seqs, parts, each, size = grads.shape
    return pl.BlockSpec((seqs, 1, each, size), lambda j, *_: (0, j, 0, 0)), parts


def weight_grad(half, order, inputs, grads, wide, first=0, earlier=()):
    count, width = inputs.shape
    size = 1024
    spec, parts = grad_spec(grads)
    rows = width // 64
    return pl.pallas_call(
        functools.partial(weight_grad_kernel, half),
        grid_spec=pltpu.PrefetchScalarGridSpec(
            num_scalar_prefetch=1,
            grid=(parts,),
            in_specs=[once((count, width)), spec]
            + [pl.BlockSpec(memory_space=pl.ANY)] * len(earlier),
            out_specs=pl.BlockSpec(
                (2, 4, 4, rows, size), lambda j, *_: (0, 0, 0, 0, first // size + j)
            ),
            scratch_shapes=[pltpu.VMEM((count, width // 2), BF16)],
        ),
        out_shape=far((2, 4, 4, rows, wide), BF16),
        input_output_aliases={3: 0} if earlier else {},
        compiler_params=params(20),
        cost_estimate=cost(count * width * parts * size, count * (width + parts * size) * 2 + width * parts * size),
        name="weight_grad",
    )(order, inputs, held(grads), *[held(a) for a in earlier])


def norm_two_kernel(lengths, hidden_grad, weight, resid, cot, table, *outs):
    grad_resid, low_ref, mixed_grad, gain_grad, bias_grad, out_bias_grad = outs
    step = pl.program_id(0)
    rows, width = resid.shape[1:]
    valid = valid_rows(lengths[step], rows)
    grad = mm(hidden_grad[0], weight[:, width:], NT)
    unit, scale = norm_parts(resid[0])
    total = cot[0].astype(F32) * valid + norm_back(unit, scale, grad, table[5:6, :])
    grad_resid[0] = total
    low = total.astype(BF16)
    low_ref[0] = low
    mixed_grad[0] = mm(low, weight[:, :width], NT).astype(BF16)
    add_first(step, gain_grad, column_sum(grad * unit))
    add_first(step, bias_grad, column_sum(grad))
    add_first(step, out_bias_grad, column_sum(low.astype(F32)))


def norm_two_back(lengths, hidden_grad, weight, resid, cot, table):
    seqs, rows, width = resid.shape
    hidden = hidden_grad.shape[1]
    row_block = pl.BlockSpec((1, rows, width), lambda s, *_: (s, 0, 0))
    vec = pl.BlockSpec((1, width), lambda s, *_: (0, 0))
    return pl.pallas_call(
        norm_two_kernel,
        grid_spec=pltpu.PrefetchScalarGridSpec(
            num_scalar_prefetch=1,
            grid=(seqs,),
            in_specs=[
                pl.BlockSpec((1, rows, hidden), lambda s, *_: (s, 0, 0)),
                once((width, width + hidden)),
                row_block,
                row_block,
                once(table.shape),
            ],
            out_specs=[row_block] * 3 + [vec] * 3,
        ),
        out_shape=[
            far(resid.shape, F32),
            jax.ShapeDtypeStruct(resid.shape, BF16),
            jax.ShapeDtypeStruct(resid.shape, BF16),
        ]
        + [jax.ShapeDtypeStruct((1, width), F32)] * 3,
        compiler_params=params(40),
        cost_estimate=cost(2 * seqs * rows * width * (hidden + width), seqs * rows * (2 * hidden + 14 * width)),
        name="norm_two_back",
    )(lengths, held(hidden_grad.reshape(seqs, rows, hidden)), held(weight), held(resid), held(cot), table)


def norm_one_kernel(lengths, thirds, weight, x, grad_resid, table, *outs):
    input_grad, gain_grad, bias_grad, q_sum, v_sum = outs
    step = pl.program_id(0)
    rows, width = x.shape[1:]
    valid = valid_rows(lengths[step], rows)
    grad = mm(thirds[0, 0], weight[:, :width], NT)
    grad += mm(thirds[0, 1], weight[:, width : 2 * width], NT)
    grad += mm(thirds[0, 2], weight[:, 2 * width : 3 * width], NT)
    unit, scale = norm_parts(x[0].astype(F32) * valid)
    input_grad[0] = (grad_resid[0] + norm_back(unit, scale, grad, table[0:1, :])) * valid
    add_first(step, gain_grad, column_sum(grad * unit))
    add_first(step, bias_grad, column_sum(grad))
    add_first(step, q_sum, column_sum(thirds[0, 0].astype(F32)))
    add_first(step, v_sum, column_sum(thirds[0, 2].astype(F32)))


def norm_one_back(lengths, thirds, weight, x, grad_resid, table):
    seqs, rows, width = x.shape
    row_block = pl.BlockSpec((1, rows, width), lambda s, *_: (s, 0, 0))
    vec = pl.BlockSpec((1, width), lambda s, *_: (0, 0))
    return pl.pallas_call(
        norm_one_kernel,
        grid_spec=pltpu.PrefetchScalarGridSpec(
            num_scalar_prefetch=1,
            grid=(seqs,),
            in_specs=[
                pl.BlockSpec((1, 3, rows, width), lambda s, *_: (s, 0, 0, 0)),
            ]
            + [once(weight.shape), row_block, row_block, once(table.shape)],
            out_specs=[row_block] + [vec] * 4,
        ),
        out_shape=[far(x.shape, F32)] + [jax.ShapeDtypeStruct((1, width), F32)] * 4,
        compiler_params=params(32),
        cost_estimate=cost(6 * seqs * rows * width * width, seqs * rows * width * 16 + 6 * width * width),
        name="norm_one_back",
    )(lengths, held(thirds), held(weight), held(x), held(grad_resid), table)

def near_kernel(*refs):
    for at in range(4):
        mine, other, out = refs[at], refs[4 + at], refs[8 + at]
        total = mine[...].astype(F32) + other[...].astype(F32)
        out[...] = total.astype(BF16).reshape(out.shape)


def near_sum(own, arrived):
    _, shards, _, rows, wide = own.shape
    over_x = (1, 1, 2, 1, rows, wide)
    over_y = (1, 1, 1, 2, rows, wide)
    specs = [
        pl.BlockSpec(over_x, lambda s: (0, s, 0, 0, 0, 0)),
        pl.BlockSpec(over_y, lambda s: (1, s, 0, 0, 0, 0)),
        pl.BlockSpec(over_x, lambda s: (0, s, 0, 1, 0, 0)),
        pl.BlockSpec(over_y, lambda s: (1, s, 1, 0, 0, 0)),
    ]
    shape = (2, shards, 2, 2, rows, wide)
    return pl.pallas_call(
        near_kernel,
        grid=(shards,),
        in_specs=specs * 2,
        out_specs=[pl.BlockSpec((1, 2, rows, wide), lambda s: (s, 0, 0, 0))] * 4,
        out_shape=[jax.ShapeDtypeStruct((shards, 2, rows, wide), BF16)] * 4,
        compiler_params=params(14),
        cost_estimate=cost(own.size, own.size * 6),
        name="near_sum",
    )(*[own.reshape(shape)] * 4, *[arrived.reshape(shape)] * 4)


AXES = ("group", "dp")
Z = 4


def permutation(move):
    pairs = []
    for g in range(4):
        for d in range(2 * Z):
            to_g, to_z, to_c = move(g, d // 2, d % 2)
            pairs.append((g * 2 * Z + d, (to_g * Z + to_z) * 2 + to_c))
    return pairs


CORE = permutation(lambda g, z, c: (g, z, 1 - c))
OVER_X = permutation(lambda g, z, c: (g ^ 1, z, c))
OVER_Y = permutation(lambda g, z, c: (g ^ 2, z, c))
OVER_XY = permutation(lambda g, z, c: (g ^ 3, z, c))
OVER_Z = [permutation(lambda g, z, c, k=k: (g, (z + k) % Z, c)) for k in range(Z)]
NEAR_Z = permutation(lambda g, z, c: (g, z ^ 1, c))
FAR_Z = permutation(lambda g, z, c: (g, z ^ 2, c))


def send(array, pairs):
    return lax.ppermute(array, AXES, pairs)


def tie(value, *others):
    return lax.optimization_barrier((value,) + others)[0]


def pick(array, index, axis):
    return lax.dynamic_index_in_dim(array, index, axis, keepdims=False)


def plus(former, latter):
    return (former.astype(F32) + latter.astype(F32)).astype(BF16)


def quarters(shard, g):
    rows, wide = shard.shape
    parts = shard.reshape(4, 2, rows // 8, wide)
    return parts, pick(parts, g, 0)


def send_quarter(mine):
    return [send(mine, OVER_Z[k]) for k in range(1, Z)]


def send_xy(first, second):
    return send(first, OVER_X), send(second, OVER_Y)


def scatter_core(other):
    return send(other, CORE)


def scatter_far(first, second, from_x, from_y):
    first = plus(first, from_x)
    second = plus(second, from_y)
    return first[:, 0], second[:, 0], first[:, 1], second[:, 1]


def scatter_z(first, second, from_y, from_x, z):
    quarter = jnp.stack([plus(first, from_y), plus(second, from_x)], 1)
    return pick(quarter, z, 0), [pick(quarter, (z + k) % Z, 0) for k in range(1, Z)]


def send_z(parts):
    return [send(part, OVER_Z[k]) for k, part in enumerate(parts, 1)]


def spread(mine, arrived):
    total = mine.astype(F32)
    for part in arrived:
        total = total + part.astype(F32)
    return total.astype(BF16)


def send_near(mine):
    return [send(mine, OVER_X), send(mine, OVER_Y), send(mine, OVER_XY)]


def placed(mine, others, g):
    grid = jnp.stack([mine, *others]).reshape(2, 2, *mine.shape)
    grid = jnp.where(g % 2 == 1, grid[:, ::-1], grid)
    grid = jnp.where(g // 2 == 1, grid[::-1], grid)
    return grid.astype(F32).reshape(-1, mine.shape[-1])


def trade(shard, g):
    rows, wide = shard.shape
    parts = shard.reshape(4, rows // 4, wide)
    return pick(parts, g, 0), [pick(parts, g ^ over, 0) for over in (1, 2, 3)]


def send_trade(parts):
    return [send(part, pairs) for part, pairs in zip(parts, (OVER_X, OVER_Y, OVER_XY))]


def spread_xy(mine):
    half = mine.shape[0] // 2
    over_x, over_y = send_xy(mine, mine)
    second, first = send_xy(over_y[half:], over_x[:half])
    return [over_x, over_y, jnp.concatenate([first, second])]


VEC = (0, 1, 3, 5, 6, 7, 9, 11)


def joined(vectors):
    total = sum(v.shape[0] for v in vectors)
    at = 0
    out = None
    for v in vectors:
        wide = lax.pad(v, jnp.zeros((), v.dtype), [(at, total - at - v.shape[0], 0)])
        out = wide if out is None else out + wide
        at += v.shape[0]
    return out


def widened(weight, vectors):
    rows = weight.shape[0]
    columns = joined(vectors).reshape(-1, rows).T
    columns = jnp.pad(columns, ((0, 0), (0, LANES - columns.shape[1])))
    return jnp.concatenate([weight, columns], 1)


def spaced(table, first, last, rows):
    part = table[first:last].reshape(last - first, -1, rows)
    return part.transpose(1, 0, 2).reshape(1, -1)


def packed_vectors(grads):
    return joined([grads[i].reshape(-1) for i in VEC])


def own_vectors(total, grads, shards):
    d = lax.axis_index("dp")
    at = 0
    summed = {}
    for i in VEC:
        size = shards[i].shape[0]
        summed[i] = lax.dynamic_slice(total, (at + d * size,), (size,))
        at += grads[i].size
    return summed


def over_dp(array):
    return lax.psum_scatter(array, "dp", scatter_dimension=0, tiled=True)


def local(ring, layer_input, lengths, *rest):
    shards, cot = rest[:12], rest[12]
    micro, seqs, rows, width = layer_input.shape
    count = micro * seqs
    g = lax.axis_index("group")
    d = lax.axis_index("dp")
    z, c = d // 2, d % 2
    pos = jnp.stack([g, z, c]).astype(jnp.int32)
    order = [2, 1 - c, c, g] if ring else [1, 0, 4, 0]
    order = jnp.stack([jnp.asarray(v, jnp.int32) for v in order])
    lens = lengths.reshape(-1)
    x = layer_input.reshape(count, rows, width)
    cot = cot.reshape(count, rows, width)
    flat = lambda a: a.reshape(count * rows, a.shape[-1])
    rows_each = shards[2].shape[0]
    wanted = (widened(shards[2], [shards[i] for i in VEC]), jnp.concatenate([shards[4], shards[8]], 1), shards[10])

    if ring:
        parts_p, mine_p = quarters(wanted[0], g)
        parts_e, mine_e = quarters(wanted[1], g)
        ring_p = send_quarter(mine_p)
        core_p, core_e = send(parts_p, CORE), send(parts_e, CORE)
        stack_p = jnp.stack(tie(ring_p, core_p, core_e), 1)
        x_p, y_p = send_xy(stack_p, stack_p)
        mine_e = tie(mine_e, stack_p)
        e_one, e_two = send(mine_e, OVER_Z[1]), send(mine_e, OVER_Z[2])
        x_p, y_p, e_one, e_two, mine_e = tie((x_p, y_p, e_one, e_two, mine_e))
        b_p, a_p = send_xy(y_p[1], x_p[0])
        e_three = send(mine_e, OVER_Z[3])
        near_p = jnp.stack([stack_p, x_p, y_p])
        near_core_p = send(near_p, CORE)
        a_p, b_p, e_three, near_core_p = tie((a_p, b_p, e_three, near_core_p))
        far_p = jnp.stack([a_p, b_p])
        pieces_p = [parts_p, near_p, far_p, core_p, near_core_p, send(far_p, CORE)]
        stack_e = jnp.stack(tie((e_one, e_two, e_three), pieces_p), 1)
        lens_project, shard_r = tie((lens, wanted[2]), stack_e)
        x_e, y_e = send_xy(stack_e, stack_e)
        reduce_w = lax.all_gather(shard_r, "dp", axis=0, tiled=True)
        vectors = ()
    else:
        pieces = [lax.all_gather(w, "dp", axis=0, tiled=True) for w in wanted]
        pieces_p, pieces_e, reduce_w = [pieces[0]], [pieces[1]], pieces[2]
        lens_project = lens
        table = pieces[0][:, 3 * width : 3 * width + 16].T.astype(F32)
        pair = spaced(table, 2, 4, rows_each)
        middle = jnp.zeros((1, width), F32)
        vectors = (table, jnp.concatenate([pair[:, :width], middle, pair[:, width:]], -1))
    normed, packed, up, up_sum, project_w, table = project(
        ring, rows_each, lens_project, pos, x, cot, pieces_p, vectors
    )
    expand_b = spaced(table, 7, 11, rows_each)
    mixed, lse = attend(0, 1, lens, packed)
    lens_attend = lens
    if ring:
        x_e, y_e = tie((x_e, y_e), mixed)
        near_e = jnp.stack([stack_e, x_e, y_e])
        lens_attend = tie(lens, near_e)
        b_e, a_e = send_xy(y_e[1], x_e[0])
        near_core_e = send(near_e, CORE)
    mixed, lse = attend(1, count - 1, lens_attend, packed, (mixed, lse))
    if ring:
        a_e, b_e = tie((a_e, b_e), mixed)
        far_e = jnp.stack([a_e, b_e])
        pieces_e = [parts_e, near_e, far_e, core_e, near_core_e, send(far_e, CORE)]
    resid, normed_two, joint_w = branch(ring, lens, pos, x, mixed, table, pieces_e)
    act, slope, reduce_grad = expand(count, flat(normed_two), flat(up), joint_w, expand_b)
    shard_r = over_dp(reduce_grad)
    hidden_grad, hidden_sum = hidden_back(count, flat(up), reduce_w, slope)
    grad_resid, branch_low, mixed_grad, gain_two_grad, bias_two_grad, output_b_grad = norm_two_back(
        lens, hidden_grad, joint_w, resid, cot, table
    )
    thirds = attend_back(0, count, lens, packed, lse, mixed_grad)
    expand_grad = whole_grad(flat(normed_two), tie(hidden_grad, thirds), 0)
    shard_e = over_dp(expand_grad)
    branch_part = flat(branch_low)
    project_far = weight_grad(0, order, flat(mixed), branch_part, 4 * width)
    project_near = weight_grad(1, order, flat(mixed), branch_part, 4 * width)
    order_far = order
    if ring:
        mine_r, parts_r = trade(tie(shard_r, (project_far, project_near)), g)
        order_far = tie(order, parts_r)
        arrived_r = send_trade(parts_r)
    project_far = weight_grad(
        0, order_far, flat(normed), thirds, 4 * width, width, (project_far,)
    )
    order_near = order
    if ring:
        order_near = tie(order, project_far)
        arrived = send(project_far, CORE)
    project_near = weight_grad(
        1, order_near, flat(normed), thirds, 4 * width, width, (project_near,)
    )
    lens_one = lens
    if ring:
        spread_r = spread(mine_r, tie(arrived_r, project_near))
        ps = near_sum(project_near, arrived)
        lens_one = tie(lens, ps, spread_r)
        from_x, from_y = send_xy(ps[2], ps[3])
    input_grad, gain_one_grad, bias_one_grad, query_sum, value_sum = norm_one_back(
        lens_one, thirds, project_w, x, grad_resid, table
    )
    vectors = {
        0: gain_one_grad,
        1: bias_one_grad,
        3: jnp.concatenate([query_sum, value_sum], -1),
        5: output_b_grad,
        6: gain_two_grad,
        7: bias_two_grad,
        9: hidden_sum,
        11: up_sum,
    }
    total = packed_vectors(vectors)
    lens_out = lens
    if ring:
        total = total.reshape(-1, LANES)
        total = total + send(total, CORE)
        total = (total + send(total, OVER_XY)) + (send(total, OVER_X) + send(total, OVER_Y))
        total, from_x, from_y = tie((total, from_x, from_y))
        ps = scatter_far(ps[0], ps[1], from_x, from_y)
        lens_out = tie(lens, ps)
        from_x, from_y = send_xy(ps[3], ps[2])
        column = [send(total, OVER_Z[k]) for k in range(1, Z)]
    layer_output = reduce_out(lens_out, resid, act, reduce_w, table)
    sums = {}
    if ring:
        (from_x, from_y, column), layer_output = lax.optimization_barrier(
            ((from_x, from_y, column), layer_output)
        )
        mine_z, parts_z = scatter_z(ps[0], ps[1], from_y, from_x, z)
        arrived_p = send_z(parts_z)
        spread_r = tie(spread_r, parts_z)
        x_r, y_r = send_xy(spread_r, spread_r)
        half = spread_r.shape[0] // 2
        b_r, a_r = send_xy(y_r[half:], x_r[:half])
        sums[10] = placed(spread_r, [x_r, y_r, jnp.concatenate([a_r, b_r])], g)
        total = (total + column[1]) + (column[0] + column[2])
        mine_e, parts_e = trade(tie(shard_e, (x_r, y_r)), g)
        arrived_e = send_trade(parts_e)
        spread_p = spread(mine_z, tie(arrived_p, parts_e))
        near_p = send_near(spread_p)
        spread_e = spread(mine_e, tie(arrived_e, spread_p))
        near_e = send_near(spread_e)
        joint_sum = placed(spread_p, near_p, g)
        sums[8] = placed(spread_e, near_e, g)
    else:
        total = lax.psum(total, ("group", "dp"))
        sums[10] = lax.psum(shard_r, "group").astype(F32)
        sums[8] = lax.psum(shard_e, "group").astype(F32)
        parts = [a.transpose(1, 2, 0, 3, 4) for a in (project_far, project_near)]
        parts = over_dp(jnp.concatenate(parts).reshape(width, 4 * width))
        joint_sum = lax.psum(parts, "group").astype(F32)
    sums.update(own_vectors(total.reshape(-1), vectors, shards))
    sums[4] = joint_sum[:, :width]
    sums[2] = joint_sum[:, width:]
    return (
        layer_output.reshape(layer_input.shape),
        input_grad.reshape(layer_input.shape),
        *[sums[i] for i in range(12)],
    )


def solution(mesh):
    ring = mesh.shape["group"] == 4 and mesh.shape["dp"] == 2 * Z
    rows = P(None, ("group", "dp"), None, None)
    vec = P("dp")
    mat = P("dp", None)
    kinds = (vec, vec, mat, vec, mat, vec, vec, vec, mat, vec, mat, vec)
    return jax.shard_map(
        functools.partial(local, ring),
        mesh=mesh,
        in_specs=(rows, P(None, ("group", "dp")), *kinds, rows),
        out_specs=(rows, rows, *kinds),
        check_vma=False,
    )
```

```python
import functools

import jax
import jax.numpy as jnp
from jax import lax
from jax.experimental import pallas as pl
from jax.experimental.pallas import tpu as pltpu
from jax.sharding import PartitionSpec as P

F32 = jnp.float32
BF16 = jnp.bfloat16
EPS = 1e-06
H = 16
E = 64
LANES = 128
HALF_ROOT = 2.0 ** -0.5
INV_ROOT_TAU = 0.3989422804014327
NN = (((1,), (0,)), ((), ()))
NT = (((1,), (1,)), ((), ()))
TN = (((0,), (0,)), ((), ()))


def mm(former, latter, dims=NN):
    return lax.dot_general(former, latter, dims, preferred_element_type=F32)


def params(mib):
    return pltpu.CompilerParams(vmem_limit_bytes=mib << 20, dimension_semantics=("arbitrary",))


def cost(flops, nbytes, other=0):
    return pl.CostEstimate(flops=int(flops), bytes_accessed=int(nbytes), transcendentals=int(other))


def once(shape):
    return pl.BlockSpec(memory_space=pltpu.VMEM)


def valid_rows(length, rows):
    return (lax.broadcasted_iota(jnp.int32, (rows, 1), 0) < length).astype(F32)


def norm_parts(values):
    centred = values - jnp.mean(values, -1, keepdims=True)
    scale = lax.rsqrt(jnp.mean(centred * centred, -1, keepdims=True) + EPS)
    return centred * scale, scale


def norm_back(unit, scale, grad, gain):
    grad_unit = grad * gain
    first = jnp.mean(grad_unit, -1, keepdims=True)
    second = jnp.mean(grad_unit * unit, -1, keepdims=True)
    return scale * (grad_unit - first - unit * second)


def far(shape, dtype):
    return pltpu.HBM(shape, dtype)


def held(array):
    return pltpu.with_memory_space_constraint(array, pltpu.HBM)


def column_sum(values):
    return jnp.sum(values, 0, keepdims=True)


def add_first(step, ref, value):
    @pl.when(step == 0)
    def _():
        ref[...] = value

    @pl.when(step > 0)
    def _():
        ref[...] += value


def collect(ring, pos, pieces, whole, sems):
    copies = []

    def put(source, target):
        copy = pltpu.make_async_copy(source, target, sems.at[len(copies)])
        copy.start()
        copies.append(copy)

    if not ring:
        put(pieces[0], whole)
    else:
        g, z, c = pos[0], pos[1], pos[2]
        for at in range(2):
            core = c if at == 0 else 1 - c
            own, near, far = pieces[3 * at : 3 * at + 3]
            put(own, whole.at[z, core])
            for k in range(1, Z):
                row = lax.rem(z + Z - k, Z)
                for over in range(3):
                    put(near.at[over, :, k - 1], whole.at[row, core, g ^ over])
                for part in range(2):
                    put(far.at[part, k - 1], whole.at[row, core, g ^ 3, part])
    for copy in copies:
        copy.wait()


def whole_shape(ring, pieces):
    if ring:
        return (Z, 2) + pieces[0].shape
    return pieces[0].shape


def collect_scratch(ring, pieces):
    return [
        pltpu.VMEM(whole_shape(ring, pieces), BF16),
        pltpu.SemaphoreType.DMA((32,)),
        pltpu.SemaphoreType.DMA,
    ]


def fill(ring, step, steps, pos, pieces, kept, whole, sems, sem):
    @pl.when(step == 0)
    def _():
        collect(ring, pos, pieces, whole, sems)
        pltpu.make_async_copy(whole, kept, sem).start()


def keep(step, steps, kept, whole, sem):
    @pl.when(step == steps - 1)
    def _():
        pltpu.make_async_copy(whole, kept, sem).wait()


def flat_rows(whole):
    value = whole[...]
    return value.reshape(-1, value.shape[-1])


def project_kernel(ring, count, rows_each, lengths, pos, x, cot, *refs):
    normed, packed, up, up_sum, kept, table, whole, sems, sem, weight_bias = refs[-10:]
    pieces = refs[:-10] if ring else refs[:-12]
    step = pl.program_id(0)
    fill(ring, step, count, pos, pieces, kept, whole, sems, sem)
    rows, width = x.shape[1:]

    @pl.when(step == 0)
    def _():
        if ring:
            columns = whole[..., 3 * width :].reshape(width, LANES).astype(F32)
            table[...] = columns.T[: table.shape[0], :]
            weight_bias[...] = jnp.zeros(weight_bias.shape, F32)
            for shard in range(width // rows_each):
                for part in range(2):
                    at = (2 * shard + part) * rows_each
                    at += width if at >= width else 0
                    source = table[2 + part : 3 + part, shard * rows_each : (shard + 1) * rows_each]
                    weight_bias[:, at : at + rows_each] = source
        else:
            table[...] = refs[-12][...]
            weight_bias[...] = refs[-11][...]

    valid = valid_rows(lengths[step], rows)
    unit, _ = norm_parts(x[0].astype(F32) * valid)
    low = (unit * table[0:1, :] + table[1:2, :]).astype(BF16)
    normed[0] = low
    weight = whole[..., : 3 * width].reshape(width, 3 * width)
    packed[0] = (mm(low, weight) + weight_bias[...]).astype(BF16)
    upstream = cot[0].astype(F32) * valid
    up[0] = upstream.astype(BF16)
    add_first(step, up_sum, column_sum(upstream))
    keep(step, count, kept, whole, sem)


def project(ring, rows_each, lengths, pos, x, cot, pieces, vectors=()):
    seqs, rows, width = x.shape
    wide = 3 * width
    row_block = pl.BlockSpec((1, rows, width), lambda s, *_: (s, 0, 0))
    anywhere = pl.BlockSpec(memory_space=pl.ANY)
    normed, packed, up, up_sum, kept, table = pl.pallas_call(
        functools.partial(project_kernel, ring, seqs, rows_each),
        grid_spec=pltpu.PrefetchScalarGridSpec(
            num_scalar_prefetch=2,
            grid=(seqs,),
            in_specs=[row_block, row_block]
            + [anywhere] * len(pieces)
            + [once(v.shape) for v in vectors],
            out_specs=[
                row_block,
                pl.BlockSpec((1, rows, wide), lambda s, *_: (s, 0, 0)),
                row_block,
                pl.BlockSpec((1, width), lambda s, *_: (0, 0)),
                anywhere,
                pl.BlockSpec((16, width), lambda s, *_: (0, 0)),
            ],
            scratch_shapes=collect_scratch(ring, pieces) + [pltpu.VMEM((1, wide), F32)],
        ),
        out_shape=[
            jax.ShapeDtypeStruct(x.shape, BF16),
            far((seqs, rows, wide), BF16),
            jax.ShapeDtypeStruct(x.shape, BF16),
            jax.ShapeDtypeStruct((1, width), F32),
            far(whole_shape(ring, pieces), BF16),
            jax.ShapeDtypeStruct((16, width), F32),
        ],
        compiler_params=params(30),
        cost_estimate=cost(2 * seqs * rows * width * wide, seqs * rows * (4 * width + wide) * 2 + 4 * width * wide),
        name="norm_project",
    )(lengths, pos, held(x), held(cot), *[held(piece) for piece in pieces], *vectors)
    return normed, packed, up, up_sum, kept.reshape(width, -1), table


LEAST = 256
RATE = E**-0.5 * 1.4426950408889634


def attend_kernel(seq, lengths, q, k, v, *refs):
    mixed, lse = refs[-2:]
    rows = q.shape[1]
    length = lengths[seq + pl.program_id(0)]
    key_ok = lax.broadcasted_iota(jnp.int32, (1, rows - LEAST), 1) + LEAST < length
    lane = lax.broadcasted_iota(jnp.int32, (rows, LANES), 1)
    low_lane = lane < E
    logs = jnp.zeros((rows, LANES), F32)
    for pair in range(q.shape[2] // LANES):
        at = slice(pair * LANES, (pair + 1) * LANES)
        qs, ks, vs = q[0, :, at], k[0, :, at], v[0, :, at]
        outs = []
        for head in range(2):
            keep = low_lane if head == 0 else ~low_lane
            scores = mm(jnp.where(keep, qs, jnp.zeros_like(qs)), ks, NT)
            scores = jnp.concatenate(
                [scores[:, :LEAST], jnp.where(key_ok, scores[:, LEAST:], -1e30)], 1
            )
            top = jnp.max(scores, -1, keepdims=True)
            weights = jnp.exp2((scores - top) * RATE)
            total = jnp.sum(weights, -1, keepdims=True)
            outs.append(mm(weights.astype(BF16), vs) * (1.0 / total))
            logs = jnp.where(lane == 2 * pair + head, top * RATE + jnp.log2(total), logs)
        mixed[0, :, at] = jnp.where(low_lane, outs[0], outs[1]).astype(BF16)
    lse[0, 0] = logs.T[: lse.shape[2], :]


def attend(seq, here, lengths, packed, earlier=()):
    seqs, rows, wide = packed.shape
    width = wide // 3
    wid = 4 * LANES
    steps = width // wid
    block = lambda part: pl.BlockSpec((1, rows, wid), lambda s, j, *_: (seq + s, 0, part * steps + j))
    return pl.pallas_call(
        functools.partial(attend_kernel, seq),
        grid_spec=pltpu.PrefetchScalarGridSpec(
            num_scalar_prefetch=1,
            grid=(here, steps),
            in_specs=[block(0), block(1), block(2)]
            + [pl.BlockSpec(memory_space=pl.ANY)] * len(earlier),
            out_specs=[
                pl.BlockSpec((1, rows, wid), lambda s, j, *_: (seq + s, 0, j)),
                pl.BlockSpec((1, 1, 8, rows), lambda s, j, *_: (seq + s, j, 0, 0)),
            ],
        ),
        out_shape=[
            jax.ShapeDtypeStruct((seqs, rows, width), BF16),
            jax.ShapeDtypeStruct((seqs, steps, 8, rows), F32),
        ],
        input_output_aliases={4: 0, 5: 1} if earlier else {},
        compiler_params=pltpu.CompilerParams(
            vmem_limit_bytes=16 << 20, dimension_semantics=("arbitrary",) * 2
        ),
        cost_estimate=cost(4 * here * rows * rows * width * 8, here * rows * wide * 3, here * H * rows * rows),
        name="attend",
    )(lengths, *[held(packed)] * 3, *earlier)


def attend_back_kernel(seq, lengths, q, k, v, lse, grad, *refs):
    out = refs[-1]
    rows = q.shape[1]
    length = lengths[seq + pl.program_id(0)]
    key_ok = lax.broadcasted_iota(jnp.int32, (rows - LEAST, 1), 0) + LEAST < length
    low_lane = lax.broadcasted_iota(jnp.int32, (rows, LANES), 1) < E
    for pair in range(q.shape[2] // LANES):
        at = slice(pair * LANES, (pair + 1) * LANES)
        qs, ks, vs, gs = q[0, :, at], k[0, :, at], v[0, :, at], grad[0, :, at]
        sums = []
        for head in range(2):
            keep = low_lane if head == 0 else ~low_lane
            scores = mm(jnp.where(keep, ks, jnp.zeros_like(ks)), qs, NT)
            grad_probs = mm(jnp.where(keep, vs, jnp.zeros_like(vs)), gs, NT)
            row = 2 * pair + head
            probs = jnp.exp2(scores * RATE - lse[0, 0, row : row + 1, :])
            probs = jnp.concatenate(
                [probs[:LEAST], jnp.where(key_ok, probs[LEAST:], 0.0)], 0
            )
            inner = jnp.sum(grad_probs * probs, 0, keepdims=True)
            grad_scores = (probs * (grad_probs - inner)).astype(BF16)
            sums.append(
                (
                    mm(grad_scores, ks, TN) * E**-0.5,
                    mm(grad_scores, qs) * E**-0.5,
                    mm(probs.astype(BF16), gs),
                )
            )
        for part, first, second in zip(range(3), sums[0], sums[1]):
            out[0, part, :, at] = jnp.where(low_lane, first, second).astype(BF16)


def attend_back(seq, here, lengths, packed, lse, grad, earlier=()):
    seqs, rows, wide = packed.shape
    width = wide // 3
    wid = 4 * LANES
    steps = width // wid
    block = lambda part: pl.BlockSpec(
        (1, rows, wid), lambda s, j, *_: (seq + s, 0, part * steps + j)
    )
    return pl.pallas_call(
        functools.partial(attend_back_kernel, seq),
        grid_spec=pltpu.PrefetchScalarGridSpec(
            num_scalar_prefetch=1,
            grid=(here, steps),
            in_specs=[
                block(0),
                block(1),
                block(2),
                pl.BlockSpec((1, 1, 8, rows), lambda s, j, *_: (seq + s, j, 0, 0)),
                pl.BlockSpec((1, rows, wid), lambda s, j, *_: (seq + s, 0, j)),
            ]
            + [pl.BlockSpec(memory_space=pl.ANY)] * len(earlier),
            out_specs=pl.BlockSpec((1, 3, rows, wid), lambda s, j, *_: (seq + s, 0, 0, j)),
        ),
        out_shape=far((seqs, 3, rows, width), BF16),
        input_output_aliases={6: 0} if earlier else {},
        compiler_params=pltpu.CompilerParams(
            vmem_limit_bytes=18 << 20, dimension_semantics=("arbitrary",) * 2
        ),
        cost_estimate=cost(10 * here * rows * rows * width * 8, here * rows * wide * 5, here * H * rows * rows),
        name="attend_back",
    )(lengths, *[held(packed)] * 3, lse, grad, *[held(a) for a in earlier])


def branch_kernel(ring, count, lengths, pos, x, mixed, table, *refs):
    pieces, (resid, normed, kept, whole, sems, sem) = refs[:-6], refs[-6:]
    step = pl.program_id(0)
    fill(ring, step, count, pos, pieces, kept, whole, sems, sem)
    rows, width = x.shape[1:]
    valid = valid_rows(lengths[step], rows)
    weight = whole[..., :width].reshape(-1, width)
    total = x[0].astype(F32) * valid + mm(mixed[0], weight) + table[4:5, :]
    resid[0] = total
    unit, _ = norm_parts(total)
    normed[0] = (unit * table[5:6, :] + table[6:7, :]).astype(BF16)
    keep(step, count, kept, whole, sem)


def branch(ring, lengths, pos, x, mixed, table, pieces):
    seqs, rows, width = x.shape
    wide = pieces[0].shape[-1]
    row_block = pl.BlockSpec((1, rows, width), lambda s, *_: (s, 0, 0))
    anywhere = pl.BlockSpec(memory_space=pl.ANY)
    resid, normed, kept = pl.pallas_call(
        functools.partial(branch_kernel, ring, seqs),
        grid_spec=pltpu.PrefetchScalarGridSpec(
            num_scalar_prefetch=2,
            grid=(seqs,),
            in_specs=[row_block, row_block, once(table.shape)] + [anywhere] * len(pieces),
            out_specs=[row_block, row_block, anywhere],
            scratch_shapes=collect_scratch(ring, pieces),
        ),
        out_shape=[
            far(x.shape, F32),
            jax.ShapeDtypeStruct(x.shape, BF16),
            far(whole_shape(ring, pieces), BF16),
        ],
        compiler_params=params(26),
        cost_estimate=cost(2 * seqs * rows * width * width, seqs * rows * width * 10 + 4 * width * wide),
        name="branch",
    )(lengths, pos, held(x), mixed, table, *pieces)
    return resid, normed, kept.reshape(-1, wide)


def store_halves(ref, value):
    _, shards, quarters, rows, _ = ref.shape
    for shard in range(shards):
        for quarter in range(quarters):
            for half in range(2):
                at = ((shard * quarters + quarter) * 2 + half) * rows
                ref[half, shard, quarter] = value[at : at + rows]


def expand_kernel(seqs, normed, up, weight, bias, act, slope, grad):
    rows = normed.shape[0] // seqs
    for s in range(seqs):
        at = slice(s * rows, (s + 1) * rows)
        hidden = mm(normed[at, :], weight[...]) + bias[...]
        phi = 0.5 + 0.5 * lax.erf(hidden * HALF_ROOT)
        act[at, :] = (hidden * phi).astype(BF16)
        slope[at, :] = (phi + hidden * (INV_ROOT_TAU * jnp.exp(-0.5 * hidden * hidden))).astype(BF16)
    grad[...] = mm(act[...], up[...], TN).astype(BF16)


def expand(seqs, normed, up, weight, bias):
    count, width = normed.shape
    hidden = bias.shape[1]
    size = hidden // 4
    skip = (weight.shape[1] - hidden) // size
    wide = pl.BlockSpec((count, size), lambda i: (0, i))
    shape = far((count, hidden), BF16)
    return pl.pallas_call(
        functools.partial(expand_kernel, seqs),
        grid=(4,),
        in_specs=[
            once((count, width)),
            once((count, width)),
            pl.BlockSpec((width, size), lambda i: (0, skip + i)),
            pl.BlockSpec((1, size), lambda i: (0, i)),
        ],
        out_specs=[wide, wide, pl.BlockSpec((size, width), lambda i: (i, 0))],
        out_shape=[shape, shape, far((hidden, width), BF16)],
        compiler_params=params(36),
        cost_estimate=cost(4 * count * width * hidden, count * hidden * 4 + width * hidden * 4, count * hidden),
        name="expand",
    )(normed, up, held(weight), bias)


def reduce_kernel(lengths, resid, act, weight, table, out):
    rows = resid.shape[1]
    valid = valid_rows(lengths[pl.program_id(0)], rows)
    out[0] = (resid[0] + mm(act[0], weight[...]) + table[11:12, :]) * valid


def reduce_out(lengths, resid, act, weight, table):
    seqs, rows, width = resid.shape
    hidden = weight.shape[0]
    row_block = pl.BlockSpec((1, rows, width), lambda s, *_: (s, 0, 0))
    return pl.pallas_call(
        reduce_kernel,
        grid_spec=pltpu.PrefetchScalarGridSpec(
            num_scalar_prefetch=1,
            grid=(seqs,),
            in_specs=[
                row_block,
                pl.BlockSpec((1, rows, hidden), lambda s, *_: (s, 0, 0)),
                once((hidden, width)),
                once(table.shape),
            ],
            out_specs=row_block,
        ),
        out_shape=far(resid.shape, F32),
        compiler_params=params(26),
        cost_estimate=cost(2 * seqs * rows * width * hidden, seqs * rows * (8 * width + 2 * hidden) + 2 * width * hidden),
        name="reduce_out",
    )(lengths, held(resid), held(act.reshape(seqs, rows, hidden)), held(weight), table)


def hidden_back_kernel(seqs, up, weight, slope, grad, grad_sum):
    rows = up.shape[0] // seqs
    total = None
    for s in range(seqs):
        at = slice(s * rows, (s + 1) * rows)
        low = (mm(up[at, :], weight[...], NT) * slope[at, :].astype(F32)).astype(BF16)
        grad[at, :] = low
        part = column_sum(low.astype(F32))
        total = part if s == 0 else total + part
    grad_sum[...] = total


def hidden_back(seqs, up, weight, slope):
    count, width = up.shape
    hidden = slope.shape[1]
    size = hidden // 4
    wide = pl.BlockSpec((count, size), lambda i: (0, i))
    return pl.pallas_call(
        functools.partial(hidden_back_kernel, seqs),
        grid=(4,),
        in_specs=[once((count, width)), pl.BlockSpec((size, width), lambda i: (i, 0)), wide],
        out_specs=[wide, pl.BlockSpec((1, size), lambda i: (0, i))],
        out_shape=[far((count, hidden), BF16), jax.ShapeDtypeStruct((1, hidden), F32)],
        compiler_params=params(28),
        cost_estimate=cost(2 * count * width * hidden, count * hidden * 4 + 2 * width * hidden),
        name="hidden_back",
    )(up, held(weight), held(slope))


def whole_grad_kernel(inputs, grads, out):
    out[...] = mm(inputs[...], grads[...], TN).astype(BF16)


def whole_grad(inputs, grads, first):
    count, width = inputs.shape
    here = grads.shape[1] - first
    size = 1024
    return pl.pallas_call(
        whole_grad_kernel,
        grid=(here // size,),
        in_specs=[
            once((count, width)),
            pl.BlockSpec((count, size), lambda j: (0, first // size + j)),
        ],
        out_specs=pl.BlockSpec((width, size), lambda j: (0, j)),
        out_shape=far((width, here), BF16),
        compiler_params=params(28),
        cost_estimate=cost(2 * count * width * here, count * (width + here) * 2 + 2 * width * here),
        name="whole_grad",
    )(inputs, held(grads))


def pick_columns(half, order, inputs, picked):
    @pl.when(pl.program_id(0) == 0)
    def _():
        for i in range(4):
            size = picked.shape[1] // 4
            at = pl.multiple_of((order[0] * i + order[1 + half]) * size, size)
            picked[:, i * size : (i + 1) * size] = inputs[:, pl.ds(at, size)]


def weight_grad_kernel(half, order, inputs, grads, *refs):
    out, picked = refs[-2:]
    pick_columns(half, order, inputs, picked)
    block = grads[...].reshape(inputs.shape[0], grads.shape[-1])
    value = mm(picked[...], block, TN).astype(BF16)
    _, shards, _, rows, _ = out.shape
    for shard in range(shards):
        for quarter in range(4):
            for part in range(2):
                at = ((shard * 4 + quarter) * 2 + part) * rows
                out[part, shard, quarter ^ order[3]] = value[at : at + rows]


def grad_spec(grads):
    if len(grads.shape) == 2:
        return pl.BlockSpec((grads.shape[0], 1024), lambda j, *_: (0, j)), 1
    seqs, parts, each, size = grads.shape
    return pl.BlockSpec((seqs, 1, each, size), lambda j, *_: (0, j, 0, 0)), parts


def weight_grad(half, order, inputs, grads, wide, first=0, earlier=()):
    count, width = inputs.shape
    size = 1024
    spec, parts = grad_spec(grads)
    rows = width // 64
    return pl.pallas_call(
        functools.partial(weight_grad_kernel, half),
        grid_spec=pltpu.PrefetchScalarGridSpec(
            num_scalar_prefetch=1,
            grid=(parts,),
            in_specs=[once((count, width)), spec]
            + [pl.BlockSpec(memory_space=pl.ANY)] * len(earlier),
            out_specs=pl.BlockSpec(
                (2, 4, 4, rows, size), lambda j, *_: (0, 0, 0, 0, first // size + j)
            ),
            scratch_shapes=[pltpu.VMEM((count, width // 2), BF16)],
        ),
        out_shape=far((2, 4, 4, rows, wide), BF16),
        input_output_aliases={3: 0} if earlier else {},
        compiler_params=params(20),
        cost_estimate=cost(count * width * parts * size, count * (width + parts * size) * 2 + width * parts * size),
        name="weight_grad",
    )(order, inputs, held(grads), *[held(a) for a in earlier])


def norm_two_kernel(lengths, hidden_grad, weight, resid, cot, table, *outs):
    grad_resid, low_ref, mixed_grad, gain_grad, bias_grad, out_bias_grad = outs
    step = pl.program_id(0)
    rows, width = resid.shape[1:]
    valid = valid_rows(lengths[step], rows)
    grad = mm(hidden_grad[0], weight[:, width:], NT)
    unit, scale = norm_parts(resid[0])
    total = cot[0].astype(F32) * valid + norm_back(unit, scale, grad, table[5:6, :])
    grad_resid[0] = total
    low = total.astype(BF16)
    low_ref[0] = low
    mixed_grad[0] = mm(low, weight[:, :width], NT).astype(BF16)
    add_first(step, gain_grad, column_sum(grad * unit))
    add_first(step, bias_grad, column_sum(grad))
    add_first(step, out_bias_grad, column_sum(low.astype(F32)))


def norm_two_back(lengths, hidden_grad, weight, resid, cot, table):
    seqs, rows, width = resid.shape
    hidden = hidden_grad.shape[1]
    row_block = pl.BlockSpec((1, rows, width), lambda s, *_: (s, 0, 0))
    vec = pl.BlockSpec((1, width), lambda s, *_: (0, 0))
    return pl.pallas_call(
        norm_two_kernel,
        grid_spec=pltpu.PrefetchScalarGridSpec(
            num_scalar_prefetch=1,
            grid=(seqs,),
            in_specs=[
                pl.BlockSpec((1, rows, hidden), lambda s, *_: (s, 0, 0)),
                once((width, width + hidden)),
                row_block,
                row_block,
                once(table.shape),
            ],
            out_specs=[row_block] * 3 + [vec] * 3,
        ),
        out_shape=[
            far(resid.shape, F32),
            jax.ShapeDtypeStruct(resid.shape, BF16),
            jax.ShapeDtypeStruct(resid.shape, BF16),
        ]
        + [jax.ShapeDtypeStruct((1, width), F32)] * 3,
        compiler_params=params(40),
        cost_estimate=cost(2 * seqs * rows * width * (hidden + width), seqs * rows * (2 * hidden + 14 * width)),
        name="norm_two_back",
    )(lengths, held(hidden_grad.reshape(seqs, rows, hidden)), held(weight), held(resid), held(cot), table)


def norm_one_kernel(lengths, thirds, weight, x, grad_resid, table, *outs):
    input_grad, gain_grad, bias_grad, q_sum, v_sum = outs
    step = pl.program_id(0)
    rows, width = x.shape[1:]
    valid = valid_rows(lengths[step], rows)
    grad = mm(thirds[0, 0], weight[:, :width], NT)
    grad += mm(thirds[0, 1], weight[:, width : 2 * width], NT)
    grad += mm(thirds[0, 2], weight[:, 2 * width : 3 * width], NT)
    unit, scale = norm_parts(x[0].astype(F32) * valid)
    input_grad[0] = (grad_resid[0] + norm_back(unit, scale, grad, table[0:1, :])) * valid
    add_first(step, gain_grad, column_sum(grad * unit))
    add_first(step, bias_grad, column_sum(grad))
    add_first(step, q_sum, column_sum(thirds[0, 0].astype(F32)))
    add_first(step, v_sum, column_sum(thirds[0, 2].astype(F32)))


def norm_one_back(lengths, thirds, weight, x, grad_resid, table):
    seqs, rows, width = x.shape
    row_block = pl.BlockSpec((1, rows, width), lambda s, *_: (s, 0, 0))
    vec = pl.BlockSpec((1, width), lambda s, *_: (0, 0))
    return pl.pallas_call(
        norm_one_kernel,
        grid_spec=pltpu.PrefetchScalarGridSpec(
            num_scalar_prefetch=1,
            grid=(seqs,),
            in_specs=[
                pl.BlockSpec((1, 3, rows, width), lambda s, *_: (s, 0, 0, 0)),
            ]
            + [once(weight.shape), row_block, row_block, once(table.shape)],
            out_specs=[row_block] + [vec] * 4,
        ),
        out_shape=[far(x.shape, F32)] + [jax.ShapeDtypeStruct((1, width), F32)] * 4,
        compiler_params=params(32),
        cost_estimate=cost(6 * seqs * rows * width * width, seqs * rows * width * 16 + 6 * width * width),
        name="norm_one_back",
    )(lengths, held(thirds), weight, x, held(grad_resid), table)

def near_kernel(*refs):
    for at in range(4):
        mine, other, out = refs[at], refs[4 + at], refs[8 + at]
        total = mine[...].astype(F32) + other[...].astype(F32)
        out[...] = total.astype(BF16).reshape(out.shape)


def near_sum(own, arrived):
    _, shards, _, rows, wide = own.shape
    over_x = (1, 1, 2, 1, rows, wide)
    over_y = (1, 1, 1, 2, rows, wide)
    specs = [
        pl.BlockSpec(over_x, lambda s: (0, s, 0, 0, 0, 0)),
        pl.BlockSpec(over_y, lambda s: (1, s, 0, 0, 0, 0)),
        pl.BlockSpec(over_x, lambda s: (0, s, 0, 1, 0, 0)),
        pl.BlockSpec(over_y, lambda s: (1, s, 1, 0, 0, 0)),
    ]
    shape = (2, shards, 2, 2, rows, wide)
    return pl.pallas_call(
        near_kernel,
        grid=(shards,),
        in_specs=specs * 2,
        out_specs=[pl.BlockSpec((1, 2, rows, wide), lambda s: (s, 0, 0, 0))] * 4,
        out_shape=[jax.ShapeDtypeStruct((shards, 2, rows, wide), BF16)] * 4,
        compiler_params=params(14),
        cost_estimate=cost(own.size, own.size * 6),
        name="near_sum",
    )(*[held(own.reshape(shape))] * 4, *[held(arrived.reshape(shape))] * 4)


AXES = ("group", "dp")
Z = 4


def permutation(move):
    pairs = []
    for g in range(4):
        for d in range(2 * Z):
            to_g, to_z, to_c = move(g, d // 2, d % 2)
            pairs.append((g * 2 * Z + d, (to_g * Z + to_z) * 2 + to_c))
    return pairs


CORE = permutation(lambda g, z, c: (g, z, 1 - c))
OVER_X = permutation(lambda g, z, c: (g ^ 1, z, c))
OVER_Y = permutation(lambda g, z, c: (g ^ 2, z, c))
OVER_XY = permutation(lambda g, z, c: (g ^ 3, z, c))
OVER_Z = [permutation(lambda g, z, c, k=k: (g, (z + k) % Z, c)) for k in range(Z)]
NEAR_Z = permutation(lambda g, z, c: (g, z ^ 1, c))
FAR_Z = permutation(lambda g, z, c: (g, z ^ 2, c))


def send(array, pairs):
    return lax.ppermute(array, AXES, pairs)


def tie(value, *others):
    return lax.optimization_barrier((value,) + others)[0]


def pick(array, index, axis):
    return lax.dynamic_index_in_dim(array, index, axis, keepdims=False)


def plus(former, latter):
    return (former.astype(F32) + latter.astype(F32)).astype(BF16)


def quarters(shard, g):
    rows, wide = shard.shape
    parts = shard.reshape(4, 2, rows // 8, wide)
    return parts, pick(parts, g, 0)


def send_quarter(mine):
    return [send(mine, OVER_Z[k]) for k in range(1, Z)]


def send_xy(first, second):
    return send(first, OVER_X), send(second, OVER_Y)


def scatter_core(other):
    return send(other, CORE)


def scatter_far(first, second, from_x, from_y):
    first = plus(first, from_x)
    second = plus(second, from_y)
    return first[:, 0], second[:, 0], first[:, 1], second[:, 1]


def scatter_z(first, second, from_y, from_x, z):
    quarter = jnp.stack([plus(first, from_y), plus(second, from_x)], 1)
    return pick(quarter, z, 0), [pick(quarter, (z + k) % Z, 0) for k in range(1, Z)]


def send_z(parts):
    return [send(part, OVER_Z[k]) for k, part in enumerate(parts, 1)]


def spread(mine, arrived):
    total = mine.astype(F32)
    for part in arrived:
        total = total + part.astype(F32)
    return total.astype(BF16)


def send_near(mine):
    return [send(mine, OVER_X), send(mine, OVER_Y), send(mine, OVER_XY)]


def placed(mine, others, g):
    grid = jnp.stack([mine, *others]).reshape(2, 2, *mine.shape)
    grid = jnp.where(g % 2 == 1, grid[:, ::-1], grid)
    grid = jnp.where(g // 2 == 1, grid[::-1], grid)
    return grid.astype(F32).reshape(-1, mine.shape[-1])


def trade(shard, g):
    rows, wide = shard.shape
    parts = shard.reshape(4, rows // 4, wide)
    return pick(parts, g, 0), [pick(parts, g ^ over, 0) for over in (1, 2, 3)]


def send_trade(parts):
    return [send(part, pairs) for part, pairs in zip(parts, (OVER_X, OVER_Y, OVER_XY))]


def spread_xy(mine):
    half = mine.shape[0] // 2
    over_x, over_y = send_xy(mine, mine)
    second, first = send_xy(over_y[half:], over_x[:half])
    return [over_x, over_y, jnp.concatenate([first, second])]


VEC = (0, 1, 3, 5, 6, 7, 9, 11)


def joined(vectors):
    total = sum(v.shape[0] for v in vectors)
    at = 0
    out = None
    for v in vectors:
        wide = lax.pad(v, jnp.zeros((), v.dtype), [(at, total - at - v.shape[0], 0)])
        out = wide if out is None else out + wide
        at += v.shape[0]
    return out


def widened(weight, vectors):
    rows = weight.shape[0]
    columns = joined(vectors).reshape(-1, rows).T
    columns = jnp.pad(columns, ((0, 0), (0, LANES - columns.shape[1])))
    return jnp.concatenate([weight, columns], 1)


def spaced(table, first, last, rows):
    part = table[first:last].reshape(last - first, -1, rows)
    return part.transpose(1, 0, 2).reshape(1, -1)


def packed_vectors(grads):
    return joined([grads[i].reshape(-1) for i in VEC])


def own_vectors(total, grads, shards):
    d = lax.axis_index("dp")
    at = 0
    summed = {}
    for i in VEC:
        size = shards[i].shape[0]
        summed[i] = lax.dynamic_slice(total, (at + d * size,), (size,))
        at += grads[i].size
    return summed


def over_dp(array):
    return lax.psum_scatter(array, "dp", scatter_dimension=0, tiled=True)


def local(ring, layer_input, lengths, *rest):
    shards, cot = rest[:12], rest[12]
    micro, seqs, rows, width = layer_input.shape
    count = micro * seqs
    g = lax.axis_index("group")
    d = lax.axis_index("dp")
    z, c = d // 2, d % 2
    pos = jnp.stack([g, z, c]).astype(jnp.int32)
    order = [2, 1 - c, c, g] if ring else [1, 0, 4, 0]
    order = jnp.stack([jnp.asarray(v, jnp.int32) for v in order])
    lens = lengths.reshape(-1)
    x = layer_input.reshape(count, rows, width)
    cot = cot.reshape(count, rows, width)
    flat = lambda a: a.reshape(count * rows, a.shape[-1])
    rows_each = shards[2].shape[0]
    wanted = (widened(shards[2], [shards[i] for i in VEC]), jnp.concatenate([shards[4], shards[8]], 1), shards[10])

    if ring:
        parts_p, mine_p = quarters(wanted[0], g)
        parts_e, mine_e = quarters(wanted[1], g)
        ring_p = send_quarter(mine_p)
        core_p, core_e = send(parts_p, CORE), send(parts_e, CORE)
        stack_p = jnp.stack(tie(ring_p, core_p, core_e), 1)
        x_p, y_p = send_xy(stack_p, stack_p)
        mine_e = tie(mine_e, stack_p)
        e_one, e_two = send(mine_e, OVER_Z[1]), send(mine_e, OVER_Z[2])
        x_p, y_p, e_one, e_two, mine_e = tie((x_p, y_p, e_one, e_two, mine_e))
        b_p, a_p = send_xy(y_p[1], x_p[0])
        e_three = send(mine_e, OVER_Z[3])
        near_p = jnp.stack([stack_p, x_p, y_p])
        near_core_p = send(near_p, CORE)
        a_p, b_p, e_three, near_core_p = tie((a_p, b_p, e_three, near_core_p))
        far_p = jnp.stack([a_p, b_p])
        pieces_p = [parts_p, near_p, far_p, core_p, near_core_p, send(far_p, CORE)]
        stack_e = jnp.stack(tie((e_one, e_two, e_three), pieces_p), 1)
        lens_project, shard_r = tie((lens, wanted[2]), stack_e)
        x_e, y_e = send_xy(stack_e, stack_e)
        reduce_w = lax.all_gather(shard_r, "dp", axis=0, tiled=True)
        vectors = ()
    else:
        pieces = [lax.all_gather(w, "dp", axis=0, tiled=True) for w in wanted]
        pieces_p, pieces_e, reduce_w = [pieces[0]], [pieces[1]], pieces[2]
        lens_project = lens
        table = pieces[0][:, 3 * width : 3 * width + 16].T.astype(F32)
        pair = spaced(table, 2, 4, rows_each)
        middle = jnp.zeros((1, width), F32)
        vectors = (table, jnp.concatenate([pair[:, :width], middle, pair[:, width:]], -1))
    normed, packed, up, up_sum, project_w, table = project(
        ring, rows_each, lens_project, pos, x, cot, pieces_p, vectors
    )
    expand_b = spaced(table, 7, 11, rows_each)
    mixed, lse = attend(0, 1, lens, packed)
    lens_attend = lens
    if ring:
        x_e, y_e = tie((x_e, y_e), mixed)
        near_e = jnp.stack([stack_e, x_e, y_e])
        lens_attend = tie(lens, near_e)
        b_e, a_e = send_xy(y_e[1], x_e[0])
        near_core_e = send(near_e, CORE)
    mixed, lse = attend(1, count - 1, lens_attend, packed, (mixed, lse))
    if ring:
        a_e, b_e = tie((a_e, b_e), mixed)
        far_e = jnp.stack([a_e, b_e])
        pieces_e = [parts_e, near_e, far_e, core_e, near_core_e, send(far_e, CORE)]
    resid, normed_two, joint_w = branch(ring, lens, pos, x, mixed, table, pieces_e)
    act, slope, reduce_grad = expand(count, flat(normed_two), flat(up), joint_w, expand_b)
    shard_r = over_dp(reduce_grad)
    hidden_grad, hidden_sum = hidden_back(count, flat(up), reduce_w, slope)
    grad_resid, branch_low, mixed_grad, gain_two_grad, bias_two_grad, output_b_grad = norm_two_back(
        lens, hidden_grad, joint_w, resid, cot, table
    )
    thirds = attend_back(0, count, lens, packed, lse, mixed_grad)
    expand_grad = whole_grad(flat(normed_two), tie(hidden_grad, thirds), 0)
    shard_e = over_dp(expand_grad)
    branch_part = flat(branch_low)
    project_far = weight_grad(0, order, flat(mixed), branch_part, 4 * width)
    project_near = weight_grad(1, order, flat(mixed), branch_part, 4 * width)
    order_far = order
    if ring:
        mine_r, parts_r = trade(tie(shard_r, (project_far, project_near)), g)
        order_far = tie(order, parts_r)
        arrived_r = send_trade(parts_r)
    project_far = weight_grad(
        0, order_far, flat(normed), thirds, 4 * width, width, (project_far,)
    )
    order_near = order
    if ring:
        order_near = tie(order, project_far)
        arrived = send(project_far, CORE)
    project_near = weight_grad(
        1, order_near, flat(normed), thirds, 4 * width, width, (project_near,)
    )
    lens_one = lens
    if ring:
        spread_r = spread(mine_r, tie(arrived_r, project_near))
        ps = near_sum(project_near, arrived)
        lens_one = tie(lens, ps, spread_r)
        from_x, from_y = send_xy(ps[2], ps[3])
    input_grad, gain_one_grad, bias_one_grad, query_sum, value_sum = norm_one_back(
        lens_one, thirds, project_w, x, grad_resid, table
    )
    vectors = {
        0: gain_one_grad,
        1: bias_one_grad,
        3: jnp.concatenate([query_sum, value_sum], -1),
        5: output_b_grad,
        6: gain_two_grad,
        7: bias_two_grad,
        9: hidden_sum,
        11: up_sum,
    }
    total = packed_vectors(vectors)
    lens_out = lens
    if ring:
        total = total.reshape(-1, LANES)
        total = total + send(total, CORE)
        total = (total + send(total, OVER_XY)) + (send(total, OVER_X) + send(total, OVER_Y))
        total, from_x, from_y = tie((total, from_x, from_y))
        ps = scatter_far(ps[0], ps[1], from_x, from_y)
        lens_out = tie(lens, ps)
        from_x, from_y = send_xy(ps[3], ps[2])
        near_r = send_near(spread_r)
    layer_output = reduce_out(lens_out, resid, act, reduce_w, table)
    sums = {}
    if ring:
        (from_x, from_y, near_r), layer_output = lax.optimization_barrier(
            ((from_x, from_y, near_r), layer_output)
        )
        mine_z, parts_z = scatter_z(ps[0], ps[1], from_y, from_x, z)
        arrived_p = send_z(parts_z)
        mine_e, parts_e = trade(tie(shard_e, parts_z), g)
        arrived_e = send_trade(parts_e)
        sums[10] = placed(spread_r, near_r, g)
        spread_e = spread(mine_e, arrived_e)
        near_e = send_near(spread_e)
        total = tie(total, spread_e)
        total = total + send(total, NEAR_Z)
        total = total + send(total, FAR_Z)
        spread_p = spread(mine_z, tie(arrived_p, spread_e))
        near_p = send_near(spread_p)
        joint_sum = placed(spread_p, near_p, g)
        sums[8] = placed(spread_e, near_e, g)
    else:
        total = lax.psum(total, ("group", "dp"))
        sums[10] = lax.psum(shard_r, "group").astype(F32)
        sums[8] = lax.psum(shard_e, "group").astype(F32)
        parts = [a.transpose(1, 2, 0, 3, 4) for a in (project_far, project_near)]
        parts = over_dp(jnp.concatenate(parts).reshape(width, 4 * width))
        joint_sum = lax.psum(parts, "group").astype(F32)
    sums.update(own_vectors(total.reshape(-1), vectors, shards))
    sums[4] = joint_sum[:, :width]
    sums[2] = joint_sum[:, width:]
    return (
        layer_output.reshape(layer_input.shape),
        input_grad.reshape(layer_input.shape),
        *[sums[i] for i in range(12)],
    )


def solution(mesh):
    ring = mesh.shape["group"] == 4 and mesh.shape["dp"] == 2 * Z
    rows = P(None, ("group", "dp"), None, None)
    vec = P("dp")
    mat = P("dp", None)
    kinds = (vec, vec, mat, vec, mat, vec, vec, vec, mat, vec, mat, vec)
    return jax.shard_map(
        functools.partial(local, ring),
        mesh=mesh,
        in_specs=(rows, P(None, ("group", "dp")), *kinds, rows),
        out_specs=(rows, rows, *kinds),
        check_vma=False,
    )
```

```python
import functools

import jax
import jax.numpy as jnp
from jax import lax
from jax.experimental import pallas as pl
from jax.experimental.pallas import tpu as pltpu
from jax.sharding import PartitionSpec as P

F32 = jnp.float32
BF16 = jnp.bfloat16
EPS = 1e-06
H = 16
E = 64
LANES = 128
HALF_ROOT = 2.0 ** -0.5
INV_ROOT_TAU = 0.3989422804014327
NN = (((1,), (0,)), ((), ()))
NT = (((1,), (1,)), ((), ()))
TN = (((0,), (0,)), ((), ()))


def mm(former, latter, dims=NN):
    return lax.dot_general(former, latter, dims, preferred_element_type=F32)


def params(mib):
    return pltpu.CompilerParams(vmem_limit_bytes=mib << 20, dimension_semantics=("arbitrary",))


def cost(flops, nbytes, other=0):
    return pl.CostEstimate(flops=int(flops), bytes_accessed=int(nbytes), transcendentals=int(other))


def once(shape):
    return pl.BlockSpec(memory_space=pltpu.VMEM)


def valid_rows(length, rows):
    return (lax.broadcasted_iota(jnp.int32, (rows, 1), 0) < length).astype(F32)


def norm_parts(values):
    centred = values - jnp.mean(values, -1, keepdims=True)
    scale = lax.rsqrt(jnp.mean(centred * centred, -1, keepdims=True) + EPS)
    return centred * scale, scale


def norm_back(unit, scale, grad, gain):
    grad_unit = grad * gain
    first = jnp.mean(grad_unit, -1, keepdims=True)
    second = jnp.mean(grad_unit * unit, -1, keepdims=True)
    return scale * (grad_unit - first - unit * second)


def far(shape, dtype):
    return pltpu.HBM(shape, dtype)


def held(array):
    return pltpu.with_memory_space_constraint(array, pltpu.HBM)


def column_sum(values):
    return jnp.sum(values, 0, keepdims=True)


def add_first(step, ref, value):
    @pl.when(step == 0)
    def _():
        ref[...] = value

    @pl.when(step > 0)
    def _():
        ref[...] += value


def collect(ring, pos, pieces, whole, sems):
    copies = []

    def put(source, target):
        copy = pltpu.make_async_copy(source, target, sems.at[len(copies)])
        copy.start()
        copies.append(copy)

    if not ring:
        put(pieces[0], whole)
    else:
        g, z, c = pos[0], pos[1], pos[2]
        for at in range(2):
            core = c if at == 0 else 1 - c
            own, near, far = pieces[3 * at : 3 * at + 3]
            put(own, whole.at[z, core])
            for k in range(1, Z):
                row = lax.rem(z + Z - k, Z)
                for over in range(3):
                    put(near.at[over, :, k - 1], whole.at[row, core, g ^ over])
                for part in range(2):
                    put(far.at[part, k - 1], whole.at[row, core, g ^ 3, part])
    for copy in copies:
        copy.wait()


def whole_shape(ring, pieces):
    if ring:
        return (Z, 2) + pieces[0].shape
    return pieces[0].shape


def collect_scratch(ring, pieces):
    return [
        pltpu.VMEM(whole_shape(ring, pieces), BF16),
        pltpu.SemaphoreType.DMA((32,)),
        pltpu.SemaphoreType.DMA,
    ]


def fill(ring, step, steps, pos, pieces, kept, whole, sems, sem):
    @pl.when(step == 0)
    def _():
        collect(ring, pos, pieces, whole, sems)
        pltpu.make_async_copy(whole, kept, sem).start()


def keep(step, steps, kept, whole, sem):
    @pl.when(step == steps - 1)
    def _():
        pltpu.make_async_copy(whole, kept, sem).wait()


def flat_rows(whole):
    value = whole[...]
    return value.reshape(-1, value.shape[-1])


def project_kernel(ring, count, rows_each, lengths, pos, x, cot, *refs):
    normed, packed, up, up_sum, kept, table, whole, sems, sem, weight_bias = refs[-10:]
    pieces = refs[:-10] if ring else refs[:-12]
    step = pl.program_id(0)
    fill(ring, step, count, pos, pieces, kept, whole, sems, sem)
    rows, width = x.shape[1:]

    @pl.when(step == 0)
    def _():
        if ring:
            columns = whole[..., 3 * width :].reshape(width, LANES).astype(F32)
            table[...] = columns.T[: table.shape[0], :]
            weight_bias[...] = jnp.zeros(weight_bias.shape, F32)
            for shard in range(width // rows_each):
                for part in range(2):
                    at = (2 * shard + part) * rows_each
                    at += width if at >= width else 0
                    source = table[2 + part : 3 + part, shard * rows_each : (shard + 1) * rows_each]
                    weight_bias[:, at : at + rows_each] = source
        else:
            table[...] = refs[-12][...]
            weight_bias[...] = refs[-11][...]

    valid = valid_rows(lengths[step], rows)
    unit, _ = norm_parts(x[0].astype(F32) * valid)
    low = (unit * table[0:1, :] + table[1:2, :]).astype(BF16)
    normed[0] = low
    weight = whole[..., : 3 * width].reshape(width, 3 * width)
    packed[0] = (mm(low, weight) + weight_bias[...]).astype(BF16)
    upstream = cot[0].astype(F32) * valid
    up[0] = upstream.astype(BF16)
    add_first(step, up_sum, column_sum(upstream))
    keep(step, count, kept, whole, sem)


def project(ring, rows_each, lengths, pos, x, cot, pieces, vectors=()):
    seqs, rows, width = x.shape
    wide = 3 * width
    row_block = pl.BlockSpec((1, rows, width), lambda s, *_: (s, 0, 0))
    anywhere = pl.BlockSpec(memory_space=pl.ANY)
    normed, packed, up, up_sum, kept, table = pl.pallas_call(
        functools.partial(project_kernel, ring, seqs, rows_each),
        grid_spec=pltpu.PrefetchScalarGridSpec(
            num_scalar_prefetch=2,
            grid=(seqs,),
            in_specs=[row_block, row_block]
            + [anywhere] * len(pieces)
            + [once(v.shape) for v in vectors],
            out_specs=[
                row_block,
                pl.BlockSpec((1, rows, wide), lambda s, *_: (s, 0, 0)),
                row_block,
                pl.BlockSpec((1, width), lambda s, *_: (0, 0)),
                anywhere,
                pl.BlockSpec((16, width), lambda s, *_: (0, 0)),
            ],
            scratch_shapes=collect_scratch(ring, pieces) + [pltpu.VMEM((1, wide), F32)],
        ),
        out_shape=[
            jax.ShapeDtypeStruct(x.shape, BF16),
            far((seqs, rows, wide), BF16),
            jax.ShapeDtypeStruct(x.shape, BF16),
            jax.ShapeDtypeStruct((1, width), F32),
            far(whole_shape(ring, pieces), BF16),
            jax.ShapeDtypeStruct((16, width), F32),
        ],
        compiler_params=params(30),
        cost_estimate=cost(2 * seqs * rows * width * wide, seqs * rows * (4 * width + wide) * 2 + 4 * width * wide),
        name="norm_project",
    )(lengths, pos, held(x), held(cot), *[held(piece) for piece in pieces], *vectors)
    return normed, packed, up, up_sum, kept.reshape(width, -1), table


LEAST = 256
RATE = E**-0.5 * 1.4426950408889634


def attend_kernel(seq, lengths, q, k, v, *refs):
    mixed, lse = refs[-2:]
    rows = q.shape[1]
    length = lengths[seq + pl.program_id(0)]
    key_ok = lax.broadcasted_iota(jnp.int32, (1, rows - LEAST), 1) + LEAST < length
    lane = lax.broadcasted_iota(jnp.int32, (rows, LANES), 1)
    low_lane = lane < E
    logs = jnp.zeros((rows, LANES), F32)
    for pair in range(q.shape[2] // LANES):
        at = slice(pair * LANES, (pair + 1) * LANES)
        qs, ks, vs = q[0, :, at], k[0, :, at], v[0, :, at]
        outs = []
        for head in range(2):
            keep = low_lane if head == 0 else ~low_lane
            scores = mm(jnp.where(keep, qs, jnp.zeros_like(qs)), ks, NT)
            scores = jnp.concatenate(
                [scores[:, :LEAST], jnp.where(key_ok, scores[:, LEAST:], -1e30)], 1
            )
            top = jnp.max(scores, -1, keepdims=True)
            weights = jnp.exp2((scores - top) * RATE)
            total = jnp.sum(weights, -1, keepdims=True)
            outs.append(mm(weights.astype(BF16), vs) * (1.0 / total))
            logs = jnp.where(lane == 2 * pair + head, top * RATE + jnp.log2(total), logs)
        mixed[0, :, at] = jnp.where(low_lane, outs[0], outs[1]).astype(BF16)
    lse[0, 0] = logs.T[: lse.shape[2], :]


def attend(seq, here, lengths, packed, earlier=()):
    seqs, rows, wide = packed.shape
    width = wide // 3
    wid = 4 * LANES
    steps = width // wid
    block = lambda part: pl.BlockSpec((1, rows, wid), lambda s, j, *_: (seq + s, 0, part * steps + j))
    return pl.pallas_call(
        functools.partial(attend_kernel, seq),
        grid_spec=pltpu.PrefetchScalarGridSpec(
            num_scalar_prefetch=1,
            grid=(here, steps),
            in_specs=[block(0), block(1), block(2)]
            + [pl.BlockSpec(memory_space=pl.ANY)] * len(earlier),
            out_specs=[
                pl.BlockSpec((1, rows, wid), lambda s, j, *_: (seq + s, 0, j)),
                pl.BlockSpec((1, 1, 8, rows), lambda s, j, *_: (seq + s, j, 0, 0)),
            ],
        ),
        out_shape=[
            jax.ShapeDtypeStruct((seqs, rows, width), BF16),
            jax.ShapeDtypeStruct((seqs, steps, 8, rows), F32),
        ],
        input_output_aliases={4: 0, 5: 1} if earlier else {},
        compiler_params=pltpu.CompilerParams(
            vmem_limit_bytes=16 << 20, dimension_semantics=("arbitrary",) * 2
        ),
        cost_estimate=cost(4 * here * rows * rows * width * 8, here * rows * wide * 3, here * H * rows * rows),
        name="attend",
    )(lengths, *[held(packed)] * 3, *earlier)


def attend_back_kernel(seq, lengths, q, k, v, lse, grad, *refs):
    out = refs[-1]
    rows = q.shape[1]
    length = lengths[seq + pl.program_id(0)]
    key_ok = lax.broadcasted_iota(jnp.int32, (rows - LEAST, 1), 0) + LEAST < length
    low_lane = lax.broadcasted_iota(jnp.int32, (rows, LANES), 1) < E
    for pair in range(q.shape[2] // LANES):
        at = slice(pair * LANES, (pair + 1) * LANES)
        qs, ks, vs, gs = q[0, :, at], k[0, :, at], v[0, :, at], grad[0, :, at]
        sums = []
        for head in range(2):
            keep = low_lane if head == 0 else ~low_lane
            scores = mm(jnp.where(keep, ks, jnp.zeros_like(ks)), qs, NT)
            grad_probs = mm(jnp.where(keep, vs, jnp.zeros_like(vs)), gs, NT)
            row = 2 * pair + head
            probs = jnp.exp2(scores * RATE - lse[0, 0, row : row + 1, :])
            probs = jnp.concatenate(
                [probs[:LEAST], jnp.where(key_ok, probs[LEAST:], 0.0)], 0
            )
            inner = jnp.sum(grad_probs * probs, 0, keepdims=True)
            grad_scores = (probs * (grad_probs - inner)).astype(BF16)
            sums.append(
                (
                    mm(grad_scores, ks, TN) * E**-0.5,
                    mm(grad_scores, qs) * E**-0.5,
                    mm(probs.astype(BF16), gs),
                )
            )
        for part, first, second in zip(range(3), sums[0], sums[1]):
            out[0, part, :, at] = jnp.where(low_lane, first, second).astype(BF16)


def attend_back(seq, here, lengths, packed, lse, grad, earlier=()):
    seqs, rows, wide = packed.shape
    width = wide // 3
    wid = 4 * LANES
    steps = width // wid
    block = lambda part: pl.BlockSpec(
        (1, rows, wid), lambda s, j, *_: (seq + s, 0, part * steps + j)
    )
    return pl.pallas_call(
        functools.partial(attend_back_kernel, seq),
        grid_spec=pltpu.PrefetchScalarGridSpec(
            num_scalar_prefetch=1,
            grid=(here, steps),
            in_specs=[
                block(0),
                block(1),
                block(2),
                pl.BlockSpec((1, 1, 8, rows), lambda s, j, *_: (seq + s, j, 0, 0)),
                pl.BlockSpec((1, rows, wid), lambda s, j, *_: (seq + s, 0, j)),
            ]
            + [pl.BlockSpec(memory_space=pl.ANY)] * len(earlier),
            out_specs=pl.BlockSpec((1, 3, rows, wid), lambda s, j, *_: (seq + s, 0, 0, j)),
        ),
        out_shape=far((seqs, 3, rows, width), BF16),
        input_output_aliases={6: 0} if earlier else {},
        compiler_params=pltpu.CompilerParams(
            vmem_limit_bytes=18 << 20, dimension_semantics=("arbitrary",) * 2
        ),
        cost_estimate=cost(10 * here * rows * rows * width * 8, here * rows * wide * 5, here * H * rows * rows),
        name="attend_back",
    )(lengths, *[held(packed)] * 3, lse, grad, *[held(a) for a in earlier])


def branch_kernel(ring, count, lengths, pos, x, mixed, table, *refs):
    pieces, (resid, normed, kept, whole, sems, sem) = refs[:-6], refs[-6:]
    step = pl.program_id(0)
    fill(ring, step, count, pos, pieces, kept, whole, sems, sem)
    rows, width = x.shape[1:]
    valid = valid_rows(lengths[step], rows)
    weight = whole[..., :width].reshape(-1, width)
    total = x[0].astype(F32) * valid + mm(mixed[0], weight) + table[4:5, :]
    resid[0] = total
    unit, _ = norm_parts(total)
    normed[0] = (unit * table[5:6, :] + table[6:7, :]).astype(BF16)
    keep(step, count, kept, whole, sem)


def branch(ring, lengths, pos, x, mixed, table, pieces):
    seqs, rows, width = x.shape
    wide = pieces[0].shape[-1]
    row_block = pl.BlockSpec((1, rows, width), lambda s, *_: (s, 0, 0))
    anywhere = pl.BlockSpec(memory_space=pl.ANY)
    resid, normed, kept = pl.pallas_call(
        functools.partial(branch_kernel, ring, seqs),
        grid_spec=pltpu.PrefetchScalarGridSpec(
            num_scalar_prefetch=2,
            grid=(seqs,),
            in_specs=[row_block, row_block, once(table.shape)] + [anywhere] * len(pieces),
            out_specs=[row_block, row_block, anywhere],
            scratch_shapes=collect_scratch(ring, pieces),
        ),
        out_shape=[
            far(x.shape, F32),
            jax.ShapeDtypeStruct(x.shape, BF16),
            far(whole_shape(ring, pieces), BF16),
        ],
        compiler_params=params(26),
        cost_estimate=cost(2 * seqs * rows * width * width, seqs * rows * width * 10 + 4 * width * wide),
        name="branch",
    )(lengths, pos, x, mixed, table, *pieces)
    return resid, normed, kept.reshape(-1, wide)


def store_halves(ref, value):
    _, shards, quarters, rows, _ = ref.shape
    for shard in range(shards):
        for quarter in range(quarters):
            for half in range(2):
                at = ((shard * quarters + quarter) * 2 + half) * rows
                ref[half, shard, quarter] = value[at : at + rows]


def expand_kernel(seqs, normed, up, weight, bias, act, slope, grad):
    rows = normed.shape[0] // seqs
    for s in range(seqs):
        at = slice(s * rows, (s + 1) * rows)
        hidden = mm(normed[at, :], weight[...]) + bias[...]
        phi = 0.5 + 0.5 * lax.erf(hidden * HALF_ROOT)
        act[at, :] = (hidden * phi).astype(BF16)
        slope[at, :] = (phi + hidden * (INV_ROOT_TAU * jnp.exp(-0.5 * hidden * hidden))).astype(BF16)
    grad[...] = mm(act[...], up[...], TN).astype(BF16)


def expand(seqs, normed, up, weight, bias):
    count, width = normed.shape
    hidden = bias.shape[1]
    size = hidden // 4
    skip = (weight.shape[1] - hidden) // size
    wide = pl.BlockSpec((count, size), lambda i: (0, i))
    shape = far((count, hidden), BF16)
    return pl.pallas_call(
        functools.partial(expand_kernel, seqs),
        grid=(4,),
        in_specs=[
            once((count, width)),
            once((count, width)),
            pl.BlockSpec((width, size), lambda i: (0, skip + i)),
            pl.BlockSpec((1, size), lambda i: (0, i)),
        ],
        out_specs=[wide, wide, pl.BlockSpec((size, width), lambda i: (i, 0))],
        out_shape=[shape, shape, far((hidden, width), BF16)],
        compiler_params=params(36),
        cost_estimate=cost(4 * count * width * hidden, count * hidden * 4 + width * hidden * 4, count * hidden),
        name="expand",
    )(normed, up, held(weight), bias)


def reduce_kernel(lengths, resid, act, weight, table, out):
    rows = resid.shape[1]
    valid = valid_rows(lengths[pl.program_id(0)], rows)
    out[0] = (resid[0] + mm(act[0], weight[...]) + table[11:12, :]) * valid


def reduce_out(lengths, resid, act, weight, table):
    seqs, rows, width = resid.shape
    hidden = weight.shape[0]
    row_block = pl.BlockSpec((1, rows, width), lambda s, *_: (s, 0, 0))
    return pl.pallas_call(
        reduce_kernel,
        grid_spec=pltpu.PrefetchScalarGridSpec(
            num_scalar_prefetch=1,
            grid=(seqs,),
            in_specs=[
                row_block,
                pl.BlockSpec((1, rows, hidden), lambda s, *_: (s, 0, 0)),
                once((hidden, width)),
                once(table.shape),
            ],
            out_specs=row_block,
        ),
        out_shape=far(resid.shape, F32),
        compiler_params=params(26),
        cost_estimate=cost(2 * seqs * rows * width * hidden, seqs * rows * (8 * width + 2 * hidden) + 2 * width * hidden),
        name="reduce_out",
    )(lengths, held(resid), held(act.reshape(seqs, rows, hidden)), held(weight), table)


def hidden_back_kernel(seqs, up, weight, slope, grad, grad_sum):
    rows = up.shape[0] // seqs
    total = None
    for s in range(seqs):
        at = slice(s * rows, (s + 1) * rows)
        low = (mm(up[at, :], weight[...], NT) * slope[at, :].astype(F32)).astype(BF16)
        grad[at, :] = low
        part = column_sum(low.astype(F32))
        total = part if s == 0 else total + part
    grad_sum[...] = total


def hidden_back(seqs, up, weight, slope):
    count, width = up.shape
    hidden = slope.shape[1]
    size = hidden // 4
    wide = pl.BlockSpec((count, size), lambda i: (0, i))
    return pl.pallas_call(
        functools.partial(hidden_back_kernel, seqs),
        grid=(4,),
        in_specs=[once((count, width)), pl.BlockSpec((size, width), lambda i: (i, 0)), wide],
        out_specs=[wide, pl.BlockSpec((1, size), lambda i: (0, i))],
        out_shape=[far((count, hidden), BF16), jax.ShapeDtypeStruct((1, hidden), F32)],
        compiler_params=params(28),
        cost_estimate=cost(2 * count * width * hidden, count * hidden * 4 + 2 * width * hidden),
        name="hidden_back",
    )(up, held(weight), held(slope))


def whole_grad_kernel(inputs, grads, out):
    out[...] = mm(inputs[...], grads[...], TN).astype(BF16)


def whole_grad(inputs, grads, first):
    count, width = inputs.shape
    here = grads.shape[1] - first
    size = 1024
    return pl.pallas_call(
        whole_grad_kernel,
        grid=(here // size,),
        in_specs=[
            once((count, width)),
            pl.BlockSpec((count, size), lambda j: (0, first // size + j)),
        ],
        out_specs=pl.BlockSpec((width, size), lambda j: (0, j)),
        out_shape=far((width, here), BF16),
        compiler_params=params(28),
        cost_estimate=cost(2 * count * width * here, count * (width + here) * 2 + 2 * width * here),
        name="whole_grad",
    )(inputs, held(grads))


def pick_columns(half, order, inputs, picked):
    @pl.when(pl.program_id(0) == 0)
    def _():
        for i in range(4):
            size = picked.shape[1] // 4
            at = pl.multiple_of((order[0] * i + order[1 + half]) * size, size)
            picked[:, i * size : (i + 1) * size] = inputs[:, pl.ds(at, size)]


def weight_grad_kernel(half, order, inputs, grads, *refs):
    out, picked = refs[-2:]
    pick_columns(half, order, inputs, picked)
    block = grads[...].reshape(inputs.shape[0], grads.shape[-1])
    value = mm(picked[...], block, TN).astype(BF16)
    _, shards, _, rows, _ = out.shape
    for shard in range(shards):
        for quarter in range(4):
            for part in range(2):
                at = ((shard * 4 + quarter) * 2 + part) * rows
                out[part, shard, quarter ^ order[3]] = value[at : at + rows]


def grad_spec(grads):
    if len(grads.shape) == 2:
        return pl.BlockSpec((grads.shape[0], 1024), lambda j, *_: (0, j)), 1
    seqs, parts, each, size = grads.shape
    return pl.BlockSpec((seqs, 1, each, size), lambda j, *_: (0, j, 0, 0)), parts


def weight_grad(half, order, inputs, grads, wide, first=0, earlier=()):
    count, width = inputs.shape
    size = 1024
    spec, parts = grad_spec(grads)
    rows = width // 64
    return pl.pallas_call(
        functools.partial(weight_grad_kernel, half),
        grid_spec=pltpu.PrefetchScalarGridSpec(
            num_scalar_prefetch=1,
            grid=(parts,),
            in_specs=[once((count, width)), spec]
            + [pl.BlockSpec(memory_space=pl.ANY)] * len(earlier),
            out_specs=pl.BlockSpec(
                (2, 4, 4, rows, size), lambda j, *_: (0, 0, 0, 0, first // size + j)
            ),
            scratch_shapes=[pltpu.VMEM((count, width // 2), BF16)],
        ),
        out_shape=far((2, 4, 4, rows, wide), BF16),
        input_output_aliases={3: 0} if earlier else {},
        compiler_params=params(20),
        cost_estimate=cost(count * width * parts * size, count * (width + parts * size) * 2 + width * parts * size),
        name="weight_grad",
    )(order, inputs, held(grads), *[held(a) for a in earlier])


def norm_two_kernel(lengths, hidden_grad, weight, resid, cot, table, *outs):
    grad_resid, low_ref, mixed_grad, gain_grad, bias_grad, out_bias_grad = outs
    step = pl.program_id(0)
    rows, width = resid.shape[1:]
    valid = valid_rows(lengths[step], rows)
    grad = mm(hidden_grad[0], weight[:, width:], NT)
    unit, scale = norm_parts(resid[0])
    total = cot[0].astype(F32) * valid + norm_back(unit, scale, grad, table[5:6, :])
    grad_resid[0] = total
    low = total.astype(BF16)
    low_ref[0] = low
    mixed_grad[0] = mm(low, weight[:, :width], NT).astype(BF16)
    add_first(step, gain_grad, column_sum(grad * unit))
    add_first(step, bias_grad, column_sum(grad))
    add_first(step, out_bias_grad, column_sum(low.astype(F32)))


def norm_two_back(lengths, hidden_grad, weight, resid, cot, table):
    seqs, rows, width = resid.shape
    hidden = hidden_grad.shape[1]
    row_block = pl.BlockSpec((1, rows, width), lambda s, *_: (s, 0, 0))
    vec = pl.BlockSpec((1, width), lambda s, *_: (0, 0))
    return pl.pallas_call(
        norm_two_kernel,
        grid_spec=pltpu.PrefetchScalarGridSpec(
            num_scalar_prefetch=1,
            grid=(seqs,),
            in_specs=[
                pl.BlockSpec((1, rows, hidden), lambda s, *_: (s, 0, 0)),
                once((width, width + hidden)),
                row_block,
                row_block,
                once(table.shape),
            ],
            out_specs=[row_block] * 3 + [vec] * 3,
        ),
        out_shape=[
            far(resid.shape, F32),
            jax.ShapeDtypeStruct(resid.shape, BF16),
            jax.ShapeDtypeStruct(resid.shape, BF16),
        ]
        + [jax.ShapeDtypeStruct((1, width), F32)] * 3,
        compiler_params=params(40),
        cost_estimate=cost(2 * seqs * rows * width * (hidden + width), seqs * rows * (2 * hidden + 14 * width)),
        name="norm_two_back",
    )(lengths, held(hidden_grad.reshape(seqs, rows, hidden)), held(weight), held(resid), held(cot), table)


def norm_one_kernel(lengths, thirds, weight, x, grad_resid, table, *outs):
    input_grad, gain_grad, bias_grad, q_sum, v_sum = outs
    step = pl.program_id(0)
    rows, width = x.shape[1:]
    valid = valid_rows(lengths[step], rows)
    grad = mm(thirds[0, 0], weight[:, :width], NT)
    grad += mm(thirds[0, 1], weight[:, width : 2 * width], NT)
    grad += mm(thirds[0, 2], weight[:, 2 * width : 3 * width], NT)
    unit, scale = norm_parts(x[0].astype(F32) * valid)
    input_grad[0] = (grad_resid[0] + norm_back(unit, scale, grad, table[0:1, :])) * valid
    add_first(step, gain_grad, column_sum(grad * unit))
    add_first(step, bias_grad, column_sum(grad))
    add_first(step, q_sum, column_sum(thirds[0, 0].astype(F32)))
    add_first(step, v_sum, column_sum(thirds[0, 2].astype(F32)))


def norm_one_back(lengths, thirds, weight, x, grad_resid, table):
    seqs, rows, width = x.shape
    row_block = pl.BlockSpec((1, rows, width), lambda s, *_: (s, 0, 0))
    vec = pl.BlockSpec((1, width), lambda s, *_: (0, 0))
    return pl.pallas_call(
        norm_one_kernel,
        grid_spec=pltpu.PrefetchScalarGridSpec(
            num_scalar_prefetch=1,
            grid=(seqs,),
            in_specs=[
                pl.BlockSpec((1, 3, rows, width), lambda s, *_: (s, 0, 0, 0)),
            ]
            + [once(weight.shape), row_block, row_block, once(table.shape)],
            out_specs=[row_block] + [vec] * 4,
        ),
        out_shape=[far(x.shape, F32)] + [jax.ShapeDtypeStruct((1, width), F32)] * 4,
        compiler_params=params(32),
        cost_estimate=cost(6 * seqs * rows * width * width, seqs * rows * width * 16 + 6 * width * width),
        name="norm_one_back",
    )(lengths, held(thirds), weight, x, held(grad_resid), table)

def near_kernel(*refs):
    for at in range(4):
        mine, other, out = refs[at], refs[4 + at], refs[8 + at]
        total = mine[...].astype(F32) + other[...].astype(F32)
        out[...] = total.astype(BF16).reshape(out.shape)


def near_sum(own, arrived):
    _, shards, _, rows, wide = own.shape
    over_x = (1, 1, 2, 1, rows, wide)
    over_y = (1, 1, 1, 2, rows, wide)
    specs = [
        pl.BlockSpec(over_x, lambda s: (0, s, 0, 0, 0, 0)),
        pl.BlockSpec(over_y, lambda s: (1, s, 0, 0, 0, 0)),
        pl.BlockSpec(over_x, lambda s: (0, s, 0, 1, 0, 0)),
        pl.BlockSpec(over_y, lambda s: (1, s, 1, 0, 0, 0)),
    ]
    shape = (2, shards, 2, 2, rows, wide)
    return pl.pallas_call(
        near_kernel,
        grid=(shards,),
        in_specs=specs * 2,
        out_specs=[pl.BlockSpec((1, 2, rows, wide), lambda s: (s, 0, 0, 0))] * 4,
        out_shape=[jax.ShapeDtypeStruct((shards, 2, rows, wide), BF16)] * 4,
        compiler_params=params(14),
        cost_estimate=cost(own.size, own.size * 6),
        name="near_sum",
    )(*[held(own.reshape(shape))] * 4, *[held(arrived.reshape(shape))] * 4)


AXES = ("group", "dp")
Z = 4


def permutation(move):
    pairs = []
    for g in range(4):
        for d in range(2 * Z):
            to_g, to_z, to_c = move(g, d // 2, d % 2)
            pairs.append((g * 2 * Z + d, (to_g * Z + to_z) * 2 + to_c))
    return pairs


CORE = permutation(lambda g, z, c: (g, z, 1 - c))
OVER_X = permutation(lambda g, z, c: (g ^ 1, z, c))
OVER_Y = permutation(lambda g, z, c: (g ^ 2, z, c))
OVER_XY = permutation(lambda g, z, c: (g ^ 3, z, c))
OVER_Z = [permutation(lambda g, z, c, k=k: (g, (z + k) % Z, c)) for k in range(Z)]
NEAR_Z = permutation(lambda g, z, c: (g, z ^ 1, c))
FAR_Z = permutation(lambda g, z, c: (g, z ^ 2, c))


def send(array, pairs):
    return lax.ppermute(array, AXES, pairs)


def tie(value, *others):
    return lax.optimization_barrier((value,) + others)[0]


def pick(array, index, axis):
    return lax.dynamic_index_in_dim(array, index, axis, keepdims=False)


def plus(former, latter):
    return (former.astype(F32) + latter.astype(F32)).astype(BF16)


def quarters(shard, g):
    rows, wide = shard.shape
    parts = shard.reshape(4, 2, rows // 8, wide)
    return parts, pick(parts, g, 0)


def send_quarter(mine):
    return [send(mine, OVER_Z[k]) for k in range(1, Z)]


def send_xy(first, second):
    return send(first, OVER_X), send(second, OVER_Y)


def scatter_core(other):
    return send(other, CORE)


def scatter_far(first, second, from_x, from_y):
    first = plus(first, from_x)
    second = plus(second, from_y)
    return first[:, 0], second[:, 0], first[:, 1], second[:, 1]


def scatter_z(first, second, from_y, from_x, z):
    quarter = jnp.stack([plus(first, from_y), plus(second, from_x)], 1)
    return pick(quarter, z, 0), [pick(quarter, (z + k) % Z, 0) for k in range(1, Z)]


def send_z(parts):
    return [send(part, OVER_Z[k]) for k, part in enumerate(parts, 1)]


def spread(mine, arrived):
    total = mine.astype(F32)
    for part in arrived:
        total = total + part.astype(F32)
    return total.astype(BF16)


def send_near(mine):
    return [send(mine, OVER_X), send(mine, OVER_Y), send(mine, OVER_XY)]


def placed(mine, others, g):
    grid = jnp.stack([mine, *others]).reshape(2, 2, *mine.shape)
    grid = jnp.where(g % 2 == 1, grid[:, ::-1], grid)
    grid = jnp.where(g // 2 == 1, grid[::-1], grid)
    return grid.astype(F32).reshape(-1, mine.shape[-1])


def trade(shard, g):
    rows, wide = shard.shape
    parts = shard.reshape(4, rows // 4, wide)
    return pick(parts, g, 0), [pick(parts, g ^ over, 0) for over in (1, 2, 3)]


def send_trade(parts):
    return [send(part, pairs) for part, pairs in zip(parts, (OVER_X, OVER_Y, OVER_XY))]


def spread_xy(mine):
    half = mine.shape[0] // 2
    over_x, over_y = send_xy(mine, mine)
    second, first = send_xy(over_y[half:], over_x[:half])
    return [over_x, over_y, jnp.concatenate([first, second])]


VEC = (0, 1, 3, 5, 6, 7, 9, 11)


def joined(vectors):
    total = sum(v.shape[0] for v in vectors)
    at = 0
    out = None
    for v in vectors:
        wide = lax.pad(v, jnp.zeros((), v.dtype), [(at, total - at - v.shape[0], 0)])
        out = wide if out is None else out + wide
        at += v.shape[0]
    return out


def widened(weight, vectors):
    rows = weight.shape[0]
    columns = joined(vectors).reshape(-1, rows).T
    columns = jnp.pad(columns, ((0, 0), (0, LANES - columns.shape[1])))
    return jnp.concatenate([weight, columns], 1)


def spaced(table, first, last, rows):
    part = table[first:last].reshape(last - first, -1, rows)
    return part.transpose(1, 0, 2).reshape(1, -1)


def packed_vectors(grads):
    return joined([grads[i].reshape(-1) for i in VEC])


def own_vectors(total, grads, shards):
    d = lax.axis_index("dp")
    at = 0
    summed = {}
    for i in VEC:
        size = shards[i].shape[0]
        summed[i] = lax.dynamic_slice(total, (at + d * size,), (size,))
        at += grads[i].size
    return summed


def over_dp(array):
    return lax.psum_scatter(array, "dp", scatter_dimension=0, tiled=True)


def local(ring, layer_input, lengths, *rest):
    shards, cot = rest[:12], rest[12]
    micro, seqs, rows, width = layer_input.shape
    count = micro * seqs
    g = lax.axis_index("group")
    d = lax.axis_index("dp")
    z, c = d // 2, d % 2
    pos = jnp.stack([g, z, c]).astype(jnp.int32)
    order = [2, 1 - c, c, g] if ring else [1, 0, 4, 0]
    order = jnp.stack([jnp.asarray(v, jnp.int32) for v in order])
    lens = lengths.reshape(-1)
    x = layer_input.reshape(count, rows, width)
    cot = cot.reshape(count, rows, width)
    flat = lambda a: a.reshape(count * rows, a.shape[-1])
    rows_each = shards[2].shape[0]
    wanted = (widened(shards[2], [shards[i] for i in VEC]), jnp.concatenate([shards[4], shards[8]], 1), shards[10])

    if ring:
        parts_p, mine_p = quarters(wanted[0], g)
        parts_e, mine_e = quarters(wanted[1], g)
        ring_p = send_quarter(mine_p)
        core_p, core_e = send(parts_p, CORE), send(parts_e, CORE)
        stack_p = jnp.stack(tie(ring_p, core_p, core_e), 1)
        x_p, y_p = send_xy(stack_p, stack_p)
        mine_e = tie(mine_e, stack_p)
        e_one, e_two = send(mine_e, OVER_Z[1]), send(mine_e, OVER_Z[2])
        x_p, y_p, e_one, e_two, mine_e = tie((x_p, y_p, e_one, e_two, mine_e))
        b_p, a_p = send_xy(y_p[1], x_p[0])
        e_three = send(mine_e, OVER_Z[3])
        near_p = jnp.stack([stack_p, x_p, y_p])
        near_core_p = send(near_p, CORE)
        a_p, b_p, e_three, near_core_p = tie((a_p, b_p, e_three, near_core_p))
        far_p = jnp.stack([a_p, b_p])
        pieces_p = [parts_p, near_p, far_p, core_p, near_core_p, send(far_p, CORE)]
        stack_e = jnp.stack(tie((e_one, e_two, e_three), pieces_p), 1)
        lens_project, shard_r = tie((lens, wanted[2]), stack_e)
        x_e, y_e = send_xy(stack_e, stack_e)
        reduce_w = lax.all_gather(shard_r, "dp", axis=0, tiled=True)
        vectors = ()
    else:
        pieces = [lax.all_gather(w, "dp", axis=0, tiled=True) for w in wanted]
        pieces_p, pieces_e, reduce_w = [pieces[0]], [pieces[1]], pieces[2]
        lens_project = lens
        table = pieces[0][:, 3 * width : 3 * width + 16].T.astype(F32)
        pair = spaced(table, 2, 4, rows_each)
        middle = jnp.zeros((1, width), F32)
        vectors = (table, jnp.concatenate([pair[:, :width], middle, pair[:, width:]], -1))
    normed, packed, up, up_sum, project_w, table = project(
        ring, rows_each, lens_project, pos, x, cot, pieces_p, vectors
    )
    expand_b = spaced(table, 7, 11, rows_each)
    mixed, lse = attend(0, 1, lens, packed)
    lens_attend = lens
    if ring:
        x_e, y_e = tie((x_e, y_e), mixed)
        near_e = jnp.stack([stack_e, x_e, y_e])
        lens_attend = tie(lens, near_e)
        b_e, a_e = send_xy(y_e[1], x_e[0])
        near_core_e = send(near_e, CORE)
    mixed, lse = attend(1, count - 1, lens_attend, packed, (mixed, lse))
    if ring:
        a_e, b_e = tie((a_e, b_e), mixed)
        far_e = jnp.stack([a_e, b_e])
        pieces_e = [parts_e, near_e, far_e, core_e, near_core_e, send(far_e, CORE)]
    resid, normed_two, joint_w = branch(ring, lens, pos, x, mixed, table, pieces_e)
    act, slope, reduce_grad = expand(count, flat(normed_two), flat(up), joint_w, expand_b)
    shard_r = over_dp(reduce_grad)
    hidden_grad, hidden_sum = hidden_back(count, flat(up), reduce_w, slope)
    grad_resid, branch_low, mixed_grad, gain_two_grad, bias_two_grad, output_b_grad = norm_two_back(
        lens, hidden_grad, joint_w, resid, cot, table
    )
    thirds = attend_back(0, count, lens, packed, lse, mixed_grad)
    expand_grad = whole_grad(flat(normed_two), tie(hidden_grad, thirds), 0)
    shard_e = over_dp(expand_grad)
    branch_part = flat(branch_low)
    project_far = weight_grad(0, order, flat(mixed), branch_part, 4 * width)
    project_near = weight_grad(1, order, flat(mixed), branch_part, 4 * width)
    order_far = order
    if ring:
        mine_r, parts_r = trade(tie(shard_r, (project_far, project_near)), g)
        order_far = tie(order, parts_r)
        arrived_r = send_trade(parts_r)
    project_far = weight_grad(
        0, order_far, flat(normed), thirds, 4 * width, width, (project_far,)
    )
    order_near = order
    if ring:
        order_near = tie(order, project_far)
        arrived = send(project_far, CORE)
    project_near = weight_grad(
        1, order_near, flat(normed), thirds, 4 * width, width, (project_near,)
    )
    lens_one = lens
    if ring:
        spread_r = spread(mine_r, tie(arrived_r, project_near))
        ps = near_sum(project_near, arrived)
        lens_one = tie(lens, ps, spread_r)
        from_x, from_y = send_xy(ps[2], ps[3])
    input_grad, gain_one_grad, bias_one_grad, query_sum, value_sum = norm_one_back(
        lens_one, thirds, project_w, x, grad_resid, table
    )
    vectors = {
        0: gain_one_grad,
        1: bias_one_grad,
        3: jnp.concatenate([query_sum, value_sum], -1),
        5: output_b_grad,
        6: gain_two_grad,
        7: bias_two_grad,
        9: hidden_sum,
        11: up_sum,
    }
    total = packed_vectors(vectors)
    lens_out = lens
    if ring:
        total = total.reshape(-1, LANES)
        total = total + send(total, CORE)
        total = (total + send(total, OVER_XY)) + (send(total, OVER_X) + send(total, OVER_Y))
        total, from_x, from_y = tie((total, from_x, from_y))
        ps = scatter_far(ps[0], ps[1], from_x, from_y)
        lens_out = tie(lens, ps)
        from_x, from_y = send_xy(ps[3], ps[2])
        near_r = send_near(spread_r)
    layer_output = reduce_out(lens_out, resid, act, reduce_w, table)
    sums = {}
    if ring:
        (from_x, from_y, near_r), layer_output = lax.optimization_barrier(
            ((from_x, from_y, near_r), layer_output)
        )
        mine_z, parts_z = scatter_z(ps[0], ps[1], from_y, from_x, z)
        arrived_p = send_z(parts_z)
        mine_e, parts_e = trade(tie(shard_e, parts_z), g)
        arrived_e = send_trade(parts_e)
        sums[10] = placed(spread_r, near_r, g)
        spread_e = spread(mine_e, arrived_e)
        near_e = send_near(spread_e)
        total = tie(total, spread_e)
        total = total + send(total, NEAR_Z)
        total = total + send(total, FAR_Z)
        spread_p = spread(mine_z, tie(arrived_p, spread_e))
        near_p = send_near(spread_p)
        joint_sum = placed(spread_p, near_p, g)
        sums[8] = placed(spread_e, near_e, g)
    else:
        total = lax.psum(total, ("group", "dp"))
        sums[10] = lax.psum(shard_r, "group").astype(F32)
        sums[8] = lax.psum(shard_e, "group").astype(F32)
        parts = [a.transpose(1, 2, 0, 3, 4) for a in (project_far, project_near)]
        parts = over_dp(jnp.concatenate(parts).reshape(width, 4 * width))
        joint_sum = lax.psum(parts, "group").astype(F32)
    sums.update(own_vectors(total.reshape(-1), vectors, shards))
    sums[4] = joint_sum[:, :width]
    sums[2] = joint_sum[:, width:]
    return (
        layer_output.reshape(layer_input.shape),
        input_grad.reshape(layer_input.shape),
        *[sums[i] for i in range(12)],
    )


def solution(mesh):
    ring = mesh.shape["group"] == 4 and mesh.shape["dp"] == 2 * Z
    rows = P(None, ("group", "dp"), None, None)
    vec = P("dp")
    mat = P("dp", None)
    kinds = (vec, vec, mat, vec, mat, vec, vec, vec, mat, vec, mat, vec)
    return jax.shard_map(
        functools.partial(local, ring),
        mesh=mesh,
        in_specs=(rows, P(None, ("group", "dp")), *kinds, rows),
        out_specs=(rows, rows, *kinds),
        check_vma=False,
    )
```
